128 devices in a mesh: req: 32 (over z_hi, x, y), tp: 4 (over z_lo, core).
Axes of the slice: x: 4, y: 4, z: 4 (z_hi: 2, z_lo: 2; z = z_hi * 2 + z_lo), core: 2. Of those that a mesh axis runs over, the one named last changes fastest.
Arguments:
- hidden_in: bfloat16 [65536, 1024], P('req'), may hold values from -6 to 6
- lengths: int32 [64], replicated, may hold values from 1 to 2048, 65536 in all
- tenant: int32 [64], replicated, may hold values from 0 to 3
- shard_map: int32 [128], replicated, may hold values from 0 to 127, each once
- wq: float32 [1024, 1024], P(('req', 'tp')), as said below
- wk: float32 [1024, 1024], P(('req', 'tp')), as said below
- wv: float32 [1024, 1024], P(('req', 'tp')), may hold values from -0.75 to 0.75
- wo: float32 [1024, 1024], P(('req', 'tp')), may hold values from -0.75 to 0.75
- wi_in: float32 [1024, 2624], P(('req', 'tp')), may hold values from -0.1875 to 0.1875
- wi_gate: float32 [1024, 2624], P(('req', 'tp')), may hold values from -0.1875 to 0.1875
- wo2: float32 [1024, 2624], P(('req', 'tp')), may hold values from -0.125 to 0.125
- head: float32 [49152, 1024], P(('req', 'tp')), may hold values from -0.56 to 0.56
- attn_gain: float32 [1024], replicated, may hold values from 0.1 to 1.9
- mlp_gain: float32 [1024], replicated, may hold values from 0.1 to 1.9
- final_gain: float32 [4, 1024], replicated, may hold values from 0.1 to 1.9
Outputs:
- hidden_out: bfloat16 [65536, 1024], P('req', 'tp')
- cache: bfloat16 [2, 65536, 1024], P(None, 'req', 'tp')
- last_rms: float32 [64], replicated
- top_logit: float32 [64], replicated
The draws below stay inside these ranges and needn't reach their ends.
Inputs may be any that keep to these rules, and one draw needn't show every extreme that they name: Prompts are packed in request order into the 65536 slots; the lengths sum to 65536 and the longest is exactly 2048. `shard_map`: A permutation: each row block is held by exactly one trainer device. `wq`: A fan-in scaled projection. `wk`: A fan-in scaled projection.
All inputs are finite; a program needn't handle non-finite values.
Results may differ from the reference program's by a relative error of at most 0.012.
The reference program's roundings to bfloat16 on the way count: a program that leaves them out, or rounds other values in their place, can miss the bound.
Values may be sent and summed in bfloat16 or wider, within the bound.
No kernel may reach another device: no remote copies, remote signals or barrier semaphores. Data moves between devices by JAX's collectives and lax.ppermute only.
A program may use at most 128 MiB of HBM per device.

```python
import math
import jax
import jax.numpy as jnp
import numpy as np
from jax import lax

D = 1024
HEADS = 16
HEAD_DIM = 64
FF = 2624
VOCAB = 49152
TENANTS = 4
MAX_LEN = 2048
TOKENS = 65536
REQS = 64
N_REQ = 32
N_TP = 4


def projection(key, salt):
    base = jax.random.normal(jax.random.fold_in(key, salt), (D, D), jnp.float32) * D ** (-0.5)
    return base


def draw_wq(key, part):
    return projection(key, 11)


def draw_wk(key, part):
    return projection(key, 23)


def touch_ends(drawn, rng, smallest, largest):
    dims = drawn.shape
    index_at = [jax.random.randint(jax.random.fold_in(rng, axis), (), 0, dims[axis]) for axis in range(len(dims))]
    drawn = drawn.at[tuple(index_at)].set(smallest)
    longest = dims.index(max(dims))
    index_at[longest] = (index_at[longest] + 1) % dims[longest]
    return drawn.at[tuple(index_at)].set(largest)


def steps_of(rng, shape, split, least, largest):
    loudness, own = 1.0, jax.random.fold_in(rng, 6)
    for axis_at, parts in split:
        draws = jnp.exp(jax.random.uniform(jax.random.fold_in(own, axis_at), (parts,), jnp.float32, least / len(split), largest / len(split)))
        loudness = loudness * jnp.repeat(draws, shape[axis_at] // parts).reshape([-1 if axis == axis_at else 1 for axis in range(len(shape))])
    return loudness


def length_profile(amount, total, limit, skew):
    portions = [(1 << 20) // math.isqrt(rank ** skew) + 1 for rank in range(2, amount + 1)]
    spare, given = total - limit - (amount - 1), [1] * (amount - 1)
    while spare > 0:
        movable = [i for i in range(amount - 1) if given[i] < limit]
        whole, remaining = sum([portions[i] for i in movable]), spare
        for i in movable:
            extra = min(limit - given[i], max(1, remaining * portions[i] // whole), spare)
            given[i] = given[i] + extra
            spare = spare - extra
    return np.array([limit] + given)


def ragged_sizes(key, number_of, total, bound, skew):
    if number_of == 2:
        one = jax.random.randint(key, (), max(1, total - bound), min(bound, total - 1) + 1)
        return jnp.stack([one, total - one])
    tallies = jnp.asarray(length_profile(number_of, total, bound, skew), jnp.int32)
    pairs = (number_of - 1) // 2
    donor, sink = tallies[1:1 + 2 * pairs:2], tallies[2:2 + 2 * pairs:2]
    slack = jnp.minimum(donor - 1, bound - sink)
    shifted = jax.random.randint(jax.random.fold_in(key, 1), (pairs,), 0, 1 << 20) % (slack + 1)
    tallies = tallies.at[1:1 + 2 * pairs:2].set(donor - shifted).at[2:2 + 2 * pairs:2].set(sink + shifted)
    return tallies[jax.random.permutation(jax.random.fold_in(key, 2), number_of)]


def scatter_about(key, shape, scale, limit, shards=(), kind=jnp.bfloat16):
    factor_of = steps_of(key, shape, shards, -0.22, 0.18) if shards else 1.0
    array = jax.random.normal(key, shape, jnp.float32) * scale * factor_of
    return jnp.minimum(jnp.maximum(array, -limit), limit).astype(kind)


def setup_inputs(seed: int = 0) -> dict:
    key_of = jax.random.split(jax.random.key(seed), 16)
    return {
        "hidden_in": scatter_about(key_of[0], (TOKENS, D), 1.0, 6.0, ((0, 32),)),
        "lengths": ragged_sizes(key_of[1], REQS, TOKENS, MAX_LEN, 2).astype(jnp.int32),
        "tenant": touch_ends(jax.random.randint(key_of[2], (REQS,), 0, TENANTS), jax.random.fold_in(key_of[2], 1), 0, TENANTS - 1).astype(jnp.int32),
        "shard_map": jax.random.permutation(key_of[3], N_REQ * N_TP).astype(jnp.int32),
        "wq": draw_wq(jax.random.fold_in(key_of[15], 71), 0),
        "wk": draw_wk(jax.random.fold_in(key_of[15], 71), 0),
        "wv": scatter_about(key_of[6], (D, D), (D // 16) ** -0.5, 0.75, ((0, 128),), jnp.float32),
        "wo": scatter_about(key_of[7], (D, D), (D // 16) ** -0.5, 0.75, ((0, 128),), jnp.float32),
        "wi_in": scatter_about(key_of[8], (D, FF), D ** -0.5, 0.1875, ((0, 128),), jnp.float32),
        "wi_gate": scatter_about(key_of[9], (D, FF), D ** -0.5, 0.1875, ((0, 128),), jnp.float32),
        "wo2": scatter_about(key_of[10], (D, FF), FF ** -0.5, 0.125, ((0, 128),), jnp.float32),
        "head": scatter_about(key_of[11], (VOCAB, D), 0.094, 0.56, ((0, 128),), jnp.float32),
        "attn_gain": jnp.clip(1.0 + 0.18 * jax.random.normal(key_of[12], (D,), jnp.float32), 0.1, 1.9),
        "mlp_gain": jnp.clip(1.0 + 0.18 * jax.random.normal(key_of[13], (D,), jnp.float32), 0.1, 1.9),
        "final_gain": jnp.clip(1.0 + 0.18 * jax.random.normal(key_of[14], (TENANTS, D), jnp.float32), 0.1, 1.9),
    }


THETA = 160000.0
EPS = 1e-05

def layer_norm(values, gain):
    center = lax.optimization_barrier(jnp.mean(values, axis=-1, keepdims=True))
    spread = lax.optimization_barrier(jnp.mean(values * values, axis=-1, keepdims=True)) - center * center
    return (values - center) * lax.rsqrt(spread + EPS) * gain

def natural_rows(weight, shard_map):
    count = N_REQ * N_TP
    inverse = jnp.zeros((count,), jnp.int32).at[shard_map].set(jnp.arange(count, dtype=jnp.int32))
    blocks = weight.reshape(count, D // count, weight.shape[1])
    return blocks[inverse].reshape(D, weight.shape[1]).astype(jnp.bfloat16)

def rotate(values, position):
    half = HEAD_DIM // 2
    freq = THETA ** (-(2.0 * jnp.arange(half, dtype=jnp.float32)) / HEAD_DIM)
    angle = position.astype(jnp.float32)[:, None] * freq[None, :]
    cosine = jnp.cos(angle)[:, None, :]
    sine = jnp.sin(angle)[:, None, :]
    first = values[..., :half]
    second = values[..., half:]
    return jnp.concatenate([first * cosine - second * sine, second * cosine + first * sine], axis=-1)

def reference(hidden_in, lengths, tenant, shard_map, wq, wk, wv, wo, wi_in, wi_gate, wo2, head, attn_gain, mlp_gain, final_gain):
    ends = jnp.cumsum(lengths).astype(jnp.int32)
    starts = (ends - lengths).astype(jnp.int32)
    index = jnp.arange(TOKENS, dtype=jnp.int32)
    segment = jnp.searchsorted(ends, index, side='right').astype(jnp.int32)
    position = index - starts[segment]
    normed = layer_norm(hidden_in.astype(jnp.float32), attn_gain).astype(jnp.bfloat16)
    query = jnp.dot(normed, natural_rows(wq, shard_map), preferred_element_type=jnp.float32)
    query = rotate(query.reshape(TOKENS, HEADS, HEAD_DIM), position).astype(jnp.bfloat16)
    keys = jnp.dot(normed, natural_rows(wk, shard_map), preferred_element_type=jnp.float32)
    keys = rotate(keys.reshape(TOKENS, HEADS, HEAD_DIM), position).astype(jnp.bfloat16)
    values = jnp.dot(normed, natural_rows(wv, shard_map), preferred_element_type=jnp.float32).astype(jnp.bfloat16)
    values = values.reshape(TOKENS, HEADS, HEAD_DIM)
    block = min(512, TOKENS)
    width = block + 2 * MAX_LEN
    padded_keys = jnp.pad(keys, ((MAX_LEN, MAX_LEN), (0, 0), (0, 0)))
    padded_values = jnp.pad(values, ((MAX_LEN, MAX_LEN), (0, 0), (0, 0)))
    padded_segment = jnp.pad(segment, (MAX_LEN, MAX_LEN), constant_values=-1)
    scale = HEAD_DIM ** (-0.5)

    def attend(number):
        start = (number * block).astype(jnp.int32)
        query_block = lax.dynamic_slice_in_dim(query, start, block, 0).astype(jnp.float32)
        key_window = lax.dynamic_slice_in_dim(padded_keys, start, width, 0).astype(jnp.float32)
        value_window = lax.dynamic_slice_in_dim(padded_values, start, width, 0).astype(jnp.float32)
        query_segment = lax.dynamic_slice_in_dim(segment, start, block, 0)
        key_segment = lax.dynamic_slice_in_dim(padded_segment, start, width, 0)
        scores = jnp.einsum('qhd,khd->hqk', query_block, key_window) * scale
        same = (query_segment[:, None] == key_segment[None, :])[None]
        scores = jnp.where(same, scores, -1e+30)
        highest = lax.optimization_barrier(jnp.max(scores, axis=-1, keepdims=True))
        weights = jnp.exp(scores - highest)
        probability = (weights / lax.optimization_barrier(jnp.sum(weights, axis=-1, keepdims=True))).astype(jnp.bfloat16)
        return jnp.einsum('hqk,khd->qhd', probability.astype(jnp.float32), value_window)
    mixed = lax.map(attend, jnp.arange(TOKENS // block, dtype=jnp.int32))
    mixed = mixed.reshape(TOKENS, D).astype(jnp.bfloat16)
    attn = jnp.dot(mixed, natural_rows(wo, shard_map).T, preferred_element_type=jnp.float32)
    first = (hidden_in.astype(jnp.float32) + attn).astype(jnp.bfloat16)
    normed2 = layer_norm(first.astype(jnp.float32), mlp_gain).astype(jnp.bfloat16)
    gate_in = jnp.dot(normed2, natural_rows(wi_in, shard_map), preferred_element_type=jnp.float32)
    gate_side = jnp.dot(normed2, natural_rows(wi_gate, shard_map), preferred_element_type=jnp.float32)
    inner = (jax.nn.gelu(gate_in, approximate=False) * gate_side).astype(jnp.bfloat16)
    down = jnp.dot(inner, natural_rows(wo2, shard_map).T, preferred_element_type=jnp.float32)
    hidden_out = (first.astype(jnp.float32) + down).astype(jnp.bfloat16)
    cache = jnp.stack([keys.reshape(TOKENS, D), values.reshape(TOKENS, D)])
    last = hidden_out[ends - 1].astype(jnp.float32)
    last_rms = jnp.sqrt(lax.optimization_barrier(jnp.mean(last * last, axis=-1)))
    final = layer_norm(last, final_gain[tenant]).astype(jnp.bfloat16)
    logits = jnp.dot(final, head.astype(jnp.bfloat16).T, preferred_element_type=jnp.float32)
    top_logit = lax.optimization_barrier(jnp.max(logits, axis=-1))
    return (hidden_out, cache, last_rms, top_logit)
```

```python
import functools

import jax
import jax.numpy as jnp
from jax import lax
from jax.experimental import pallas as pl
from jax.experimental.pallas import tpu as pltpu
from jax.sharding import PartitionSpec as P

HEADS = 16
HEAD_DIM = 64
THETA = 160000.0
EPS = 1e-05
BF = jnp.bfloat16
F32 = jnp.float32
BOTH = ("req", "tp")
NEG = -1e30
FFP = 768
QB = 256
KC = 512
VMEM_LIMIT = 60 * 1024 * 1024


def vmem(*shape):
    return pl.BlockSpec(shape, lambda *_: (0,) * len(shape))


def params():
    return pltpu.CompilerParams(vmem_limit_bytes=VMEM_LIMIT)


def prep_kernel(wq, wk, wv, wo, wi, wg, w2, qkv, wob, mlp):
    row = lax.broadcasted_iota(jnp.int32, (256, 256), 0)
    col = lax.broadcasted_iota(jnp.int32, (256, 256), 1)
    source = (col % 128) // 32 * 64 + col // 128 * 32 + col % 32
    turn = jnp.where(row == source, 1.0, 0.0).astype(BF)
    trow = lax.broadcasted_iota(jnp.int32, (64, 128), 0)
    tcol = lax.broadcasted_iota(jnp.int32, (64, 128), 1)
    for t in range(4):
        at = slice(256 * t, 256 * t + 256)
        for n, w in enumerate((wq, wk)):
            qkv[t, :, 256 * n : 256 * n + 256] = jnp.dot(
                w[:, at].astype(BF), turn, preferred_element_type=F32
            ).astype(BF)
        qkv[t, :, 512:768] = wv[:, at].astype(BF)
        pick = jnp.where((trow == tcol + 16 * t) & (tcol < 16), 1.0, 0.0).astype(BF)
        for n, w in enumerate((wi, wg, w2)):
            mlp[t, :, FFP * n : FFP * n + 640] = w[:, 640 * t : 640 * t + 640].astype(BF)
            mlp[t, :, FFP * n + 640 : FFP * n + 768] = jnp.dot(
                w[:, 2560:2624].astype(BF), pick, preferred_element_type=F32
            ).astype(BF)
    wob[...] = wo[...].astype(BF)


def prep(wq, wk, wv, wo, wi, wg, w2):
    return pl.pallas_call(
        prep_kernel,
        out_shape=(
            jax.ShapeDtypeStruct((4, 8, 768), BF),
            jax.ShapeDtypeStruct((8, 1024), BF),
            jax.ShapeDtypeStruct((4, 8, 3 * FFP), BF),
        ),
        compiler_params=params(),
        name="prep",
    )(wq, wk, wv, wo, wi, wg, w2)


def layer_norm(values, gain):
    center = jnp.mean(values, axis=-1, keepdims=True)
    spread = jnp.mean(values * values, axis=-1, keepdims=True) - center * center
    return (values - center) * lax.rsqrt(spread + EPS) * gain


def norm_kernel(h, gain, out):
    out[...] = layer_norm(h[...].astype(F32), gain[...]).astype(BF)


def norm(h, gain):
    rows = h.shape[0]
    return pl.pallas_call(
        norm_kernel,
        grid=(rows // 512,),
        in_specs=[pl.BlockSpec((512, 1024), lambda i: (i, 0)), vmem(1, 1024)],
        out_specs=pl.BlockSpec((512, 1024), lambda i: (i, 0)),
        out_shape=jax.ShapeDtypeStruct((rows, 1024), BF),
        compiler_params=params(),
        name="norm",
    )(h, gain.reshape(1, 1024))


def qkv_kernel(x, w, cos, sin, q, kv, cache):
    row = lax.broadcasted_iota(jnp.int32, (256, 256), 0)
    col = lax.broadcasted_iota(jnp.int32, (256, 256), 1)
    source = (col % 128) // 32 * 64 + col // 128 * 32 + col % 32
    back = jnp.where(source == row, 1.0, 0.0).astype(BF)
    y = jnp.dot(x[...], w[...], preferred_element_type=F32)
    c = cos[...]
    s = sin[...]

    def turned(a, b):
        return jnp.concatenate([a * c - b * s, b * c + a * s], axis=1)

    q[...] = (turned(y[:, :128], y[:, 128:256]).astype(BF).astype(F32) * 0.125).astype(BF)
    k = turned(y[:, 256:384], y[:, 384:512]).astype(BF)
    v = y[:, 512:].astype(BF)
    kv[0] = k
    kv[1] = v
    cache[0] = lax.dot_general(
        k, back, (((1,), (1,)), ((), ())), preferred_element_type=F32
    ).astype(BF)
    cache[1] = v


def qkv_project(x, w, cos, sin):
    rows = x.shape[0]
    n = 512
    return pl.pallas_call(
        qkv_kernel,
        grid=(rows // n,),
        in_specs=[
            pl.BlockSpec((n, 1024), lambda i: (i, 0)),
            vmem(1024, 768),
            pl.BlockSpec((n, 128), lambda i: (i, 0)),
            pl.BlockSpec((n, 128), lambda i: (i, 0)),
        ],
        out_specs=[
            pl.BlockSpec((n, 256), lambda i: (i, 0)),
            pl.BlockSpec((2, n, 256), lambda i: (0, i, 0)),
            pl.BlockSpec((2, n, 256), lambda i: (0, i, 0)),
        ],
        out_shape=(
            jax.ShapeDtypeStruct((rows, 256), BF),
            jax.ShapeDtypeStruct((2, rows, 256), BF),
            jax.ShapeDtypeStruct((2, rows, 256), BF),
        ),
        compiler_params=params(),
        name="qkv",
    )(x, w, cos, sin)


def attend_chunk(start, q4, kv, kseg, qseg, m_sc, l_sc, acc):
    start = pl.multiple_of(start, 128)
    k = kv[0, pl.ds(start, KC), :]
    v = kv[1, pl.ds(start, KC), :]
    same = qseg[...] == kseg[0:1, pl.ds(start, KC)]
    for h in range(4):
        at = slice(h * QB, h * QB + QB)
        s = lax.dot_general(
            q4[at, :], k, (((1,), (1,)), ((), ())), preferred_element_type=F32
        )
        s = jnp.where(same, s, NEG)
        old = m_sc[at, :]
        new = jnp.maximum(old, jnp.max(s, axis=1, keepdims=True))
        p = jnp.exp(s - new)
        fade = jnp.exp(old - new)
        l_sc[at, :] = l_sc[at, :] * fade + jnp.sum(p, axis=1, keepdims=True)
        m_sc[at, :] = new
        acc[at, :] = acc[at, :] * fade + jnp.dot(
            p.astype(BF), v, preferred_element_type=F32
        )


def spread_heads(q, q4):
    lane = lax.broadcasted_iota(jnp.int32, (QB, 256), 1)
    for h in range(4):
        q4[h * QB : h * QB + QB, :] = jnp.where(
            (lane % 128) // 32 == h, q[...].astype(F32), 0.0
        ).astype(BF)


def own_kernel(table, q, qseg, kv, kseg, acc_out, ml_out, q4, m_sc, l_sc, acc):
    i = pl.program_id(0)
    spread_heads(q, q4)
    m_sc[...] = jnp.full_like(m_sc, NEG)
    l_sc[...] = jnp.zeros_like(l_sc)
    acc[...] = jnp.zeros_like(acc)

    @pl.loop(0, table[1, i])
    def _(c):
        attend_chunk(table[0, i] + c * KC, q4, kv, kseg, qseg, m_sc, l_sc, acc)

    lane = lax.broadcasted_iota(jnp.int32, (QB, 256), 1)
    mine = lax.broadcasted_iota(jnp.int32, (QB, 128), 1)
    total = jnp.zeros((QB, 256), F32)
    ml = jnp.zeros((QB, 128), F32)
    for h in range(4):
        at = slice(h * QB, h * QB + QB)
        total = jnp.where(lane // 64 == h, acc[at, :], total)
        ml = jnp.where(mine == h, m_sc[at, :], ml)
        ml = jnp.where(mine == h + 4, l_sc[at, :], ml)
    acc_out[...] = total
    ml_out[...] = ml


def halo_kernel(table, q, qseg, lkv, lseg, rkv, rseg, acc_in, ml_in, out, q4, m_sc, l_sc, acc):
    i = pl.program_id(0)
    spread_heads(q, q4)
    for h in range(4):
        at = slice(h * QB, h * QB + QB)
        m_sc[at, :] = ml_in[:, h : h + 1]
        l_sc[at, :] = ml_in[:, h + 4 : h + 5]
        acc[at, :] = acc_in[...]

    @pl.loop(0, table[3, i])
    def _(c):
        attend_chunk(table[2, i] + c * KC, q4, lkv, lseg, qseg, m_sc, l_sc, acc)

    @pl.loop(0, table[5, i])
    def _(c):
        attend_chunk(table[4, i] + c * KC, q4, rkv, rseg, qseg, m_sc, l_sc, acc)

    lane = lax.broadcasted_iota(jnp.int32, (QB, 256), 1)
    total = jnp.zeros((QB, 256), F32)
    for h in range(4):
        at = slice(h * QB, h * QB + QB)
        total = jnp.where(lane // 64 == h, acc[at, :] / l_sc[at, :], total)
    out[...] = total.astype(BF)


def attn_scratch():
    return [
        pltpu.VMEM((4 * QB, 256), BF),
        pltpu.VMEM((4 * QB, 1), F32),
        pltpu.VMEM((4 * QB, 1), F32),
        pltpu.VMEM((4 * QB, 256), F32),
    ]


def by_block(width):
    return pl.BlockSpec((QB, width), lambda i, *_: (i, 0))


def attend_own(table, q, qseg, kv, kseg):
    rows = q.shape[0]
    return pl.pallas_call(
        own_kernel,
        grid_spec=pltpu.PrefetchScalarGridSpec(
            num_scalar_prefetch=1,
            grid=(rows // QB,),
            in_specs=[by_block(256), by_block(1), vmem(2, rows, 256), vmem(1, rows)],
            out_specs=[by_block(256), by_block(128)],
            scratch_shapes=attn_scratch(),
        ),
        out_shape=(
            jax.ShapeDtypeStruct((rows, 256), F32),
            jax.ShapeDtypeStruct((rows, 128), F32),
        ),
        compiler_params=params(),
        name="attend_own",
    )(table, q, qseg, kv, kseg)


def attend_halo(table, q, qseg, lkv, lseg, rkv, rseg, acc, ml):
    rows = q.shape[0]
    return pl.pallas_call(
        halo_kernel,
        grid_spec=pltpu.PrefetchScalarGridSpec(
            num_scalar_prefetch=1,
            grid=(rows // QB,),
            in_specs=[
                by_block(256),
                by_block(1),
                vmem(2, rows, 256),
                vmem(1, rows),
                vmem(2, rows, 256),
                vmem(1, rows),
                by_block(256),
                by_block(128),
            ],
            out_specs=by_block(256),
            scratch_shapes=attn_scratch(),
        ),
        out_shape=jax.ShapeDtypeStruct((rows, 256), BF),
        compiler_params=params(),
        name="attend_halo",
    )(table, q, qseg, lkv, lseg, rkv, rseg, acc, ml)


def contract_last(a, b):
    return lax.dot_general(a, b, (((1,), (1,)), ((), ())), preferred_element_type=F32)


def mlp_kernel(order, m0, m1, m2, m3, h, o0, o1, o2, o3, gain, wi, wg, d0, d1, d2, d3, keep, send):
    mixed = (m0, m1, m2, m3)
    outs = (o0, o1, o2, o3)
    downs = (d0, d1, d2, d3)
    summed = h[...].astype(F32)
    total = contract_last(m0[...], o0[...])
    for a, b in zip(mixed[1:], outs[1:]):
        total += contract_last(a[...], b[...])
    first = (summed + total).astype(BF)
    wide = first.astype(F32)
    normed = layer_norm(wide, gain[...]).astype(BF)
    a = jnp.dot(normed, wi[...], preferred_element_type=F32)
    b = jnp.dot(normed, wg[...], preferred_element_type=F32)
    inner = (0.5 * a * (1.0 + lax.erf(a * (0.5**0.5))) * b).astype(BF)
    mine = jnp.zeros((h.shape[0], 256), F32)
    for t in range(4):
        mine = jnp.where(order[0] == t, wide[:, 256 * t : 256 * t + 256], mine)
    keep[:, :256] = contract_last(inner, downs[0][...]) + mine
    keep[:, 256:] = contract_last(inner, downs[1][...])
    send[:, :256] = contract_last(inner, downs[2][...]).astype(BF)
    send[:, 256:] = contract_last(inner, downs[3][...]).astype(BF)


def mlp(order, mixed, h, wo, gain, weights, part, parts):
    rows = h.shape[0] // parts
    n = 256
    steps = rows // n
    base = part * steps

    def rowblock(width):
        return pl.BlockSpec((n, width), lambda i, *_: (i + base, 0))

    def outblock(width):
        return pl.BlockSpec((n, width), lambda i, *_: (i, 0))

    return pl.pallas_call(
        mlp_kernel,
        grid_spec=pltpu.PrefetchScalarGridSpec(
            num_scalar_prefetch=1,
            grid=(steps,),
            in_specs=[rowblock(256)] * 4
            + [rowblock(1024)]
            + [pl.BlockSpec((1024, 256), lambda i, s, m=m: (0, s[m])) for m in range(4)]
            + [vmem(1, 1024)]
            + [
                pl.BlockSpec((1024, FFP), lambda i, s: (0, 0)),
                pl.BlockSpec((1024, FFP), lambda i, s: (0, 1)),
            ]
            + [pl.BlockSpec((256, FFP), lambda i, s, m=m: (s[m], 2)) for m in range(4)],
            out_specs=[outblock(512), outblock(512)],
        ),
        out_shape=(
            jax.ShapeDtypeStruct((rows, 512), F32),
            jax.ShapeDtypeStruct((rows, 512), BF),
        ),
        compiler_params=params(),
        name="mlp",
    )(order, *mixed, h, wo, wo, wo, wo, gain.reshape(1, 1024), weights, weights, *([weights] * 4))


def swap(x, bit):
    return lax.ppermute(x, "tp", [(i, i ^ bit) for i in range(4)])


def shift(x, by):
    count = lax.axis_size("req")
    return lax.ppermute(x, "req", [(i, i + by) for i in range(count) if 0 <= i + by < count])


def exchange(x, axes):
    return lax.all_to_all(x, axes, split_axis=0, concat_axis=0, tiled=True)


def body(
    hidden_in,
    lengths,
    tenant,
    shard_map,
    wq,
    wk,
    wv,
    wo,
    wi_in,
    wi_gate,
    wo2,
    head,
    attn_gain,
    mlp_gain,
    final_gain,
):
    req_count = lax.axis_size("req")
    tp_count = lax.axis_size("tp")
    count = req_count * tp_count
    req_index = lax.axis_index("req")
    tp_index = lax.axis_index("tp")
    slots, width = hidden_in.shape
    requests = lengths.shape[0]

    qkv_block, out_block, mlp_block = prep(wq, wk, wv, wo, wi_in, wi_gate, wo2)
    place = jnp.arange(count, dtype=jnp.int32)
    source = jnp.sum(
        jnp.where(shard_map[None, :] == place[:, None], place[None, :], 0), axis=1
    )
    qkv_all = exchange(
        jnp.broadcast_to(qkv_block[None], (req_count, 4, 8, 768)).reshape(count, 8, 768), BOTH
    )
    qkv_w = qkv_all[source].reshape(width, 768)
    mlp_rows = exchange(mlp_block, "tp")
    mlp_all = lax.all_gather(mlp_rows.reshape(4 * 8, 3 * FFP), "req", axis=0, tiled=True)
    mlp_w = mlp_all.reshape(count, 8, 3 * FFP)[source].reshape(width, 3 * FFP)

    ends = jnp.cumsum(lengths)
    base = req_index * slots
    index = base - slots + jnp.arange(3 * slots, dtype=jnp.int32)
    segment = jnp.sum((ends[None, :] <= index[:, None]).astype(jnp.int32), axis=1)
    segment = jnp.where((index >= 0) & (index < slots * req_count), segment, -1)
    own = base + jnp.arange(slots, dtype=jnp.int32)
    start_of = jnp.max(jnp.where(ends[None, :] <= own[:, None], ends[None, :], 0), axis=1)
    position = (own - start_of).astype(F32)
    half = HEAD_DIM // 2
    lane = jnp.arange(128, dtype=jnp.int32) % half
    freq = THETA ** (-(2.0 * lane.astype(F32)) / HEAD_DIM)
    angle = position[:, None] * freq[None, :]
    cos = jnp.cos(angle)
    sin = jnp.sin(angle)
    begin = base + jnp.arange(slots // QB, dtype=jnp.int32) * QB
    close = begin + QB - 1
    low = jnp.max(jnp.where(ends[None, :] <= begin[:, None], ends[None, :], 0), axis=1) - base
    high = jnp.min(jnp.where(ends[None, :] > close[:, None], ends[None, :], 1 << 30), axis=1) - base

    def span(lo, hi):
        lo = jnp.maximum(lo, 0) // 128 * 128
        n = jnp.maximum((hi - lo + KC - 1) // KC, 0)
        return jnp.minimum(lo, slots - n * KC), n

    own_lo, own_n = span(low, jnp.minimum(high, slots))
    left_lo, left_n = span(jnp.minimum(low, 0) + slots, jnp.full_like(low, slots))
    right_lo, right_n = span(jnp.zeros_like(high), high - slots)
    table = jnp.stack([own_lo, own_n, left_lo, left_n, right_lo, right_n])
    segs = segment.reshape(3, 1, slots)
    qseg = segment[slots : 2 * slots].reshape(slots, 1)

    normed = norm(hidden_in, attn_gain)
    query, kv, cache = qkv_project(normed, qkv_w, cos, sin)
    left = shift(kv, 1)
    right = shift(kv, -1)
    out_all = exchange(
        jnp.broadcast_to(out_block[None], (count, 8, width)), BOTH
    )
    out_w = out_all[source].reshape(width, width)
    acc, ml = attend_own(table, query, qseg, kv, segs[1])
    mixed = attend_halo(table, query, qseg, left, segs[0], right, segs[2], acc, ml)

    far = swap(mixed, 2)
    near = swap(mixed, 1)
    both = swap(far, 1)
    order = tp_index ^ jnp.array([0, 2, 1, 3], jnp.int32)
    parts = 2
    pieces = []
    for part in range(parts):
        keep, send = mlp(
            order, (mixed, far, near, both), hidden_in, out_w, mlp_gain, mlp_w, part, parts
        )
        got = swap(send, 1).astype(F32)
        other = swap((keep[:, 256:] + got[:, 256:]).astype(BF), 2).astype(F32)
        pieces.append((keep[:, :256] + got[:, :256] + other).astype(BF))
    hidden_out = jnp.concatenate(pieces, axis=0)

    last_slot = ends - 1 - base
    holds = (last_slot >= 0) & (last_slot < slots)
    picked = jnp.where(holds[:, None], hidden_out[jnp.clip(last_slot, 0, slots - 1)], 0)
    each = requests // req_count
    mine = exchange(picked.reshape(req_count, each, 256), "req").astype(F32).sum(axis=0).astype(BF)
    spread = exchange(jnp.broadcast_to(mine[None], (count, each, 256)), BOTH)
    last = (
        spread.reshape(req_count, tp_count, each, 256)
        .transpose(0, 2, 1, 3)
        .reshape(requests, width)
        .astype(F32)
    )
    last_rms = jnp.sqrt(jnp.mean(last * last, axis=-1))
    choose = (tenant[:, None] == jnp.arange(final_gain.shape[0], dtype=jnp.int32)[None, :]).astype(
        F32
    )
    gain_rows = jnp.dot(
        choose, final_gain, precision=lax.Precision.HIGHEST, preferred_element_type=F32
    )
    final = layer_norm(last, gain_rows).astype(BF)
    logits = contract_last(final, head.astype(BF))
    top = jnp.max(logits, axis=-1)
    tops = exchange(jnp.broadcast_to(top[None], (count, requests)), BOTH)
    top_logit = jnp.max(tops, axis=0)
    return (hidden_out, cache, last_rms, top_logit)


def solution(mesh):
    rows = P(BOTH, None)
    placed = (P("req", None), P(), P(), P()) + (rows,) * 8 + (P(), P(), P())
    return jax.shard_map(
        body,
        mesh=mesh,
        in_specs=placed,
        out_specs=(P("req", "tp"), P(None, "req", "tp"), P(), P()),
        check_vma=False,
    )
```

```python
import functools

import jax
import jax.numpy as jnp
from jax import lax
from jax.experimental import pallas as pl
from jax.experimental.pallas import tpu as pltpu
from jax.sharding import PartitionSpec as P

HEADS = 16
HEAD_DIM = 64
THETA = 160000.0
EPS = 1e-05
BF = jnp.bfloat16
F32 = jnp.float32
BOTH = ("req", "tp")
NEG = -1e30
FFP = 768
REST = 3 * FFP + 1024
QB = 256
KC = 512


def vmem(*shape):
    return pl.BlockSpec(shape, lambda *_: (0,) * len(shape))


def params(mib):
    return pltpu.CompilerParams(vmem_limit_bytes=mib * 1024 * 1024)


def cost(flops, moved, transcendentals=0):
    return pl.CostEstimate(flops=flops, bytes_accessed=moved, transcendentals=transcendentals)


def prep_kernel(wq, wk, wv, wo, wi, wg, w2, qkv, rest):
    row = lax.broadcasted_iota(jnp.int32, (256, 256), 0)
    col = lax.broadcasted_iota(jnp.int32, (256, 256), 1)
    source = (col % 128) // 32 * 64 + col // 128 * 32 + col % 32
    turn = jnp.where(row == source, 1.0, 0.0).astype(BF)
    trow = lax.broadcasted_iota(jnp.int32, (64, 128), 0)
    tcol = lax.broadcasted_iota(jnp.int32, (64, 128), 1)
    for t in range(4):
        at = slice(256 * t, 256 * t + 256)
        q, k = (
            jnp.dot(w[:, at].astype(BF), turn, preferred_element_type=F32).astype(BF)
            for w in (wq, wk)
        )
        mine = jnp.concatenate([q, k, wv[:, at].astype(BF)], axis=1)
        for r in range(qkv.shape[0]):
            qkv[r, t] = mine
        pick = jnp.where((trow == tcol + 16 * t) & (tcol < 16), 1.0, 0.0).astype(BF)
        for n, w in enumerate((wi, wg, w2)):
            rest[t, :, FFP * n : FFP * n + 640] = w[:, 640 * t : 640 * t + 640].astype(BF)
            rest[t, :, FFP * n + 640 : FFP * n + 768] = jnp.dot(
                w[:, 2560:2624].astype(BF), pick, preferred_element_type=F32
            ).astype(BF)
        rest[t, :, 3 * FFP :] = wo[...].astype(BF)


def prep(req_count, *weights):
    return pl.pallas_call(
        prep_kernel,
        out_shape=(
            jax.ShapeDtypeStruct((req_count, 4, 8, 768), BF),
            jax.ShapeDtypeStruct((4, 8, REST), BF),
        ),
        compiler_params=params(24),
        name="prep",
    )(*weights)


def layer_norm(values, gain):
    center = jnp.mean(values, axis=-1, keepdims=True)
    spread = jnp.mean(values * values, axis=-1, keepdims=True) - center * center
    return (values - center) * lax.rsqrt(spread + EPS) * gain


def norm_kernel(h, gain, out):
    out[...] = layer_norm(h[...].astype(F32), gain[...]).astype(BF)


def norm(h, gain):
    rows = h.shape[0]
    return pl.pallas_call(
        norm_kernel,
        grid=(rows // 512,),
        in_specs=[pl.BlockSpec((512, 1024), lambda i: (i, 0)), vmem(1, 1024)],
        out_specs=pl.BlockSpec((512, 1024), lambda i: (i, 0)),
        out_shape=jax.ShapeDtypeStruct((rows, 1024), BF),
        compiler_params=params(24),
        cost_estimate=cost(1 << 24, 1 << 23),
        name="norm",
    )(h, gain.reshape(1, 1024))


def qkv_kernel(x, w, cos, sin, q, key, vt, cache):
    row = lax.broadcasted_iota(jnp.int32, (256, 256), 0)
    col = lax.broadcasted_iota(jnp.int32, (256, 256), 1)
    source = (col % 128) // 32 * 64 + col // 128 * 32 + col % 32
    back = jnp.where(source == row, 1.0, 0.0).astype(BF)
    y = jnp.dot(x[...], w[...], preferred_element_type=F32)
    c = cos[...]
    s = sin[...]

    def turned(a, b):
        return jnp.concatenate([a * c - b * s, b * c + a * s], axis=1)

    q[...] = (turned(y[:, :128], y[:, 128:256]).astype(BF).astype(F32) * 0.125).astype(BF)
    k = turned(y[:, 256:384], y[:, 384:512]).astype(BF)
    v = y[:, 512:].astype(BF)
    key[...] = k
    vt[...] = jnp.transpose(v)
    cache[0] = lax.dot_general(
        k, back, (((1,), (1,)), ((), ())), preferred_element_type=F32
    ).astype(BF)
    cache[1] = v


def qkv_project(x, w, cos, sin):
    rows = x.shape[0]
    n = 512
    return pl.pallas_call(
        qkv_kernel,
        grid=(rows // n,),
        in_specs=[
            pl.BlockSpec((n, 1024), lambda i: (i, 0)),
            vmem(1024, 768),
            pl.BlockSpec((n, 128), lambda i: (i, 0)),
            pl.BlockSpec((n, 128), lambda i: (i, 0)),
        ],
        out_specs=[
            pl.BlockSpec((n, 256), lambda i: (i, 0)),
            pl.BlockSpec((n, 256), lambda i: (i, 0)),
            pl.BlockSpec((256, n), lambda i: (0, i)),
            pl.BlockSpec((2, n, 256), lambda i: (0, i, 0)),
        ],
        out_shape=(
            jax.ShapeDtypeStruct((rows, 256), BF),
            jax.ShapeDtypeStruct((rows, 256), BF),
            jax.ShapeDtypeStruct((256, rows), BF),
            jax.ShapeDtypeStruct((2, rows, 256), BF),
        ),
        compiler_params=params(32),
        cost_estimate=cost(2 * rows * 1024 * 768, 12 << 20),
        name="qkv",
    )(x, w, cos, sin)


VR = HEAD_DIM + 8


def attend_chunk(start, size, qm, key, vt, kseg, qseg, m_sc, acc):
    start = pl.multiple_of(start, 128)
    k = key[pl.ds(start, size), :]
    same = kseg[pl.ds(start, size), 0:1] == qseg[...]
    ones = jnp.ones((8, size), BF)
    scores = []
    for h in range(4):
        s = contract_last(k, qm[h])
        scores.append(jnp.where(same, s, NEG))
    for h in range(4):
        old = m_sc[h]
        new = jnp.maximum(old, jnp.max(scores[h], axis=0, keepdims=True))
        p = jnp.exp(scores[h] - new).astype(BF)
        fade = jnp.exp(old - new)
        m_sc[h] = new
        v = jnp.concatenate(
            [vt[HEAD_DIM * h : HEAD_DIM * h + HEAD_DIM, pl.ds(start, size)], ones], axis=0
        )
        acc[h] = acc[h] * fade + jnp.dot(v, p, preferred_element_type=F32)


def attend_span(table, at, i, *refs):
    start = table[at, i]
    whole = table[at + 1, i] // 2

    @pl.loop(0, whole)
    def _(c):
        attend_chunk(start + c * KC, KC, *refs)

    @pl.when(table[at + 1, i] % 2 == 1)
    def _():
        attend_chunk(start + whole * KC, KC // 2, *refs)


def spread_heads(q, qm):
    lane = lax.broadcasted_iota(jnp.int32, (QB, 256), 1)
    for h in range(4):
        qm[h] = jnp.where((lane % 128) // 32 == h, q[...].astype(F32), 0.0).astype(BF)


def own_kernel(table, q, qseg, key, vt, kseg, acc_out, m_out, qm, m_sc, acc):
    i = pl.program_id(0)
    spread_heads(q, qm)
    m_sc[...] = jnp.full_like(m_sc, NEG)
    acc[...] = jnp.zeros_like(acc)
    attend_span(table, 0, i, qm, key, vt, kseg, qseg, m_sc, acc)
    acc_out[...] = acc[...]
    m_out[...] = m_sc[...]


def halo_kernel(
    base, table, q, qseg, lkey, lvt, lseg, rkey, rvt, rseg, acc_in, m_in, last, out, picked, qm, m_sc, acc
):
    i = pl.program_id(0) + base
    spread_heads(q, qm)
    m_sc[...] = m_in[...]
    acc[...] = acc_in[...]
    attend_span(table, 2, i, qm, lkey, lvt, lseg, qseg, m_sc, acc)
    attend_span(table, 4, i, qm, rkey, rvt, rseg, qseg, m_sc, acc)
    heads = [acc[h, :HEAD_DIM] / acc[h, HEAD_DIM : HEAD_DIM + 1] for h in range(4)]
    mixed = jnp.transpose(jnp.concatenate(heads, axis=0)).astype(BF)
    out[...] = mixed
    slot = lax.broadcasted_iota(jnp.int32, (last.shape[0], QB), 1) + i * QB
    mine = jnp.where(last[...] == slot, 1.0, 0.0).astype(BF)

    @pl.when(pl.program_id(0) == 0)
    def _():
        picked[...] = jnp.zeros_like(picked)

    picked[...] += jnp.dot(mine, mixed, preferred_element_type=F32)


def attn_scratch():
    return [
        pltpu.VMEM((4, QB, 256), BF),
        pltpu.VMEM((4, 1, QB), F32),
        pltpu.VMEM((4, VR, QB), F32),
    ]


def attend_own(table, q, qseg, key, vt, kseg):
    rows = q.shape[0]
    return pl.pallas_call(
        own_kernel,
        grid_spec=pltpu.PrefetchScalarGridSpec(
            num_scalar_prefetch=1,
            grid=(rows // QB,),
            in_specs=[
                pl.BlockSpec((QB, 256), lambda i, *_: (i, 0)),
                pl.BlockSpec((1, QB), lambda i, *_: (0, i)),
                vmem(rows, 256),
                vmem(256, rows),
                vmem(rows, 1),
            ],
            out_specs=[
                pl.BlockSpec((4, VR, QB), lambda i, *_: (0, 0, i)),
                pl.BlockSpec((4, 1, QB), lambda i, *_: (0, 0, i)),
            ],
            scratch_shapes=attn_scratch(),
        ),
        out_shape=(
            jax.ShapeDtypeStruct((4, VR, rows), F32),
            jax.ShapeDtypeStruct((4, 1, rows), F32),
        ),
        compiler_params=params(32),
        cost_estimate=cost(20 << 30, 8 << 20, 12 << 20),
        name="attend_own",
    )(table, q, qseg, key, vt, kseg)


def attend_halo(part, parts, table, q, qseg, lkey, lvt, lseg, rkey, rvt, rseg, acc, m, last):
    rows = q.shape[0]
    steps = rows // QB // parts
    base = part * steps
    return pl.pallas_call(
        functools.partial(halo_kernel, base),
        grid_spec=pltpu.PrefetchScalarGridSpec(
            num_scalar_prefetch=1,
            grid=(steps,),
            in_specs=[
                pl.BlockSpec((QB, 256), lambda i, *_: (i + base, 0)),
                pl.BlockSpec((1, QB), lambda i, *_: (0, i + base)),
                vmem(rows, 256),
                vmem(256, rows),
                vmem(rows, 1),
                vmem(rows, 256),
                vmem(256, rows),
                vmem(rows, 1),
                pl.BlockSpec((4, VR, QB), lambda i, *_: (0, 0, i + base)),
                pl.BlockSpec((4, 1, QB), lambda i, *_: (0, 0, i + base)),
                vmem(*last.shape),
            ],
            out_specs=[pl.BlockSpec((QB, 256), lambda i, *_: (i, 0)), vmem(last.shape[0], 256)],
            scratch_shapes=attn_scratch(),
        ),
        out_shape=(
            jax.ShapeDtypeStruct((rows // parts, 256), BF),
            jax.ShapeDtypeStruct((last.shape[0], 256), F32),
        ),
        compiler_params=params(40),
        cost_estimate=cost(8 << 30, 8 << 20, 6 << 20),
        name="attend_halo",
    )(table, q, qseg, lkey, lvt, lseg, rkey, rvt, rseg, acc, m, last)


def contract_last(a, b):
    return lax.dot_general(a, b, (((1,), (1,)), ((), ())), preferred_element_type=F32)


def mlp_kernel(table, m0, m1, m2, m3, h, gain, weights, keep, send, w, sem):
    count = weights.shape[0]

    @pl.when(pl.program_id(0) == 0)
    def _():
        @pl.loop(0, count)
        def _(k):
            pltpu.make_async_copy(weights.at[table[4 + k]], w.at[k], sem).start()

        pltpu.make_async_copy(weights, w, sem).wait()

    def rows(at, size, lo, width):
        return w[pl.ds(at, size), :, pl.ds(lo, width)].reshape(8 * size, width)

    n = h.shape[0]
    wide = h[...].astype(F32)
    total = None
    for j, m in enumerate((m0, m1, m2, m3)):
        lo = pl.multiple_of(3 * FFP + 256 * table[j], 128)
        piece = contract_last(m[...], rows(0, count, lo, 256))
        total = piece if total is None else total + piece
    first = (wide + total).astype(BF)
    wide = first.astype(F32)
    normed = layer_norm(wide, gain[...]).astype(BF)
    a = jnp.dot(normed, rows(0, count, 0, FFP), preferred_element_type=F32)
    b = jnp.dot(normed, rows(0, count, FFP, FFP), preferred_element_type=F32)
    inner = (0.5 * a * (1.0 + lax.erf(a * (0.5**0.5))) * b).astype(BF)
    mine = jnp.zeros((n, 256), F32)
    for t in range(4):
        mine = jnp.where(table[0] == t, wide[:, 256 * t : 256 * t + 256], mine)

    def down(j):
        return contract_last(inner, rows(table[j] * (count // 4), count // 4, 2 * FFP, FFP))

    keep[:, :256] = down(0) + mine
    keep[:, 256:] = down(1)
    send[:, :256] = down(2).astype(BF)
    send[:, 256:] = down(3).astype(BF)


def mlp(table, mixed, h, base, gain, weights, n):
    rows = mixed[0].shape[0]
    count = weights.shape[0]

    def block(width):
        return pl.BlockSpec((n, width), lambda i, *_: (i, 0))

    return pl.pallas_call(
        mlp_kernel,
        grid_spec=pltpu.PrefetchScalarGridSpec(
            num_scalar_prefetch=1,
            grid=(rows // n,),
            in_specs=[block(256)] * 4
            + [pl.BlockSpec((n, 1024), lambda i, *_: (i + base, 0))]
            + [vmem(1, 1024), pl.BlockSpec(memory_space=pl.ANY)],
            out_specs=[block(512), block(512)],
            scratch_shapes=[pltpu.VMEM((count, 8, REST), BF), pltpu.SemaphoreType.DMA(())],
        ),
        out_shape=(
            jax.ShapeDtypeStruct((rows, 512), F32),
            jax.ShapeDtypeStruct((rows, 512), BF),
        ),
        compiler_params=params(40),
        cost_estimate=cost(rows * 1024 * (1024 + 3 * FFP) * 2, 12 << 20, rows * FFP),
        name="mlp",
    )(table, *mixed, h, gain.reshape(1, 1024), weights)


def gather_tp(x):
    far = swap(x, 2)
    return x, far, swap(x, 1), swap(far, 1)


def reduce_tp(keep, send):
    got = swap(send, 1).astype(F32)
    other = swap((keep[:, 256:] + got[:, 256:]).astype(BF), 2).astype(F32)
    return (keep[:, :256] + got[:, :256] + other).astype(BF)


def swap(x, bit):
    return lax.ppermute(x, "tp", [(i, i ^ bit) for i in range(4)])


def shift(x, by):
    count = lax.axis_size("req")
    return lax.ppermute(x, "req", [(i, i + by) for i in range(count) if 0 <= i + by < count])


def exchange(x, axes):
    return lax.all_to_all(x, axes, split_axis=0, concat_axis=0, tiled=True)


def body(
    hidden_in,
    lengths,
    tenant,
    shard_map,
    wq,
    wk,
    wv,
    wo,
    wi_in,
    wi_gate,
    wo2,
    head,
    attn_gain,
    mlp_gain,
    final_gain,
):
    req_count = lax.axis_size("req")
    tp_count = lax.axis_size("tp")
    count = req_count * tp_count
    req_index = lax.axis_index("req")
    tp_index = lax.axis_index("tp")
    slots, width = hidden_in.shape
    requests = lengths.shape[0]

    qkv_block, rest_block = prep(req_count, wq, wk, wv, wo, wi_in, wi_gate, wo2)
    place = jnp.arange(count, dtype=jnp.int32)
    source = jnp.sum(
        jnp.where(shard_map[None, :] == place[:, None], place[None, :], 0), axis=1
    )
    qkv_all = exchange(qkv_block.reshape(count, 8, 768), BOTH)
    qkv_w = qkv_all[source].reshape(width, 768)
    rest_rows = exchange(rest_block, "tp")
    rest = lax.all_gather(rest_rows.reshape(4 * 8, REST), "req", axis=0, tiled=True)
    rest = rest.reshape(count, 8, REST)

    ends = jnp.cumsum(lengths)
    base = req_index * slots
    index = base - slots + jnp.arange(3 * slots, dtype=jnp.int32)
    segment = jnp.sum((ends[None, :] <= index[:, None]).astype(jnp.int32), axis=1)
    segment = jnp.where((index >= 0) & (index < slots * req_count), segment, -1)
    own = base + jnp.arange(slots, dtype=jnp.int32)
    start_of = jnp.max(jnp.where(ends[None, :] <= own[:, None], ends[None, :], 0), axis=1)
    position = (own - start_of).astype(F32)
    half = HEAD_DIM // 2
    lane = jnp.arange(128, dtype=jnp.int32) % half
    freq = THETA ** (-(2.0 * lane.astype(F32)) / HEAD_DIM)
    angle = position[:, None] * freq[None, :]
    cos = jnp.cos(angle)
    sin = jnp.sin(angle)
    begin = base + jnp.arange(slots // QB, dtype=jnp.int32) * QB
    close = begin + QB - 1
    low = jnp.max(jnp.where(ends[None, :] <= begin[:, None], ends[None, :], 0), axis=1) - base
    high = jnp.min(jnp.where(ends[None, :] > close[:, None], ends[None, :], 1 << 30), axis=1) - base

    def span(lo, hi):
        lo = jnp.maximum(lo, 0) // 128 * 128
        n = jnp.maximum((hi - lo + KC // 2 - 1) // (KC // 2), 0)
        return jnp.minimum(lo, slots - n * (KC // 2)), n

    own_lo, own_n = span(low, jnp.minimum(high, slots))
    left_lo, left_n = span(jnp.minimum(low, 0) + slots, jnp.full_like(low, slots))
    right_lo, right_n = span(jnp.zeros_like(high), high - slots)
    table = jnp.stack([own_lo, own_n, left_lo, left_n, right_lo, right_n])
    segs = segment.reshape(3, slots, 1)
    qseg = segment[slots : 2 * slots].reshape(1, slots)

    normed = norm(hidden_in, attn_gain)
    query, key, vt, cache = qkv_project(normed, qkv_w, cos, sin)
    halo = (shift(key, 1), shift(vt, 1), segs[0], shift(key, -1), shift(vt, -1), segs[2])
    acc, m = attend_own(table, query, qseg, key, vt, segs[1])
    last_slot = ends - 1 - base
    holds = (last_slot >= 0) & (last_slot < slots)
    parts = 2
    halves = [
        attend_halo(part, parts, table, query, qseg, *halo, acc, m, last_slot.reshape(requests, 1))
        for part in range(parts)
    ]

    order = jnp.concatenate([tp_index ^ jnp.array([0, 2, 1, 3], jnp.int32), source])
    hidden_out = jnp.concatenate(
        [
            reduce_tp(
                *mlp(
                    order,
                    gather_tp(half[0]),
                    hidden_in,
                    part * (slots // parts // 256),
                    mlp_gain,
                    rest,
                    256,
                )
            )
            for part, half in enumerate(halves)
        ],
        axis=0,
    )

    each = requests // req_count
    rows = 16
    quarter = lax.dynamic_slice_in_dim(hidden_in, tp_index * 256, 256, 1)
    picked_in = jnp.where(holds[:, None], quarter[jnp.clip(last_slot, 0, slots - 1)], 0)
    picked_mixed = sum(half[1] for half in halves).astype(BF)
    picked = jnp.concatenate([picked_mixed, picked_in], axis=1)
    taken = exchange(picked.reshape(req_count, each, 512), "req").astype(F32).sum(axis=0).astype(BF)
    taken = gather_tp(jnp.pad(taken, ((0, rows - each), (0, 0))))
    pieces = jnp.stack([piece[:, 256:] for piece in taken])
    place_of = jnp.array([0, 2, 1, 3], jnp.int32)[jnp.arange(4, dtype=jnp.int32) ^ tp_index]
    whole_in = pieces[place_of].transpose(1, 0, 2).reshape(rows, width)
    last_mine = reduce_tp(
        *mlp(order, [piece[:, :256] for piece in taken], whole_in, 0, mlp_gain, rest, rows)
    )[:each]
    spread = exchange(jnp.broadcast_to(last_mine[None], (count, each, 256)), BOTH)
    last = (
        spread.reshape(req_count, tp_count, each, 256)
        .transpose(0, 2, 1, 3)
        .reshape(requests, width)
        .astype(F32)
    )
    last_rms = jnp.sqrt(jnp.mean(last * last, axis=-1))
    choose = (tenant[:, None] == jnp.arange(final_gain.shape[0], dtype=jnp.int32)[None, :]).astype(
        F32
    )
    gain_rows = jnp.dot(
        choose, final_gain, precision=lax.Precision.HIGHEST, preferred_element_type=F32
    )
    final = layer_norm(last, gain_rows).astype(BF)
    logits = contract_last(final, head.astype(BF))
    top = jnp.max(logits, axis=-1)
    tops = exchange(jnp.broadcast_to(top[None], (count, requests)), BOTH)
    top_logit = jnp.max(tops, axis=0)
    return (hidden_out, cache, last_rms, top_logit)


def solution(mesh):
    rows = P(BOTH, None)
    placed = (P("req", None), P(), P(), P()) + (rows,) * 8 + (P(), P(), P())
    return jax.shard_map(
        body,
        mesh=mesh,
        in_specs=placed,
        out_specs=(P("req", "tp"), P(None, "req", "tp"), P(), P()),
        check_vma=False,
    )
```

```python
import functools

import jax
import jax.numpy as jnp
from jax import lax
from jax.experimental import pallas as pl
from jax.experimental.pallas import tpu as pltpu
from jax.sharding import PartitionSpec as P

HEADS = 16
HEAD_DIM = 64
THETA = 160000.0
EPS = 1e-05
BF = jnp.bfloat16
F32 = jnp.float32
BOTH = ("req", "tp")
NEG = -1e30
FFP = 768
REST = 3 * FFP + 1024
QB = 256
KB = 256


def vmem(*shape):
    return pl.BlockSpec(shape, lambda *_: (0,) * len(shape))


def params():
    return pltpu.CompilerParams(vmem_limit_bytes=60 * 1024 * 1024)


def cost(flops, moved, transcendentals=0):
    return pl.CostEstimate(flops=flops, bytes_accessed=moved, transcendentals=transcendentals)


def prep_kernel(order, wq, wk, wv, wo, wi, wg, w2, qkv, rest):
    row = lax.broadcasted_iota(jnp.int32, (256, 256), 0)
    col = lax.broadcasted_iota(jnp.int32, (256, 256), 1)
    source = (col % 128) // 32 * 64 + col // 128 * 32 + col % 32
    turn = jnp.where(row == source, 1.0, 0.0).astype(BF)
    trow = lax.broadcasted_iota(jnp.int32, (64, 128), 0)
    tcol = lax.broadcasted_iota(jnp.int32, (64, 128), 1)
    for t in range(4):
        at = slice(256 * t, 256 * t + 256)
        q, k = (
            jnp.dot(w[:, at].astype(BF), turn, preferred_element_type=F32).astype(BF)
            for w in (wq, wk)
        )
        mine = jnp.concatenate([q, k, wv[:, at].astype(BF)], axis=1)
        for r in range(qkv.shape[0]):
            qkv[r, t] = mine
        pick = jnp.where((trow == tcol + 16 * t) & (tcol < 16), 1.0, 0.0).astype(BF)
        to = order[t]
        for n, w in enumerate((wi, wg, w2)):
            rest[to, :, FFP * n : FFP * n + 640] = w[:, 640 * t : 640 * t + 640].astype(BF)
            rest[to, :, FFP * n + 640 : FFP * n + 768] = jnp.dot(
                w[:, 2560:2624].astype(BF), pick, preferred_element_type=F32
            ).astype(BF)
        rest[to, :, 3 * FFP :] = wo[...].astype(BF)


def prep(req_count, order, *weights):
    return pl.pallas_call(
        prep_kernel,
        in_specs=[pl.BlockSpec(memory_space=pltpu.SMEM)] + [vmem(*w.shape) for w in weights],
        out_shape=(
            jax.ShapeDtypeStruct((req_count, 4, 8, 768), BF),
            jax.ShapeDtypeStruct((4, 8, REST), BF),
        ),
        compiler_params=params(),
        name="prep",
    )(order, *weights)


def layer_norm(values, gain):
    center = jnp.mean(values, axis=-1, keepdims=True)
    spread = jnp.mean(values * values, axis=-1, keepdims=True) - center * center
    return (values - center) * lax.rsqrt(spread + EPS) * gain


def norm_kernel(h, gain, out):
    out[...] = layer_norm(h[...].astype(F32), gain[...]).astype(BF)


def norm(h, gain):
    rows = h.shape[0]
    return pl.pallas_call(
        norm_kernel,
        grid=(rows // 512,),
        in_specs=[pl.BlockSpec((512, 1024), lambda i: (i, 0)), vmem(1, 1024)],
        out_specs=pl.BlockSpec((512, 1024), lambda i: (i, 0)),
        out_shape=jax.ShapeDtypeStruct((rows, 1024), BF),
        compiler_params=params(),
        cost_estimate=cost(1 << 24, 1 << 23),
        name="norm",
    )(h, gain.reshape(1, 1024))


def qkv_kernel(x, w, cos, sin, q, low, high, cache):
    row = lax.broadcasted_iota(jnp.int32, (256, 256), 0)
    col = lax.broadcasted_iota(jnp.int32, (256, 256), 1)
    source = (col % 128) // 32 * 64 + col // 128 * 32 + col % 32
    back = jnp.where(source == row, 1.0, 0.0).astype(BF)
    y = jnp.dot(x[...], w[...], preferred_element_type=F32)
    c = cos[...]
    s = sin[...]

    def turned(a, b):
        return jnp.concatenate([a * c - b * s, b * c + a * s], axis=1)

    q[...] = (turned(y[:, :128], y[:, 128:256]).astype(BF).astype(F32) * 0.125).astype(BF)
    k = turned(y[:, 256:384], y[:, 384:512]).astype(BF)
    v = y[:, 512:].astype(BF)
    i = pl.program_id(0)
    half = pl.num_programs(0) // 2
    blocks = x.shape[0] // KB
    for part, ref in enumerate((low, high)):

        @pl.when(i // half == part)
        def _():
            for n in range(blocks):
                at = (i - part * half) * blocks + n
                ref[at, 0] = k[KB * n : KB * n + KB]
                ref[at, 1] = jnp.transpose(v[KB * n : KB * n + KB])

    cache[0] = lax.dot_general(
        k, back, (((1,), (1,)), ((), ())), preferred_element_type=F32
    ).astype(BF)
    cache[1] = v


def qkv_project(x, w, cos, sin):
    rows = x.shape[0]
    n = 512
    pairs = (rows // KB // 2, 2, KB, 256)
    return pl.pallas_call(
        qkv_kernel,
        grid=(rows // n,),
        in_specs=[
            pl.BlockSpec((n, 1024), lambda i: (i, 0)),
            vmem(1024, 768),
            pl.BlockSpec((n, 128), lambda i: (i, 0)),
            pl.BlockSpec((n, 128), lambda i: (i, 0)),
        ],
        out_specs=[
            pl.BlockSpec((n, 256), lambda i: (i, 0)),
            vmem(*pairs),
            vmem(*pairs),
            pl.BlockSpec((2, n, 256), lambda i: (0, i, 0)),
        ],
        out_shape=(
            jax.ShapeDtypeStruct((rows, 256), BF),
            jax.ShapeDtypeStruct(pairs, BF),
            jax.ShapeDtypeStruct(pairs, BF),
            jax.ShapeDtypeStruct((2, rows, 256), BF),
        ),
        compiler_params=params(),
        cost_estimate=cost(2 * rows * 1024 * 768, 12 << 20),
        name="qkv",
    )(x, w, cos, sin)


VR = HEAD_DIM + 8


def attend_chunk(at, blocks, qm, kv, kseg, qseg, m_sc, acc):
    size = blocks * KB
    k = kv[pl.ds(at, blocks), 0].reshape(size, 256)
    same = kseg[pl.ds(pl.multiple_of(at * KB, KB), size), 0:1] == qseg[...]
    ones = jnp.ones((8, size), BF)
    scores = []
    for h in range(4):
        s = contract_last(k, qm[h])
        scores.append(jnp.where(same, s, NEG))
    for h in range(4):
        old = m_sc[h]
        new = jnp.maximum(old, jnp.max(scores[h], axis=0, keepdims=True))
        p = jnp.exp(scores[h] - new).astype(BF)
        fade = jnp.exp(old - new)
        m_sc[h] = new
        v = [kv[at + n, 1, HEAD_DIM * h : HEAD_DIM * h + HEAD_DIM, :] for n in range(blocks)]
        v = jnp.concatenate([jnp.concatenate(v, axis=1), ones], axis=0)
        acc[h] = acc[h] * fade + jnp.dot(v, p, preferred_element_type=F32)


def attend_span(short, table, at, i, *refs):
    start = table[at, i]
    if short:

        @pl.loop(0, table[at + 1, i])
        def _(c):
            attend_chunk(start + c, 1, *refs)

        return
    pairs = table[at + 1, i] // 2

    @pl.loop(0, pairs)
    def _(c):
        attend_chunk(start + 2 * c, 2, *refs)

    @pl.when(table[at + 1, i] % 2 == 1)
    def _():
        attend_chunk(start + 2 * pairs, 1, *refs)


def attend_kernel(stage, base, table, q, qseg, kv0, seg0, kv1, seg1, *refs):
    i = pl.program_id(0) + base
    if stage == 0:
        acc_out, m_out, qm, m_sc, acc = refs
    elif stage == 1:
        acc_in, m_in, acc_out, m_out, qm, m_sc, acc = refs
    else:
        acc_in, m_in, out, qm, m_sc, acc = refs
    lane = lax.broadcasted_iota(jnp.int32, (QB, 256), 1)
    for h in range(4):
        qm[h] = jnp.where((lane % 128) // 32 == h, q[...].astype(F32), 0.0).astype(BF)
    if stage == 0:
        m_sc[...] = jnp.full_like(m_sc, NEG)
        acc[...] = jnp.zeros_like(acc)
    else:
        m_sc[...] = m_in[...]
        acc[...] = acc_in[...]
    attend_span(stage == 2, table, 4 * stage, i, qm, kv0, seg0, qseg, m_sc, acc)
    attend_span(stage == 2, table, 4 * stage + 2, i, qm, kv1, seg1, qseg, m_sc, acc)
    if stage < 2:
        acc_out[...] = acc[...]
        m_out[...] = m_sc[...]
    else:
        heads = [acc[h, :HEAD_DIM] / acc[h, HEAD_DIM : HEAD_DIM + 1] for h in range(4)]
        out[...] = jnp.transpose(jnp.concatenate(heads, axis=0)).astype(BF)


def attend(stage, part, parts, table, q, qseg, kv0, seg0, kv1, seg1, *state):
    rows = q.shape[0]
    steps = rows // QB // parts
    base = part * steps
    state_specs = [
        pl.BlockSpec((4, VR, QB), lambda i, *_: (0, 0, i + base)),
        pl.BlockSpec((4, 1, QB), lambda i, *_: (0, 0, i + base)),
    ]
    if stage < 2:
        out_specs = state_specs
        out_shape = (
            jax.ShapeDtypeStruct((4, VR, rows), F32),
            jax.ShapeDtypeStruct((4, 1, rows), F32),
        )
    else:
        out_specs = pl.BlockSpec((QB, 256), lambda i, *_: (i, 0))
        out_shape = jax.ShapeDtypeStruct((rows // parts, 256), BF)
    return pl.pallas_call(
        functools.partial(attend_kernel, stage, base),
        grid_spec=pltpu.PrefetchScalarGridSpec(
            num_scalar_prefetch=1,
            grid=(steps,),
            in_specs=[
                pl.BlockSpec((QB, 256), lambda i, *_: (i + base, 0)),
                pl.BlockSpec((1, QB), lambda i, *_: (0, i + base)),
                vmem(*kv0.shape),
                vmem(*seg0.shape),
                vmem(*kv1.shape),
                vmem(*seg1.shape),
            ]
            + state_specs[: len(state)],
            out_specs=out_specs,
            scratch_shapes=[
                pltpu.VMEM((4, QB, 256), BF),
                pltpu.VMEM((4, 1, QB), F32),
                pltpu.VMEM((4, VR, QB), F32),
            ],
        ),
        out_shape=out_shape,
        compiler_params=params(),
        cost_estimate=cost((20 << 30, 10 << 30, 5 << 30)[stage], 8 << 20, 12 << 20),
        name=("attend_own", "attend_near", "attend_far")[stage],
    )(table, q, qseg, kv0, seg0, kv1, seg1, *state)


def contract_last(a, b):
    return lax.dot_general(a, b, (((1,), (1,)), ((), ())), preferred_element_type=F32)


def mlp_kernel(base, table, m0, m1, m2, m3, h, gain, last, before, weights, keep, send, picked, w, sem):
    count = weights.shape[0]

    @pl.when(pl.program_id(0) == 0)
    def _():
        @pl.loop(0, count)
        def _(k):
            pltpu.make_async_copy(weights.at[table[4 + k]], w.at[k], sem).start()

        pltpu.make_async_copy(weights, w, sem).wait()

    def rows(at, size, lo, width):
        return w[pl.ds(at, size), :, pl.ds(lo, width)].reshape(8 * size, width)

    n = h.shape[0]
    wide = h[...].astype(F32)
    total = None
    for j, m in enumerate((m0, m1, m2, m3)):
        lo = pl.multiple_of(3 * FFP + 256 * table[j], 128)
        piece = contract_last(m[...], rows(0, count, lo, 256))
        total = piece if total is None else total + piece
    first = (wide + total).astype(BF)
    wide = first.astype(F32)
    normed = layer_norm(wide, gain[...]).astype(BF)
    a = jnp.dot(normed, rows(0, count, 0, FFP), preferred_element_type=F32)
    b = jnp.dot(normed, rows(0, count, FFP, FFP), preferred_element_type=F32)
    inner = (0.5 * a * (1.0 + lax.erf(a * (0.5**0.5))) * b).astype(BF)
    mine = jnp.zeros((n, 256), F32)
    for t in range(4):
        mine = jnp.where(table[0] == t, wide[:, 256 * t : 256 * t + 256], mine)

    def down(j):
        return contract_last(inner, rows(table[j] * (count // 4), count // 4, 2 * FFP, FFP))

    kept = jnp.concatenate([down(0) + mine, down(1)], axis=1)
    sent = jnp.concatenate([down(2), down(3)], axis=1).astype(BF)
    keep[...] = kept
    send[...] = sent
    slot = lax.broadcasted_iota(jnp.int32, (last.shape[0], n), 1) + (pl.program_id(0) + base) * n
    ends_here = jnp.where(last[...] == slot, 1.0, 0.0).astype(BF)
    coarse = kept.astype(BF)
    fine = (kept - coarse.astype(F32)).astype(BF)

    def pick(x):
        return jnp.dot(ends_here, x, preferred_element_type=F32)

    @pl.when(pl.program_id(0) == 0)
    def _():
        picked[...] = before[...]

    picked[0] += pick(coarse) + pick(fine)
    picked[1] += pick(sent)


def mlp(table, mixed, h, base, gain, last, before, weights):
    n = 256
    rows = mixed[0].shape[0]
    count = weights.shape[0]

    def block(width):
        return pl.BlockSpec((n, width), lambda i, *_: (i, 0))

    return pl.pallas_call(
        functools.partial(mlp_kernel, base),
        grid_spec=pltpu.PrefetchScalarGridSpec(
            num_scalar_prefetch=1,
            grid=(rows // n,),
            in_specs=[block(256)] * 4
            + [pl.BlockSpec((n, 1024), lambda i, *_: (i + base, 0))]
            + [vmem(1, 1024), vmem(*last.shape), vmem(*before.shape)]
            + [pl.BlockSpec(memory_space=pl.ANY)],
            out_specs=[block(512), block(512), vmem(*before.shape)],
            scratch_shapes=[pltpu.VMEM((count, 8, REST), BF), pltpu.SemaphoreType.DMA(())],
        ),
        out_shape=(
            jax.ShapeDtypeStruct((rows, 512), F32),
            jax.ShapeDtypeStruct((rows, 512), BF),
            jax.ShapeDtypeStruct(before.shape, F32),
        ),
        compiler_params=params(),
        cost_estimate=cost(rows * 1024 * (1024 + 3 * FFP) * 2, 12 << 20, rows * FFP),
        name="mlp",
    )(table, *mixed, h, gain.reshape(1, 1024), last, before, weights)


def gather_tp(x, after=None):
    far = swap(x, 2)
    near = swap(x, 1)
    if after is not None:
        far, _ = lax.optimization_barrier((far, after))
    return x, far, near, swap(far, 1)


def reduce_tp(keep, send):
    got = swap(send, 1).astype(F32)
    other = swap((keep[:, 256:] + got[:, 256:]).astype(BF), 2).astype(F32)
    return (keep[:, :256] + got[:, :256] + other).astype(BF)


def swap(x, bit):
    return lax.ppermute(x, "tp", [(i, i ^ bit) for i in range(4)])


def shift(x, by):
    count = lax.axis_size("req")
    return lax.ppermute(x, "req", [(i, i + by) for i in range(count) if 0 <= i + by < count])


def exchange(x, axes):
    return lax.all_to_all(x, axes, split_axis=0, concat_axis=0, tiled=True)


def body(
    hidden_in,
    lengths,
    tenant,
    shard_map,
    wq,
    wk,
    wv,
    wo,
    wi_in,
    wi_gate,
    wo2,
    head,
    attn_gain,
    mlp_gain,
    final_gain,
):
    req_count = lax.axis_size("req")
    tp_count = lax.axis_size("tp")
    count = req_count * tp_count
    req_index = lax.axis_index("req")
    tp_index = lax.axis_index("tp")
    slots, width = hidden_in.shape
    requests = lengths.shape[0]

    tp_order = jnp.array([0, 2, 1, 3], jnp.int32)
    place_of = tp_order[jnp.arange(4, dtype=jnp.int32) ^ tp_index]
    qkv_block, rest_block = prep(req_count, place_of, wq, wk, wv, wo, wi_in, wi_gate, wo2)
    place = jnp.arange(count, dtype=jnp.int32)
    source = jnp.sum(
        jnp.where(shard_map[None, :] == place[:, None], place[None, :], 0), axis=1
    )
    qkv_all = exchange(qkv_block.reshape(count, 8, 768), BOTH)
    qkv_w = qkv_all[source].reshape(width, 768)
    ends = jnp.cumsum(lengths)
    base = req_index * slots
    index = base - slots + jnp.arange(3 * slots, dtype=jnp.int32)
    segment = jnp.sum((ends[None, :] <= index[:, None]).astype(jnp.int32), axis=1)
    segment = jnp.where((index >= 0) & (index < slots * req_count), segment, -1)
    own = base + jnp.arange(slots, dtype=jnp.int32)
    start_of = jnp.max(jnp.where(ends[None, :] <= own[:, None], ends[None, :], 0), axis=1)
    position = (own - start_of).astype(F32)
    half = HEAD_DIM // 2
    lane = jnp.arange(128, dtype=jnp.int32) % half
    freq = THETA ** (-(2.0 * lane.astype(F32)) / HEAD_DIM)
    angle = position[:, None] * freq[None, :]
    cos = jnp.cos(angle)
    sin = jnp.sin(angle)
    begin = base + jnp.arange(slots // QB, dtype=jnp.int32) * QB
    close = begin + QB - 1
    low = jnp.max(jnp.where(ends[None, :] <= begin[:, None], ends[None, :], 0), axis=1) - base
    high = jnp.min(jnp.where(ends[None, :] > close[:, None], ends[None, :], 1 << 30), axis=1) - base

    half = slots // KB // 2
    own_0 = jnp.maximum(low, 0) // KB
    own_1 = (jnp.minimum(high, slots) + KB - 1) // KB
    left_0 = (jnp.minimum(low, 0) + slots) // KB
    right_1 = (jnp.maximum(high - slots, 0) + KB - 1) // KB
    spans = (
        (own_0, jnp.minimum(own_1, half)),
        (jnp.maximum(own_0 - half, 0), own_1 - half),
        (jnp.maximum(left_0 - half, 0), half),
        (jnp.zeros_like(right_1), jnp.minimum(right_1, half)),
        (left_0, half),
        (jnp.zeros_like(right_1), right_1 - half),
    )
    table = jnp.stack(
        [row for first, end in spans for row in (first, jnp.maximum(end - first, 0))]
    )
    segs = segment.reshape(6, slots // 2, 1)
    qseg = segment[slots : 2 * slots].reshape(1, slots)

    normed = norm(hidden_in, attn_gain)
    rest_block, normed = lax.optimization_barrier((rest_block, normed))
    rest_rows = jnp.concatenate(
        [rest_block[0], swap(rest_block[1], 2), swap(rest_block[2], 1), swap(rest_block[3], 3)], axis=0
    )
    rest = lax.all_gather(rest_rows, "req", axis=0, tiled=True).reshape(count, 8, REST)
    rest_source = source // tp_count * tp_count + place_of[source % tp_count]
    query, kv_low, kv_high, cache = qkv_project(normed, qkv_w, cos, sin)
    left_near = shift(kv_high, 1)
    right_near = shift(kv_low, -1)
    left_far = shift(kv_low, 1)
    right_far = shift(kv_high, -1)
    parts = 2
    state = attend(0, 0, 1, table, query, qseg, kv_low, segs[2], kv_high, segs[3])
    state = attend(1, 0, 1, table, query, qseg, left_near, segs[1], right_near, segs[4], *state)
    mixed = [
        attend(2, part, parts, table, query, qseg, left_far, segs[0], right_far, segs[5], *state)
        for part in range(parts)
    ]

    last_slot = (ends - 1 - base).reshape(requests, 1)
    order = jnp.concatenate([tp_index ^ tp_order, rest_source])
    picked = jnp.zeros((2, requests, 512), F32)
    bulk = []
    for part in range(parts):
        keep, send, picked = mlp(
            order,
            gather_tp(mixed[part], bulk[-1] if bulk else None),
            hidden_in,
            part * (slots // parts // 256),
            mlp_gain,
            last_slot,
            picked,
            rest,
        )
        bulk.append((keep, send))

    each = requests // req_count
    last_mine = reduce_tp(picked[0], picked[1].astype(BF))
    taken = exchange(last_mine.reshape(req_count, each, 256), "req").astype(F32).sum(axis=0)
    spread = exchange(jnp.broadcast_to(taken.astype(BF)[None], (count, each, 256)), BOTH)
    hidden_out = jnp.concatenate([reduce_tp(*pair) for pair in bulk], axis=0)
    last = (
        spread.reshape(req_count, tp_count, each, 256)
        .transpose(0, 2, 1, 3)
        .reshape(requests, width)
        .astype(F32)
    )
    last_rms = jnp.sqrt(jnp.mean(last * last, axis=-1))
    choose = (tenant[:, None] == jnp.arange(final_gain.shape[0], dtype=jnp.int32)[None, :]).astype(
        F32
    )
    gain_rows = jnp.dot(
        choose, final_gain, precision=lax.Precision.HIGHEST, preferred_element_type=F32
    )
    final = layer_norm(last, gain_rows).astype(BF)
    logits = contract_last(final, head.astype(BF))
    top = jnp.max(logits, axis=-1)
    tops = exchange(jnp.broadcast_to(top[None], (count, requests)), BOTH)
    top_logit = jnp.max(tops, axis=0)
    return (hidden_out, cache, last_rms, top_logit)


def solution(mesh):
    rows = P(BOTH, None)
    placed = (P("req", None), P(), P(), P()) + (rows,) * 8 + (P(), P(), P())
    return jax.shard_map(
        body,
        mesh=mesh,
        in_specs=placed,
        out_specs=(P("req", "tp"), P(None, "req", "tp"), P(), P()),
        check_vma=False,
    )
```

```python
import functools

import jax
import jax.numpy as jnp
from jax import lax
from jax.experimental import pallas as pl
from jax.experimental.pallas import tpu as pltpu
from jax.sharding import PartitionSpec as P

HEADS = 16
HEAD_DIM = 64
THETA = 160000.0
EPS = 1e-05
BF = jnp.bfloat16
F32 = jnp.float32
BOTH = ("req", "tp")
NEG = -1e30
FFP = 768
REST = 3 * FFP + 1024
QB = 256
KB = 256


def vmem(*shape):
    return pl.BlockSpec(shape, lambda *_: (0,) * len(shape))


def params():
    return pltpu.CompilerParams(vmem_limit_bytes=60 * 1024 * 1024)


def cost(flops, moved, transcendentals=0):
    return pl.CostEstimate(flops=flops, bytes_accessed=moved, transcendentals=transcendentals)


def prep_kernel(order, wq, wk, wv, wo, wi, wg, w2, qkv, rest):
    row = lax.broadcasted_iota(jnp.int32, (256, 256), 0)
    col = lax.broadcasted_iota(jnp.int32, (256, 256), 1)
    source = (col % 128) // 32 * 64 + col // 128 * 32 + col % 32
    turn = jnp.where(row == source, 1.0, 0.0).astype(BF)
    trow = lax.broadcasted_iota(jnp.int32, (64, 128), 0)
    tcol = lax.broadcasted_iota(jnp.int32, (64, 128), 1)
    for t in range(4):
        at = slice(256 * t, 256 * t + 256)
        q, k = (
            jnp.dot(w[:, at].astype(BF), turn, preferred_element_type=F32).astype(BF)
            for w in (wq, wk)
        )
        mine = jnp.concatenate([q, k, wv[:, at].astype(BF)], axis=1)
        for r in range(qkv.shape[0]):
            qkv[r, t] = mine
        pick = jnp.where((trow == tcol + 16 * t) & (tcol < 16), 1.0, 0.0).astype(BF)
        to = order[t]
        for n, w in enumerate((wi, wg, w2)):
            rest[to, :, FFP * n : FFP * n + 640] = w[:, 640 * t : 640 * t + 640].astype(BF)
            rest[to, :, FFP * n + 640 : FFP * n + 768] = jnp.dot(
                w[:, 2560:2624].astype(BF), pick, preferred_element_type=F32
            ).astype(BF)
        rest[to, :, 3 * FFP :] = wo[...].astype(BF)


def prep(req_count, order, *weights):
    return pl.pallas_call(
        prep_kernel,
        in_specs=[pl.BlockSpec(memory_space=pltpu.SMEM)] + [vmem(*w.shape) for w in weights],
        out_shape=(
            jax.ShapeDtypeStruct((req_count, 4, 8, 768), BF),
            jax.ShapeDtypeStruct((4, 8, REST), BF),
        ),
        compiler_params=params(),
        name="prep",
    )(order, *weights)


def layer_norm(values, gain):
    center = jnp.mean(values, axis=-1, keepdims=True)
    spread = jnp.mean(values * values, axis=-1, keepdims=True) - center * center
    return (values - center) * lax.rsqrt(spread + EPS) * gain


def norm_kernel(h, gain, out):
    out[...] = layer_norm(h[...].astype(F32), gain[...]).astype(BF)


def norm(h, gain):
    rows = h.shape[0]
    return pl.pallas_call(
        norm_kernel,
        grid=(rows // 512,),
        in_specs=[pl.BlockSpec((512, 1024), lambda i: (i, 0)), vmem(1, 1024)],
        out_specs=pl.BlockSpec((512, 1024), lambda i: (i, 0)),
        out_shape=jax.ShapeDtypeStruct((rows, 1024), BF),
        compiler_params=params(),
        cost_estimate=cost(1 << 24, 1 << 23),
        name="norm",
    )(h, gain.reshape(1, 1024))


def qkv_kernel(x, w, cos, sin, q, kv, cache):
    row = lax.broadcasted_iota(jnp.int32, (256, 256), 0)
    col = lax.broadcasted_iota(jnp.int32, (256, 256), 1)
    source = (col % 128) // 32 * 64 + col // 128 * 32 + col % 32
    back = jnp.where(source == row, 1.0, 0.0).astype(BF)
    y = jnp.dot(x[...], w[...], preferred_element_type=F32)
    c = cos[...]
    s = sin[...]

    def turned(a, b):
        return jnp.concatenate([a * c - b * s, b * c + a * s], axis=1)

    q[...] = (turned(y[:, :128], y[:, 128:256]).astype(BF).astype(F32) * 0.125).astype(BF)
    k = turned(y[:, 256:384], y[:, 384:512]).astype(BF)
    v = y[:, 512:].astype(BF)
    for n in range(x.shape[0] // KB):
        kv[n, 0] = k[KB * n : KB * n + KB]
        kv[n, 1] = jnp.transpose(v[KB * n : KB * n + KB])
    cache[0] = lax.dot_general(
        k, back, (((1,), (1,)), ((), ())), preferred_element_type=F32
    ).astype(BF)
    cache[1] = v


def qkv_project(x, w, cos, sin):
    rows = x.shape[0]
    n = 512
    return pl.pallas_call(
        qkv_kernel,
        grid=(rows // n,),
        in_specs=[
            pl.BlockSpec((n, 1024), lambda i: (i, 0)),
            vmem(1024, 768),
            pl.BlockSpec((n, 128), lambda i: (i, 0)),
            pl.BlockSpec((n, 128), lambda i: (i, 0)),
        ],
        out_specs=[
            pl.BlockSpec((n, 256), lambda i: (i, 0)),
            pl.BlockSpec((n // KB, 2, KB, 256), lambda i: (i, 0, 0, 0)),
            pl.BlockSpec((2, n, 256), lambda i: (0, i, 0)),
        ],
        out_shape=(
            jax.ShapeDtypeStruct((rows, 256), BF),
            jax.ShapeDtypeStruct((rows // KB, 2, KB, 256), BF),
            jax.ShapeDtypeStruct((2, rows, 256), BF),
        ),
        compiler_params=params(),
        cost_estimate=cost(2 * rows * 1024 * 768, 12 << 20),
        name="qkv",
    )(x, w, cos, sin)


VR = HEAD_DIM + 8


def attend_chunk(at, blocks, qm, kv, kseg, qseg, m_sc, acc):
    size = blocks * KB
    k = kv[pl.ds(at, blocks), 0].reshape(size, 256)
    same = kseg[pl.ds(pl.multiple_of(at * KB, KB), size), 0:1] == qseg[...]
    ones = jnp.ones((8, size), BF)
    scores = []
    for h in range(4):
        s = contract_last(k, qm[h])
        scores.append(jnp.where(same, s, NEG))
    for h in range(4):
        old = m_sc[h]
        new = jnp.maximum(old, jnp.max(scores[h], axis=0, keepdims=True))
        p = jnp.exp(scores[h] - new).astype(BF)
        fade = jnp.exp(old - new)
        m_sc[h] = new
        v = [kv[at + n, 1, HEAD_DIM * h : HEAD_DIM * h + HEAD_DIM, :] for n in range(blocks)]
        v = jnp.concatenate([jnp.concatenate(v, axis=1), ones], axis=0)
        acc[h] = acc[h] * fade + jnp.dot(v, p, preferred_element_type=F32)


def attend_span(table, at, i, *refs):
    start = table[at, i]
    pairs = table[at + 1, i] // 2

    @pl.loop(0, pairs)
    def _(c):
        attend_chunk(start + 2 * c, 2, *refs)

    @pl.when(table[at + 1, i] % 2 == 1)
    def _():
        attend_chunk(start + 2 * pairs, 1, *refs)


def spread_heads(q, qm):
    lane = lax.broadcasted_iota(jnp.int32, (QB, 256), 1)
    for h in range(4):
        qm[h] = jnp.where((lane % 128) // 32 == h, q[...].astype(F32), 0.0).astype(BF)


def own_kernel(table, q, qseg, kv, kseg, acc_out, m_out, qm, m_sc, acc):
    i = pl.program_id(0)
    spread_heads(q, qm)
    m_sc[...] = jnp.full_like(m_sc, NEG)
    acc[...] = jnp.zeros_like(acc)
    attend_span(table, 0, i, qm, kv, kseg, qseg, m_sc, acc)
    acc_out[...] = acc[...]
    m_out[...] = m_sc[...]


def halo_kernel(base, table, q, qseg, lkv, lseg, rkv, rseg, acc_in, m_in, out, qm, m_sc, acc):
    i = pl.program_id(0) + base
    spread_heads(q, qm)
    m_sc[...] = m_in[...]
    acc[...] = acc_in[...]
    attend_span(table, 2, i, qm, lkv, lseg, qseg, m_sc, acc)
    attend_span(table, 4, i, qm, rkv, rseg, qseg, m_sc, acc)
    heads = [acc[h, :HEAD_DIM] / acc[h, HEAD_DIM : HEAD_DIM + 1] for h in range(4)]
    out[...] = jnp.transpose(jnp.concatenate(heads, axis=0)).astype(BF)


def attend(part, parts, table, q, qseg, sources, state):
    rows = q.shape[0]
    steps = rows // QB // parts
    base = part * steps
    state_specs = [
        pl.BlockSpec((4, VR, QB), lambda i, *_: (0, 0, i + base)),
        pl.BlockSpec((4, 1, QB), lambda i, *_: (0, 0, i + base)),
    ]
    if state:
        kernel = functools.partial(halo_kernel, base)
        out_specs = pl.BlockSpec((QB, 256), lambda i, *_: (i, 0))
        out_shape = jax.ShapeDtypeStruct((rows // parts, 256), BF)
    else:
        kernel = own_kernel
        out_specs = state_specs
        out_shape = (
            jax.ShapeDtypeStruct((4, VR, rows), F32),
            jax.ShapeDtypeStruct((4, 1, rows), F32),
        )
    return pl.pallas_call(
        kernel,
        grid_spec=pltpu.PrefetchScalarGridSpec(
            num_scalar_prefetch=1,
            grid=(steps,),
            in_specs=[
                pl.BlockSpec((QB, 256), lambda i, *_: (i + base, 0)),
                pl.BlockSpec((1, QB), lambda i, *_: (0, i + base)),
            ]
            + [vmem(*x.shape) for x in sources]
            + state_specs[: len(state)],
            out_specs=out_specs,
            scratch_shapes=[
                pltpu.VMEM((4, QB, 256), BF),
                pltpu.VMEM((4, 1, QB), F32),
                pltpu.VMEM((4, VR, QB), F32),
            ],
        ),
        out_shape=out_shape,
        compiler_params=params(),
        cost_estimate=cost(12 << 30, 8 << 20, 12 << 20),
        name="attend_halo" if state else "attend_own",
    )(table, q, qseg, *sources, *state)


def contract_last(a, b):
    return lax.dot_general(a, b, (((1,), (1,)), ((), ())), preferred_element_type=F32)


def mlp_kernel(base, table, m0, m1, m2, m3, h, gain, last, before, *refs):
    *pieces, keep, send, picked, w, sem = refs
    count = w.shape[0]

    @pl.when(pl.program_id(0) == 0)
    def _():
        done = 4
        for piece in pieces:

            @pl.loop(0, piece.shape[0])
            def _(n, piece=piece, done=done):
                pltpu.make_async_copy(piece.at[n], w.at[table[done + n]], sem).start()

            done += piece.shape[0]
        pltpu.make_async_copy(w, w, sem).wait()

    def rows(at, size, lo, width):
        return w[pl.ds(at, size), :, pl.ds(lo, width)].reshape(8 * size, width)

    n = h.shape[0]
    wide = h[...].astype(F32)
    total = None
    for j, m in enumerate((m0, m1, m2, m3)):
        lo = pl.multiple_of(3 * FFP + 256 * table[j], 128)
        piece = contract_last(m[...], rows(0, count, lo, 256))
        total = piece if total is None else total + piece
    first = (wide + total).astype(BF)
    wide = first.astype(F32)
    normed = layer_norm(wide, gain[...]).astype(BF)
    a = jnp.dot(normed, rows(0, count, 0, FFP), preferred_element_type=F32)
    b = jnp.dot(normed, rows(0, count, FFP, FFP), preferred_element_type=F32)
    inner = (0.5 * a * (1.0 + lax.erf(a * (0.5**0.5))) * b).astype(BF)
    mine = jnp.zeros((n, 256), F32)
    for t in range(4):
        mine = jnp.where(table[0] == t, wide[:, 256 * t : 256 * t + 256], mine)

    def down(j):
        return contract_last(inner, rows(table[j] * (count // 4), count // 4, 2 * FFP, FFP))

    kept = jnp.concatenate([down(0) + mine, down(1)], axis=1)
    sent = jnp.concatenate([down(2), down(3)], axis=1).astype(BF)
    keep[...] = kept
    send[...] = sent
    slot = lax.broadcasted_iota(jnp.int32, (last.shape[0], n), 1) + (pl.program_id(0) + base) * n
    ends_here = jnp.where(last[...] == slot, 1.0, 0.0).astype(BF)
    coarse = kept.astype(BF)
    fine = (kept - coarse.astype(F32)).astype(BF)

    def pick(x):
        return jnp.dot(ends_here, x, preferred_element_type=F32)

    @pl.when(pl.program_id(0) == 0)
    def _():
        picked[...] = before[...]

    picked[0] += pick(coarse) + pick(fine)
    picked[1] += pick(sent)


def mlp(table, mixed, h, base, gain, last, before, pieces):
    n = 256
    rows = mixed[0].shape[0]
    count = sum(piece.shape[0] for piece in pieces)

    def block(width):
        return pl.BlockSpec((n, width), lambda i, *_: (i, 0))

    return pl.pallas_call(
        functools.partial(mlp_kernel, base),
        grid_spec=pltpu.PrefetchScalarGridSpec(
            num_scalar_prefetch=1,
            grid=(rows // n,),
            in_specs=[block(256)] * 4
            + [pl.BlockSpec((n, 1024), lambda i, *_: (i + base, 0))]
            + [vmem(1, 1024), vmem(*last.shape), vmem(*before.shape)]
            + [pl.BlockSpec(memory_space=pl.ANY)] * len(pieces),
            out_specs=[block(512), block(512), vmem(*before.shape)],
            scratch_shapes=[pltpu.VMEM((count, 8, REST), BF), pltpu.SemaphoreType.DMA(())],
        ),
        out_shape=(
            jax.ShapeDtypeStruct((rows, 512), F32),
            jax.ShapeDtypeStruct((rows, 512), BF),
            jax.ShapeDtypeStruct(before.shape, F32),
        ),
        compiler_params=params(),
        cost_estimate=cost(rows * 1024 * (1024 + 3 * FFP) * 2, 12 << 20, rows * FFP),
        name="mlp",
    )(table, *mixed, h, gain.reshape(1, 1024), last, before, *pieces)


def swap(x, bit):
    return lax.ppermute(x, "tp", [(i, i ^ bit) for i in range(4)])


def gather_tp(x, after=None):
    far = swap(x, 2)
    near = swap(x, 1)
    if after is not None:
        far, _ = lax.optimization_barrier((far, after))
    return x, far, near, swap(far, 1)


def reduce_core(keep, send):
    got = swap(send, 1).astype(F32)
    return keep[:, :256] + got[:, :256], (keep[:, 256:] + got[:, 256:]).astype(BF)


def reduce_far(mine, send):
    return (mine + swap(send, 2).astype(F32)).astype(BF)


def from_offset(x, dx, dy, dz=0):
    pairs = []
    for i in range(32):
        far = (i // 16 + dz) % 2 * 16 + (i // 4 + dx) % 4 * 4 + (i + dy) % 4
        pairs.append((far, i))
    return lax.ppermute(x, "req", pairs)


def sum_req(x, moves):
    return sum([from_offset(x, *move) for move in moves], x)


def shift(x, by):
    count = lax.axis_size("req")
    return lax.ppermute(x, "req", [(i, i + by) for i in range(count) if 0 <= i + by < count])


def exchange(x, axes):
    return lax.all_to_all(x, axes, split_axis=0, concat_axis=0, tiled=True)


def body(
    hidden_in,
    lengths,
    tenant,
    shard_map,
    wq,
    wk,
    wv,
    wo,
    wi_in,
    wi_gate,
    wo2,
    head,
    attn_gain,
    mlp_gain,
    final_gain,
):
    req_count = lax.axis_size("req")
    tp_count = lax.axis_size("tp")
    count = req_count * tp_count
    req_index = lax.axis_index("req")
    tp_index = lax.axis_index("tp")
    slots, width = hidden_in.shape
    requests = lengths.shape[0]

    tp_order = jnp.array([0, 2, 1, 3], jnp.int32)
    place_of = tp_order[jnp.arange(4, dtype=jnp.int32) ^ tp_index]
    qkv_block, rest_block = prep(req_count, place_of, wq, wk, wv, wo, wi_in, wi_gate, wo2)
    place = jnp.arange(count, dtype=jnp.int32)
    source = jnp.sum(
        jnp.where(shard_map[None, :] == place[:, None], place[None, :], 0), axis=1
    )
    ends = jnp.cumsum(lengths)
    base = req_index * slots
    index = base - slots + jnp.arange(3 * slots, dtype=jnp.int32)
    segment = jnp.sum((ends[None, :] <= index[:, None]).astype(jnp.int32), axis=1)
    segment = jnp.where((index >= 0) & (index < slots * req_count), segment, -1)
    own = base + jnp.arange(slots, dtype=jnp.int32)
    start_of = jnp.max(jnp.where(ends[None, :] <= own[:, None], ends[None, :], 0), axis=1)
    position = (own - start_of).astype(F32)
    half = HEAD_DIM // 2
    lane = jnp.arange(128, dtype=jnp.int32) % half
    freq = THETA ** (-(2.0 * lane.astype(F32)) / HEAD_DIM)
    angle = position[:, None] * freq[None, :]
    cos = jnp.cos(angle)
    sin = jnp.sin(angle)
    begin = base + jnp.arange(slots // QB, dtype=jnp.int32) * QB
    close = begin + QB - 1
    low = jnp.max(jnp.where(ends[None, :] <= begin[:, None], ends[None, :], 0), axis=1) - base
    high = jnp.min(jnp.where(ends[None, :] > close[:, None], ends[None, :], 1 << 30), axis=1) - base

    blocks = slots // KB
    own_0 = jnp.maximum(low, 0) // KB
    own_1 = (jnp.minimum(high, slots) + KB - 1) // KB
    left_0 = (jnp.minimum(low, 0) + slots) // KB
    right_1 = (jnp.maximum(high - slots, 0) + KB - 1) // KB
    table = jnp.stack(
        [own_0, own_1 - own_0, left_0, blocks - left_0, jnp.zeros_like(right_1), right_1]
    )
    segs = segment.reshape(3, slots, 1)
    qseg = segment[slots : 2 * slots].reshape(1, slots)

    later, qkv_block = lax.optimization_barrier((hidden_in, qkv_block))
    normed = norm(later, attn_gain)
    rest_block, normed = lax.optimization_barrier((rest_block, normed))
    rest_rows = jnp.concatenate(
        [rest_block[0], swap(rest_block[1], 2), swap(rest_block[2], 1), swap(rest_block[3], 3)], axis=0
    )
    level = jnp.concatenate([rest_rows, from_offset(rest_rows, 0, 0, 1)], axis=0)
    level = jnp.concatenate([level] + [from_offset(level, 0, d) for d in (1, 3, 2)], axis=0)
    ahead = from_offset(level, 1, 0)
    behind = from_offset(level, 3, 0)
    far = jnp.arange(count, dtype=jnp.int32)
    slot_x, slot_y = (jnp.array([0, 1, 3, 2], jnp.int32)[n] for n in (far // 32, far // 8 % 4))
    from_req = (
        (req_index // 16 + far // 4) % 2 * 16
        + (req_index // 4 + slot_x) % 4 * 4
        + (req_index + slot_y) % 4
    )
    rest_target = shard_map[from_req * tp_count + (tp_index ^ tp_order[far % 4])]
    qkv_all = exchange(qkv_block.reshape(count, 8, 768), BOTH)
    qkv_w = qkv_all[source].reshape(width, 768)
    query, kv, cache = qkv_project(normed, qkv_w, cos, sin)
    left = shift(kv, 1)
    right = shift(kv, -1)
    parts = 2
    state = attend(0, 1, table, query, qseg, (kv, segs[1]), ())
    ahead, behind, state = lax.optimization_barrier((ahead, behind, state))
    rest = [
        piece.reshape(-1, 8, REST)
        for piece in (
            level,
            ahead,
            behind,
            from_offset(ahead[:128], 1, 0),
            from_offset(behind[128:], 3, 0),
        )
    ]
    mixed = [
        attend(part, parts, table, query, qseg, (left, segs[0], right, segs[2]), state)
        for part in range(parts)
    ]

    last_slot = (ends - 1 - base).reshape(requests, 1)
    order = jnp.concatenate([tp_index ^ tp_order, rest_target])
    picked = jnp.zeros((2, requests, 512), F32)
    bulk = []
    after = mixed[1]
    for part in range(parts):
        keep, send, picked = mlp(
            order,
            gather_tp(mixed[part], after),
            hidden_in,
            part * (slots // parts // 256),
            mlp_gain,
            last_slot,
            picked,
            rest,
        )
        after = (keep, send)
        bulk.append((keep, send))

    pieces = gather_tp(reduce_far(*reduce_core(picked[0], picked[1].astype(BF))))
    wide = jnp.stack(pieces)[place_of].transpose(1, 0, 2).reshape(requests, width)
    wide = sum_req(wide, ((0, 0, 1),))
    bulk, wide = lax.optimization_barrier((bulk, wide))
    hidden_out = jnp.concatenate([reduce_far(*reduce_core(*pair)) for pair in bulk], axis=0)
    wide = sum_req(wide, tuple((0, d, 0) for d in (1, 3, 2)))
    wide = sum_req(wide, tuple((d, 0, 0) for d in (1, 3, 2)))
    last = wide.astype(F32)
    last_rms = jnp.sqrt(jnp.mean(last * last, axis=-1))
    choose = (tenant[:, None] == jnp.arange(final_gain.shape[0], dtype=jnp.int32)[None, :]).astype(
        F32
    )
    gain_rows = jnp.dot(
        choose, final_gain, precision=lax.Precision.HIGHEST, preferred_element_type=F32
    )
    final = layer_norm(last, gain_rows).astype(BF)
    logits = contract_last(final, head.astype(BF))
    top = jnp.max(logits, axis=-1)
    tops = exchange(jnp.broadcast_to(top[None], (count, requests)), BOTH)
    top_logit = jnp.max(tops, axis=0)
    return (hidden_out, cache, last_rms, top_logit)


def solution(mesh):
    rows = P(BOTH, None)
    placed = (P("req", None), P(), P(), P()) + (rows,) * 8 + (P(), P(), P())
    return jax.shard_map(
        body,
        mesh=mesh,
        in_specs=placed,
        out_specs=(P("req", "tp"), P(None, "req", "tp"), P(), P()),
        check_vma=False,
    )
```

```python
import functools

import jax
import jax.numpy as jnp
from jax import lax
from jax.experimental import pallas as pl
from jax.experimental.pallas import tpu as pltpu
from jax.sharding import PartitionSpec as P

HEADS = 16
HEAD_DIM = 64
THETA = 160000.0
EPS = 1e-05
BF = jnp.bfloat16
F32 = jnp.float32
BOTH = ("req", "tp")
NEG = -1e30
FFP = 768
REST = 3 * FFP + 1024
QB = 256
KB = 256


def vmem(*shape):
    return pl.BlockSpec(shape, lambda *_: (0,) * len(shape))


def params():
    return pltpu.CompilerParams(vmem_limit_bytes=60 * 1024 * 1024)


def cost(flops, moved, transcendentals=0):
    return pl.CostEstimate(flops=flops, bytes_accessed=moved, transcendentals=transcendentals)


def prep_kernel(order, wq, wk, wv, wo, wi, wg, w2, qkv, rest):
    row = lax.broadcasted_iota(jnp.int32, (256, 256), 0)
    col = lax.broadcasted_iota(jnp.int32, (256, 256), 1)
    source = (col % 128) // 32 * 64 + col // 128 * 32 + col % 32
    turn = jnp.where(row == source, 1.0, 0.0).astype(BF)
    trow = lax.broadcasted_iota(jnp.int32, (64, 128), 0)
    tcol = lax.broadcasted_iota(jnp.int32, (64, 128), 1)
    for t in range(4):
        at = slice(256 * t, 256 * t + 256)
        q, k = (
            jnp.dot(w[:, at].astype(BF), turn, preferred_element_type=F32).astype(BF)
            for w in (wq, wk)
        )
        mine = jnp.concatenate([q, k, wv[:, at].astype(BF)], axis=1)
        for r in range(qkv.shape[0]):
            qkv[r, t] = mine
        pick = jnp.where((trow == tcol + 16 * t) & (tcol < 16), 1.0, 0.0).astype(BF)
        to = order[t]
        for n, w in enumerate((wi, wg, w2)):
            rest[to, :, FFP * n : FFP * n + 640] = w[:, 640 * t : 640 * t + 640].astype(BF)
            rest[to, :, FFP * n + 640 : FFP * n + 768] = jnp.dot(
                w[:, 2560:2624].astype(BF), pick, preferred_element_type=F32
            ).astype(BF)
        rest[to, :, 3 * FFP :] = wo[...].astype(BF)


def prep(req_count, order, *weights):
    return pl.pallas_call(
        prep_kernel,
        in_specs=[pl.BlockSpec(memory_space=pltpu.SMEM)] + [vmem(*w.shape) for w in weights],
        out_shape=(
            jax.ShapeDtypeStruct((req_count, 4, 8, 768), BF),
            jax.ShapeDtypeStruct((4, 8, REST), BF),
        ),
        compiler_params=params(),
        name="prep",
    )(order, *weights)


def layer_norm(values, gain):
    center = jnp.mean(values, axis=-1, keepdims=True)
    spread = jnp.mean(values * values, axis=-1, keepdims=True) - center * center
    return (values - center) * lax.rsqrt(spread + EPS) * gain


def norm_kernel(h, gain, out):
    out[...] = layer_norm(h[...].astype(F32), gain[...]).astype(BF)


def norm(h, gain):
    rows = h.shape[0]
    return pl.pallas_call(
        norm_kernel,
        grid=(rows // 512,),
        in_specs=[pl.BlockSpec((512, 1024), lambda i: (i, 0)), vmem(1, 1024)],
        out_specs=pl.BlockSpec((512, 1024), lambda i: (i, 0)),
        out_shape=jax.ShapeDtypeStruct((rows, 1024), BF),
        compiler_params=params(),
        cost_estimate=cost(1 << 24, 1 << 23),
        name="norm",
    )(h, gain.reshape(1, 1024))


def qkv_kernel(x, w, cos, sin, q, kv, cache):
    row = lax.broadcasted_iota(jnp.int32, (256, 256), 0)
    col = lax.broadcasted_iota(jnp.int32, (256, 256), 1)
    source = (col % 128) // 32 * 64 + col // 128 * 32 + col % 32
    back = jnp.where(source == row, 1.0, 0.0).astype(BF)
    y = jnp.dot(x[...], w[...], preferred_element_type=F32)
    c = cos[...]
    s = sin[...]

    def turned(a, b):
        return jnp.concatenate([a * c - b * s, b * c + a * s], axis=1)

    q[...] = (turned(y[:, :128], y[:, 128:256]).astype(BF).astype(F32) * 0.125).astype(BF)
    k = turned(y[:, 256:384], y[:, 384:512]).astype(BF)
    v = y[:, 512:].astype(BF)
    for n in range(x.shape[0] // KB):
        kv[n, 0] = k[KB * n : KB * n + KB]
        kv[n, 1] = jnp.transpose(v[KB * n : KB * n + KB])
    cache[0] = lax.dot_general(
        k, back, (((1,), (1,)), ((), ())), preferred_element_type=F32
    ).astype(BF)
    cache[1] = v


def qkv_project(x, w, cos, sin):
    rows = x.shape[0]
    n = 512
    return pl.pallas_call(
        qkv_kernel,
        grid=(rows // n,),
        in_specs=[
            pl.BlockSpec((n, 1024), lambda i: (i, 0)),
            vmem(1024, 768),
            pl.BlockSpec((n, 128), lambda i: (i, 0)),
            pl.BlockSpec((n, 128), lambda i: (i, 0)),
        ],
        out_specs=[
            pl.BlockSpec((n, 256), lambda i: (i, 0)),
            pl.BlockSpec((n // KB, 2, KB, 256), lambda i: (i, 0, 0, 0)),
            pl.BlockSpec((2, n, 256), lambda i: (0, i, 0)),
        ],
        out_shape=(
            jax.ShapeDtypeStruct((rows, 256), BF),
            jax.ShapeDtypeStruct((rows // KB, 2, KB, 256), BF),
            jax.ShapeDtypeStruct((2, rows, 256), BF),
        ),
        compiler_params=params(),
        cost_estimate=cost(2 * rows * 1024 * 768, 12 << 20),
        name="qkv",
    )(x, w, cos, sin)


def halo_kv_kernel(order, x0, x1, w, cos, sin, kv):
    x = jnp.where(pl.program_id(0) < 2, x0[...], x1[...])
    y = jnp.dot(x, w[...], preferred_element_type=F32)
    c = cos[...]
    s = sin[...]
    k = jnp.concatenate(
        [y[:, :128] * c - y[:, 128:256] * s, y[:, 128:256] * c + y[:, :128] * s], axis=1
    ).astype(BF)
    v = y[:, 256:].astype(BF)
    for n in range(x.shape[0] // KB):
        kv[n, 0] = k[KB * n : KB * n + KB]
        kv[n, 1] = jnp.transpose(v[KB * n : KB * n + KB])


def halo_project(order, x0, x1, w, cos, sin):
    rows = 2 * x0.shape[0]
    n = 512
    half = rows // n // 2

    def place(i, order):
        return (i // half ^ order[0]) * half + i % half

    return pl.pallas_call(
        halo_kv_kernel,
        grid_spec=pltpu.PrefetchScalarGridSpec(
            num_scalar_prefetch=1,
            grid=(rows // n,),
            in_specs=[
                pl.BlockSpec((n, 1024), lambda i, o: (jnp.minimum(i, half - 1), 0)),
                pl.BlockSpec((n, 1024), lambda i, o: (jnp.maximum(i - half, 0), 0)),
                vmem(1024, 512),
                pl.BlockSpec((n, 128), lambda i, o: (place(i, o), 0)),
                pl.BlockSpec((n, 128), lambda i, o: (place(i, o), 0)),
            ],
            out_specs=pl.BlockSpec((n // KB, 2, KB, 256), lambda i, o: (place(i, o), 0, 0, 0)),
        ),
        out_shape=jax.ShapeDtypeStruct((rows // KB, 2, KB, 256), BF),
        compiler_params=params(),
        cost_estimate=cost(2 * rows * 1024 * 512, 12 << 20),
        name="halo_kv",
    )(order, x0, x1, w, cos, sin)


VR = HEAD_DIM + 8


def attend_chunk(at, blocks, qm, kv, kseg, qseg, m_sc, acc):
    size = blocks * KB
    k = kv[pl.ds(at, blocks), 0].reshape(size, 256)
    same = kseg[pl.ds(pl.multiple_of(at * KB, KB), size), 0:1] == qseg[...]
    ones = jnp.ones((8, size), BF)
    scores = []
    for h in range(4):
        s = contract_last(k, qm[h])
        scores.append(jnp.where(same, s, NEG))
    for h in range(4):
        old = m_sc[h]
        new = jnp.maximum(old, jnp.max(scores[h], axis=0, keepdims=True))
        p = jnp.exp(scores[h] - new).astype(BF)
        fade = jnp.exp(old - new)
        m_sc[h] = new
        v = [kv[at + n, 1, HEAD_DIM * h : HEAD_DIM * h + HEAD_DIM, :] for n in range(blocks)]
        v = jnp.concatenate([jnp.concatenate(v, axis=1), ones], axis=0)
        acc[h] = acc[h] * fade + jnp.dot(v, p, preferred_element_type=F32)


def attend_span(table, at, i, *refs):
    start = table[at, i]
    pairs = table[at + 1, i] // 2

    @pl.loop(0, pairs)
    def _(c):
        attend_chunk(start + 2 * c, 2, *refs)

    @pl.when(table[at + 1, i] % 2 == 1)
    def _():
        attend_chunk(start + 2 * pairs, 1, *refs)


def spread_heads(q, qm):
    lane = lax.broadcasted_iota(jnp.int32, (QB, 256), 1)
    for h in range(4):
        qm[h] = jnp.where((lane % 128) // 32 == h, q[...].astype(F32), 0.0).astype(BF)


def own_kernel(table, q, qseg, kv, kseg, acc_out, m_out, qm, m_sc, acc):
    i = pl.program_id(0)
    spread_heads(q, qm)
    m_sc[...] = jnp.full_like(m_sc, NEG)
    acc[...] = jnp.zeros_like(acc)
    attend_span(table, 0, i, qm, kv, kseg, qseg, m_sc, acc)
    acc_out[...] = acc[...]
    m_out[...] = m_sc[...]


def halo_kernel(base, table, q, qseg, lkv, lseg, rkv, rseg, acc_in, m_in, out, qm, m_sc, acc):
    i = pl.program_id(0) + base
    spread_heads(q, qm)
    m_sc[...] = m_in[...]
    acc[...] = acc_in[...]
    attend_span(table, 2, i, qm, lkv, lseg, qseg, m_sc, acc)
    attend_span(table, 4, i, qm, rkv, rseg, qseg, m_sc, acc)
    heads = [acc[h, :HEAD_DIM] / acc[h, HEAD_DIM : HEAD_DIM + 1] for h in range(4)]
    out[...] = jnp.transpose(jnp.concatenate(heads, axis=0)).astype(BF)


def attend(part, parts, table, q, qseg, sources, state):
    rows = q.shape[0]
    steps = rows // QB // parts
    base = part * steps
    state_specs = [
        pl.BlockSpec((4, VR, QB), lambda i, *_: (0, 0, i + base)),
        pl.BlockSpec((4, 1, QB), lambda i, *_: (0, 0, i + base)),
    ]
    if state:
        kernel = functools.partial(halo_kernel, base)
        out_specs = pl.BlockSpec((QB, 256), lambda i, *_: (i, 0))
        out_shape = jax.ShapeDtypeStruct((rows // parts, 256), BF)
    else:
        kernel = own_kernel
        out_specs = state_specs
        out_shape = (
            jax.ShapeDtypeStruct((4, VR, rows), F32),
            jax.ShapeDtypeStruct((4, 1, rows), F32),
        )
    return pl.pallas_call(
        kernel,
        grid_spec=pltpu.PrefetchScalarGridSpec(
            num_scalar_prefetch=1,
            grid=(steps,),
            in_specs=[
                pl.BlockSpec((QB, 256), lambda i, *_: (i + base, 0)),
                pl.BlockSpec((1, QB), lambda i, *_: (0, i + base)),
            ]
            + [vmem(*x.shape) for x in sources]
            + state_specs[: len(state)],
            out_specs=out_specs,
            scratch_shapes=[
                pltpu.VMEM((4, QB, 256), BF),
                pltpu.VMEM((4, 1, QB), F32),
                pltpu.VMEM((4, VR, QB), F32),
            ],
        ),
        out_shape=out_shape,
        compiler_params=params(),
        cost_estimate=cost(12 << 30, 8 << 20, 12 << 20),
        name="attend_halo" if state else "attend_own",
    )(table, q, qseg, *sources, *state)


def contract_last(a, b):
    return lax.dot_general(a, b, (((1,), (1,)), ((), ())), preferred_element_type=F32)


def mlp_kernel(base, table, m0, m1, m2, m3, h, gain, last, before, *refs):
    *pieces, keep, send, picked, w, sem = refs
    count = w.shape[0]

    @pl.when(pl.program_id(0) == 0)
    def _():
        done = 4
        for piece in pieces:

            @pl.loop(0, piece.shape[0])
            def _(n, piece=piece, done=done):
                pltpu.make_async_copy(piece.at[n], w.at[table[done + n]], sem).start()

            done += piece.shape[0]
        pltpu.make_async_copy(w, w, sem).wait()

    def rows(at, size, lo, width):
        return w[pl.ds(at, size), :, pl.ds(lo, width)].reshape(8 * size, width)

    n = h.shape[0]
    wide = h[...].astype(F32)
    total = None
    for j, m in enumerate((m0, m1, m2, m3)):
        lo = pl.multiple_of(3 * FFP + 256 * table[j], 128)
        piece = contract_last(m[...], rows(0, count, lo, 256))
        total = piece if total is None else total + piece
    first = (wide + total).astype(BF)
    wide = first.astype(F32)
    normed = layer_norm(wide, gain[...]).astype(BF)
    a = jnp.dot(normed, rows(0, count, 0, FFP), preferred_element_type=F32)
    b = jnp.dot(normed, rows(0, count, FFP, FFP), preferred_element_type=F32)
    inner = (0.5 * a * (1.0 + lax.erf(a * (0.5**0.5))) * b).astype(BF)
    mine = jnp.zeros((n, 256), F32)
    for t in range(4):
        mine = jnp.where(table[0] == t, wide[:, 256 * t : 256 * t + 256], mine)

    def down(j):
        return contract_last(inner, rows(table[j] * (count // 4), count // 4, 2 * FFP, FFP))

    kept = jnp.concatenate([down(0) + mine, down(1)], axis=1)
    sent = jnp.concatenate([down(2), down(3)], axis=1).astype(BF)
    keep[...] = kept
    send[...] = sent
    slot = lax.broadcasted_iota(jnp.int32, (last.shape[0], n), 1) + (pl.program_id(0) + base) * n
    ends_here = jnp.where(last[...] == slot, 1.0, 0.0).astype(BF)
    coarse = kept.astype(BF)
    fine = (kept - coarse.astype(F32)).astype(BF)

    def pick(x):
        return jnp.dot(ends_here, x, preferred_element_type=F32)

    @pl.when(pl.program_id(0) == 0)
    def _():
        picked[...] = before[...]

    picked[0] += pick(coarse) + pick(fine)
    picked[1] += pick(sent)


def mlp(table, mixed, h, base, gain, last, before, pieces):
    n = 256
    rows = mixed[0].shape[0]
    count = sum(piece.shape[0] for piece in pieces)

    def block(width):
        return pl.BlockSpec((n, width), lambda i, *_: (i, 0))

    return pl.pallas_call(
        functools.partial(mlp_kernel, base),
        grid_spec=pltpu.PrefetchScalarGridSpec(
            num_scalar_prefetch=1,
            grid=(rows // n,),
            in_specs=[block(256)] * 4
            + [pl.BlockSpec((n, 1024), lambda i, *_: (i + base, 0))]
            + [vmem(1, 1024), vmem(*last.shape), vmem(*before.shape)]
            + [pl.BlockSpec(memory_space=pl.ANY)] * len(pieces),
            out_specs=[block(512), block(512), vmem(*before.shape)],
            scratch_shapes=[pltpu.VMEM((count, 8, REST), BF), pltpu.SemaphoreType.DMA(())],
        ),
        out_shape=(
            jax.ShapeDtypeStruct((rows, 512), F32),
            jax.ShapeDtypeStruct((rows, 512), BF),
            jax.ShapeDtypeStruct(before.shape, F32),
        ),
        compiler_params=params(),
        cost_estimate=cost(rows * 1024 * (1024 + 3 * FFP) * 2, 12 << 20, rows * FFP),
        name="mlp",
    )(table, *mixed, h, gain.reshape(1, 1024), last, before, *pieces)


def swap(x, bit):
    return lax.ppermute(x, "tp", [(i, i ^ bit) for i in range(4)])


def gather_tp(x, after=None):
    far = swap(x, 2)
    near = swap(x, 1)
    if after is not None:
        far, _ = lax.optimization_barrier((far, after))
    return x, far, near, swap(far, 1)


def reduce_core(keep, send):
    got = swap(send, 1).astype(F32)
    return keep[:, :256] + got[:, :256], (keep[:, 256:] + got[:, 256:]).astype(BF)


def reduce_far(mine, send):
    return (mine + swap(send, 2).astype(F32)).astype(BF)


def shift(x, by):
    count = lax.axis_size("req")
    return lax.ppermute(x, "req", [(i, i + by) for i in range(count) if 0 <= i + by < count])


def exchange(x, axes):
    return lax.all_to_all(x, axes, split_axis=0, concat_axis=0, tiled=True)


def body(
    hidden_in,
    lengths,
    tenant,
    shard_map,
    wq,
    wk,
    wv,
    wo,
    wi_in,
    wi_gate,
    wo2,
    head,
    attn_gain,
    mlp_gain,
    final_gain,
):
    req_count = lax.axis_size("req")
    tp_count = lax.axis_size("tp")
    count = req_count * tp_count
    req_index = lax.axis_index("req")
    tp_index = lax.axis_index("tp")
    slots, width = hidden_in.shape
    requests = lengths.shape[0]

    tp_order = jnp.array([0, 2, 1, 3], jnp.int32)
    place_of = tp_order[jnp.arange(4, dtype=jnp.int32) ^ tp_index]
    qkv_block, rest_block = prep(req_count, place_of, wq, wk, wv, wo, wi_in, wi_gate, wo2)
    place = jnp.arange(count, dtype=jnp.int32)
    source = jnp.sum(
        jnp.where(shard_map[None, :] == place[:, None], place[None, :], 0), axis=1
    )
    ends = jnp.cumsum(lengths)
    base = req_index * slots
    index = base - slots + jnp.arange(3 * slots, dtype=jnp.int32)
    segment = jnp.sum((ends[None, :] <= index[:, None]).astype(jnp.int32), axis=1)
    segment = jnp.where((index >= 0) & (index < slots * req_count), segment, -1)
    start_of = jnp.max(jnp.where(ends[None, :] <= index[:, None], ends[None, :], 0), axis=1)
    position = (index - start_of).astype(F32)
    lane = jnp.arange(128, dtype=jnp.int32) % (HEAD_DIM // 2)
    freq = THETA ** (-(2.0 * lane.astype(F32)) / HEAD_DIM)
    turns = []
    for n in range(3):
        angle = position[n * slots : (n + 1) * slots, None] * freq[None, :]
        turns.append((jnp.cos(angle), jnp.sin(angle)))

    begin = base + jnp.arange(slots // QB, dtype=jnp.int32) * QB
    close = begin + QB - 1
    low = jnp.max(jnp.where(ends[None, :] <= begin[:, None], ends[None, :], 0), axis=1) - base
    high = jnp.min(jnp.where(ends[None, :] > close[:, None], ends[None, :], 1 << 30), axis=1) - base

    blocks = slots // KB
    own_0 = jnp.maximum(low, 0) // KB
    own_1 = (jnp.minimum(high, slots) + KB - 1) // KB
    left_0 = (jnp.minimum(low, 0) + slots) // KB
    right_1 = (jnp.maximum(high - slots, 0) + KB - 1) // KB
    table = jnp.stack(
        [own_0, own_1 - own_0, left_0, blocks - left_0, jnp.zeros_like(right_1), right_1]
    )
    segs = segment.reshape(3, slots, 1)
    qseg = segment[slots : 2 * slots].reshape(1, slots)

    later, qkv_block = lax.optimization_barrier((hidden_in, qkv_block))
    normed = norm(later, attn_gain)
    rest_block, normed = lax.optimization_barrier((rest_block, normed))
    half = slots // 2
    mine = lax.dynamic_slice_in_dim(normed, tp_index % 2 * half, half, 0)
    sides = (shift(mine, 1), shift(mine, -1))
    rest_rows = jnp.concatenate(
        [rest_block[0], swap(rest_block[1], 2), swap(rest_block[2], 1), swap(rest_block[3], 3)], axis=0
    )
    grid = [[[z * 16 + x * 4 + y for x in range(4)] for y in range(4)] for z in range(2)]
    plane = [[grid[z][y][x] for z in range(2) for y in range(4)] for x in range(4)]
    column = [grid[z][y] for z in range(2) for y in range(4)]
    rest = lax.all_gather(rest_rows, "req", axis=0, tiled=True, axis_index_groups=plane)
    qkv_all = exchange(qkv_block.reshape(count, 8, 768), BOTH)
    rest, qkv_all = lax.optimization_barrier((rest, qkv_all))
    rest = lax.all_gather(rest, "req", axis=0, tiled=True, axis_index_groups=column)
    rest = [rest.reshape(count, 8, REST)]
    far = jnp.arange(count, dtype=jnp.int32)
    from_req = far // 16 % 2 * 16 + far // 32 * 4 + far // 4 % 4
    rest_target = shard_map[from_req * tp_count + (tp_index ^ tp_order[far % 4])]
    qkv_w = qkv_all[source].reshape(width, 768)
    query, kv, cache = qkv_project(normed, qkv_w, *turns[1])
    parts = 2
    state = attend(0, 1, table, query, qseg, (kv, segs[1]), ())
    core = (tp_index % 2).reshape(1)
    others = [swap(side, 1) for side in sides]
    others, state = lax.optimization_barrier((others, state))
    left, right = (
        halo_project(core, side, other, qkv_w[:, 256:], *turn)
        for side, other, turn in zip(sides, others, (turns[0], turns[2]))
    )
    mixed = [
        attend(part, parts, table, query, qseg, (left, segs[0], right, segs[2]), state)
        for part in range(parts)
    ]

    last_slot = (ends - 1 - base).reshape(requests, 1)
    order = jnp.concatenate([tp_index ^ tp_order, rest_target])
    picked = jnp.zeros((2, requests, 512), F32)
    bulk = []
    after = mixed[1]
    for part in range(parts):
        keep, send, picked = mlp(
            order,
            gather_tp(mixed[part], after),
            hidden_in,
            part * (slots // parts // 256),
            mlp_gain,
            last_slot,
            picked,
            rest,
        )
        after = (keep, send)
        bulk.append((keep, send))

    each = requests // req_count
    last_mine = reduce_far(*reduce_core(picked[0], picked[1].astype(BF)))
    bulk, last_mine = lax.optimization_barrier((bulk, last_mine))
    taken = exchange(last_mine.reshape(req_count, each, 256), "req").astype(F32).sum(axis=0)
    spread = exchange(jnp.broadcast_to(taken.astype(BF)[None], (count, each, 256)), BOTH)
    hidden_out = jnp.concatenate([reduce_far(*reduce_core(*pair)) for pair in bulk], axis=0)
    last = (
        spread.reshape(req_count, tp_count, each, 256)
        .transpose(0, 2, 1, 3)
        .reshape(requests, width)
        .astype(F32)
    )
    last_rms = jnp.sqrt(jnp.mean(last * last, axis=-1))
    choose = (tenant[:, None] == jnp.arange(final_gain.shape[0], dtype=jnp.int32)[None, :]).astype(
        F32
    )
    gain_rows = jnp.dot(
        choose, final_gain, precision=lax.Precision.HIGHEST, preferred_element_type=F32
    )
    final = layer_norm(last, gain_rows).astype(BF)
    logits = contract_last(final, head.astype(BF))
    top = jnp.max(logits, axis=-1)
    tops = exchange(jnp.broadcast_to(top[None], (count, requests)), BOTH)
    top_logit = jnp.max(tops, axis=0)
    return (hidden_out, cache, last_rms, top_logit)


def solution(mesh):
    rows = P(BOTH, None)
    placed = (P("req", None), P(), P(), P()) + (rows,) * 8 + (P(), P(), P())
    return jax.shard_map(
        body,
        mesh=mesh,
        in_specs=placed,
        out_specs=(P("req", "tp"), P(None, "req", "tp"), P(), P()),
        check_vma=False,
    )
```

```python
import functools

import jax
import jax.numpy as jnp
from jax import lax
from jax.experimental import pallas as pl
from jax.experimental.pallas import tpu as pltpu
from jax.sharding import PartitionSpec as P

HEADS = 16
HEAD_DIM = 64
THETA = 160000.0
EPS = 1e-05
BF = jnp.bfloat16
F32 = jnp.float32
BOTH = ("req", "tp")
NEG = -1e30
FFP = 768
REST = 3 * FFP + 1024
QB = 256
KB = 256


def vmem(*shape):
    return pl.BlockSpec(shape, lambda *_: (0,) * len(shape))


def params():
    return pltpu.CompilerParams(vmem_limit_bytes=60 * 1024 * 1024)


def cost(flops, moved, transcendentals=0):
    return pl.CostEstimate(flops=flops, bytes_accessed=moved, transcendentals=transcendentals)


def prep_kernel(order, wq, wk, wv, wo, wi, wg, w2, qkv, rest):
    row = lax.broadcasted_iota(jnp.int32, (256, 256), 0)
    col = lax.broadcasted_iota(jnp.int32, (256, 256), 1)
    source = (col % 128) // 32 * 64 + col // 128 * 32 + col % 32
    turn = jnp.where(row == source, 1.0, 0.0).astype(BF)
    trow = lax.broadcasted_iota(jnp.int32, (64, 128), 0)
    tcol = lax.broadcasted_iota(jnp.int32, (64, 128), 1)
    for t in range(4):
        at = slice(256 * t, 256 * t + 256)
        q, k = (
            jnp.dot(w[:, at].astype(BF), turn, preferred_element_type=F32).astype(BF)
            for w in (wq, wk)
        )
        mine = jnp.concatenate([q, k, wv[:, at].astype(BF)], axis=1)
        for r in range(qkv.shape[0]):
            qkv[r, t] = mine
        pick = jnp.where((trow == tcol + 16 * t) & (tcol < 16), 1.0, 0.0).astype(BF)
        to = order[t]
        for n, w in enumerate((wi, wg, w2)):
            rest[to, :, FFP * n : FFP * n + 640] = w[:, 640 * t : 640 * t + 640].astype(BF)
            rest[to, :, FFP * n + 640 : FFP * n + 768] = jnp.dot(
                w[:, 2560:2624].astype(BF), pick, preferred_element_type=F32
            ).astype(BF)
        rest[to, :, 3 * FFP :] = wo[...].astype(BF)


def prep(req_count, order, *weights):
    return pl.pallas_call(
        prep_kernel,
        in_specs=[pl.BlockSpec(memory_space=pltpu.SMEM)] + [vmem(*w.shape) for w in weights],
        out_shape=(
            jax.ShapeDtypeStruct((req_count, 4, 8, 768), BF),
            jax.ShapeDtypeStruct((4, 8, REST), BF),
        ),
        compiler_params=params(),
        name="prep",
    )(order, *weights)


def layer_norm(values, gain):
    center = jnp.mean(values, axis=-1, keepdims=True)
    spread = jnp.mean(values * values, axis=-1, keepdims=True) - center * center
    return (values - center) * lax.rsqrt(spread + EPS) * gain


def norm_kernel(h, gain, out):
    out[...] = layer_norm(h[...].astype(F32), gain[...]).astype(BF)


def norm(h, gain):
    rows = h.shape[0]
    return pl.pallas_call(
        norm_kernel,
        grid=(rows // 512,),
        in_specs=[pl.BlockSpec((512, 1024), lambda i: (i, 0)), vmem(1, 1024)],
        out_specs=pl.BlockSpec((512, 1024), lambda i: (i, 0)),
        out_shape=jax.ShapeDtypeStruct((rows, 1024), BF),
        compiler_params=params(),
        cost_estimate=cost(1 << 24, 1 << 23),
        name="norm",
    )(h, gain.reshape(1, 1024))


def qkv_kernel(x, w, cos, sin, q, kv, cache):
    row = lax.broadcasted_iota(jnp.int32, (256, 256), 0)
    col = lax.broadcasted_iota(jnp.int32, (256, 256), 1)
    source = (col % 128) // 32 * 64 + col // 128 * 32 + col % 32
    back = jnp.where(source == row, 1.0, 0.0).astype(BF)
    y = jnp.dot(x[...], w[...], preferred_element_type=F32)
    c = cos[...]
    s = sin[...]

    def turned(a, b):
        return jnp.concatenate([a * c - b * s, b * c + a * s], axis=1)

    q[...] = (turned(y[:, :128], y[:, 128:256]).astype(BF).astype(F32) * 0.125).astype(BF)
    k = turned(y[:, 256:384], y[:, 384:512]).astype(BF)
    v = y[:, 512:].astype(BF)
    for n in range(x.shape[0] // KB):
        kv[n, 0] = k[KB * n : KB * n + KB]
        kv[n, 1] = jnp.transpose(v[KB * n : KB * n + KB])
    cache[0] = lax.dot_general(
        k, back, (((1,), (1,)), ((), ())), preferred_element_type=F32
    ).astype(BF)
    cache[1] = v


def qkv_project(x, w, cos, sin):
    rows = x.shape[0]
    n = 512
    return pl.pallas_call(
        qkv_kernel,
        grid=(rows // n,),
        in_specs=[
            pl.BlockSpec((n, 1024), lambda i: (i, 0)),
            vmem(1024, 768),
            pl.BlockSpec((n, 128), lambda i: (i, 0)),
            pl.BlockSpec((n, 128), lambda i: (i, 0)),
        ],
        out_specs=[
            pl.BlockSpec((n, 256), lambda i: (i, 0)),
            pl.BlockSpec((n // KB, 2, KB, 256), lambda i: (i, 0, 0, 0)),
            pl.BlockSpec((2, n, 256), lambda i: (0, i, 0)),
        ],
        out_shape=(
            jax.ShapeDtypeStruct((rows, 256), BF),
            jax.ShapeDtypeStruct((rows // KB, 2, KB, 256), BF),
            jax.ShapeDtypeStruct((2, rows, 256), BF),
        ),
        compiler_params=params(),
        cost_estimate=cost(2 * rows * 1024 * 768, 12 << 20),
        name="qkv",
    )(x, w, cos, sin)


VR = HEAD_DIM + 8


def attend_chunk(at, blocks, qm, kv, kseg, qseg, m_sc, acc):
    size = blocks * KB
    k = kv[pl.ds(at, blocks), 0].reshape(size, 256)
    same = kseg[pl.ds(pl.multiple_of(at * KB, KB), size), 0:1] == qseg[...]
    ones = jnp.ones((8, size), BF)
    scores = []
    for h in range(4):
        s = contract_last(k, qm[h])
        scores.append(jnp.where(same, s, NEG))
    for h in range(4):
        old = m_sc[h]
        new = jnp.maximum(old, jnp.max(scores[h], axis=0, keepdims=True))
        p = jnp.exp(scores[h] - new).astype(BF)
        fade = jnp.exp(old - new)
        m_sc[h] = new
        v = [kv[at + n, 1, HEAD_DIM * h : HEAD_DIM * h + HEAD_DIM, :] for n in range(blocks)]
        v = jnp.concatenate([jnp.concatenate(v, axis=1), ones], axis=0)
        acc[h] = acc[h] * fade + jnp.dot(v, p, preferred_element_type=F32)


def attend_span(table, at, i, *refs):
    start = table[at, i]
    pairs = table[at + 1, i] // 2

    @pl.loop(0, pairs)
    def _(c):
        attend_chunk(start + 2 * c, 2, *refs)

    @pl.when(table[at + 1, i] % 2 == 1)
    def _():
        attend_chunk(start + 2 * pairs, 1, *refs)


def spread_heads(q, qm):
    lane = lax.broadcasted_iota(jnp.int32, (QB, 256), 1)
    for h in range(4):
        qm[h] = jnp.where((lane % 128) // 32 == h, q[...].astype(F32), 0.0).astype(BF)


def own_kernel(table, q, qseg, kv, kseg, acc_out, m_out, qm, m_sc, acc):
    i = pl.program_id(0)
    spread_heads(q, qm)
    m_sc[...] = jnp.full_like(m_sc, NEG)
    acc[...] = jnp.zeros_like(acc)
    attend_span(table, 0, i, qm, kv, kseg, qseg, m_sc, acc)
    acc_out[...] = acc[...]
    m_out[...] = m_sc[...]


def halo_kernel(base, table, q, qseg, lkv, lseg, rkv, rseg, acc_in, m_in, out, qm, m_sc, acc):
    i = pl.program_id(0) + base
    spread_heads(q, qm)
    m_sc[...] = m_in[...]
    acc[...] = acc_in[...]
    attend_span(table, 2, i, qm, lkv, lseg, qseg, m_sc, acc)
    attend_span(table, 4, i, qm, rkv, rseg, qseg, m_sc, acc)
    heads = [acc[h, :HEAD_DIM] / acc[h, HEAD_DIM : HEAD_DIM + 1] for h in range(4)]
    out[...] = jnp.transpose(jnp.concatenate(heads, axis=0)).astype(BF)


def attend(part, parts, table, q, qseg, sources, state):
    rows = q.shape[0]
    steps = rows // QB // parts
    base = part * steps
    state_specs = [
        pl.BlockSpec((4, VR, QB), lambda i, *_: (0, 0, i + base)),
        pl.BlockSpec((4, 1, QB), lambda i, *_: (0, 0, i + base)),
    ]
    if state:
        kernel = functools.partial(halo_kernel, base)
        out_specs = pl.BlockSpec((QB, 256), lambda i, *_: (i, 0))
        out_shape = jax.ShapeDtypeStruct((rows // parts, 256), BF)
    else:
        kernel = own_kernel
        out_specs = state_specs
        out_shape = (
            jax.ShapeDtypeStruct((4, VR, rows), F32),
            jax.ShapeDtypeStruct((4, 1, rows), F32),
        )
    return pl.pallas_call(
        kernel,
        grid_spec=pltpu.PrefetchScalarGridSpec(
            num_scalar_prefetch=1,
            grid=(steps,),
            in_specs=[
                pl.BlockSpec((QB, 256), lambda i, *_: (i + base, 0)),
                pl.BlockSpec((1, QB), lambda i, *_: (0, i + base)),
            ]
            + [vmem(*x.shape) for x in sources]
            + state_specs[: len(state)],
            out_specs=out_specs,
            scratch_shapes=[
                pltpu.VMEM((4, QB, 256), BF),
                pltpu.VMEM((4, 1, QB), F32),
                pltpu.VMEM((4, VR, QB), F32),
            ],
        ),
        out_shape=out_shape,
        compiler_params=params(),
        cost_estimate=cost(12 << 30, 8 << 20, 12 << 20),
        name="attend_halo" if state else "attend_own",
    )(table, q, qseg, *sources, *state)


def contract_last(a, b):
    return lax.dot_general(a, b, (((1,), (1,)), ((), ())), preferred_element_type=F32)


def mlp_kernel(base, table, m0, m1, m2, m3, h, gain, last, before, *refs):
    *pieces, keep, send, picked, w, sem = refs
    count = w.shape[0]

    @pl.when(pl.program_id(0) == 0)
    def _():
        done = 4
        for piece in pieces:

            @pl.loop(0, piece.shape[0])
            def _(n, piece=piece, done=done):
                pltpu.make_async_copy(piece.at[n], w.at[table[done + n]], sem).start()

            done += piece.shape[0]
        pltpu.make_async_copy(w, w, sem).wait()

    def rows(at, size, lo, width):
        return w[pl.ds(at, size), :, pl.ds(lo, width)].reshape(8 * size, width)

    n = h.shape[0]
    wide = h[...].astype(F32)
    total = None
    for j, m in enumerate((m0, m1, m2, m3)):
        lo = pl.multiple_of(3 * FFP + 256 * table[j], 128)
        piece = contract_last(m[...], rows(0, count, lo, 256))
        total = piece if total is None else total + piece
    first = (wide + total).astype(BF)
    wide = first.astype(F32)
    normed = layer_norm(wide, gain[...]).astype(BF)
    a = jnp.dot(normed, rows(0, count, 0, FFP), preferred_element_type=F32)
    b = jnp.dot(normed, rows(0, count, FFP, FFP), preferred_element_type=F32)
    inner = (0.5 * a * (1.0 + lax.erf(a * (0.5**0.5))) * b).astype(BF)
    mine = jnp.zeros((n, 256), F32)
    for t in range(4):
        mine = jnp.where(table[0] == t, wide[:, 256 * t : 256 * t + 256], mine)

    def down(j):
        return contract_last(inner, rows(table[j] * (count // 4), count // 4, 2 * FFP, FFP))

    kept = jnp.concatenate([down(0) + mine, down(1)], axis=1)
    sent = jnp.concatenate([down(2), down(3)], axis=1).astype(BF)
    keep[...] = kept
    send[...] = sent
    slot = lax.broadcasted_iota(jnp.int32, (last.shape[0], n), 1) + (pl.program_id(0) + base) * n
    ends_here = jnp.where(last[...] == slot, 1.0, 0.0).astype(BF)
    coarse = kept.astype(BF)
    fine = (kept - coarse.astype(F32)).astype(BF)

    def pick(x):
        return jnp.dot(ends_here, x, preferred_element_type=F32)

    @pl.when(pl.program_id(0) == 0)
    def _():
        picked[...] = before[...]

    picked[0] += pick(coarse) + pick(fine)
    picked[1] += pick(sent)


def mlp(table, mixed, h, base, gain, last, before, pieces):
    n = 256
    rows = mixed[0].shape[0]
    count = sum(piece.shape[0] for piece in pieces)

    def block(width):
        return pl.BlockSpec((n, width), lambda i, *_: (i, 0))

    return pl.pallas_call(
        functools.partial(mlp_kernel, base),
        grid_spec=pltpu.PrefetchScalarGridSpec(
            num_scalar_prefetch=1,
            grid=(rows // n,),
            in_specs=[block(256)] * 4
            + [pl.BlockSpec((n, 1024), lambda i, *_: (i + base, 0))]
            + [vmem(1, 1024), vmem(*last.shape), vmem(*before.shape)]
            + [pl.BlockSpec(memory_space=pl.ANY)] * len(pieces),
            out_specs=[block(512), block(512), vmem(*before.shape)],
            scratch_shapes=[pltpu.VMEM((count, 8, REST), BF), pltpu.SemaphoreType.DMA(())],
        ),
        out_shape=(
            jax.ShapeDtypeStruct((rows, 512), F32),
            jax.ShapeDtypeStruct((rows, 512), BF),
            jax.ShapeDtypeStruct(before.shape, F32),
        ),
        compiler_params=params(),
        cost_estimate=cost(rows * 1024 * (1024 + 3 * FFP) * 2, 12 << 20, rows * FFP),
        name="mlp",
    )(table, *mixed, h, gain.reshape(1, 1024), last, before, *pieces)


def swap(x, bit):
    return lax.ppermute(x, "tp", [(i, i ^ bit) for i in range(4)])


def turn_bits(n):
    return n % 2 * 2 + n // 2


def gather_tp(x, after=None):
    far = swap(x, 2)
    near = swap(x, 1)
    if after is not None:
        far, _ = lax.optimization_barrier((far, after))
    return x, far, near, swap(far, 1)


def reduce_core(keep, send):
    got = swap(send, 1).astype(F32)
    return keep[:, :256] + got[:, :256], (keep[:, 256:] + got[:, 256:]).astype(BF)


def reduce_far(mine, send):
    return (mine + swap(send, 2).astype(F32)).astype(BF)


def shift(x, by):
    count = lax.axis_size("req")
    return lax.ppermute(x, "req", [(i, i + by) for i in range(count) if 0 <= i + by < count])


def exchange(x, axes):
    return lax.all_to_all(x, axes, split_axis=0, concat_axis=0, tiled=True)


def body(
    hidden_in,
    lengths,
    tenant,
    shard_map,
    wq,
    wk,
    wv,
    wo,
    wi_in,
    wi_gate,
    wo2,
    head,
    attn_gain,
    mlp_gain,
    final_gain,
):
    req_count = lax.axis_size("req")
    tp_count = lax.axis_size("tp")
    count = req_count * tp_count
    req_index = lax.axis_index("req")
    tp_index = lax.axis_index("tp")
    slots, width = hidden_in.shape
    requests = lengths.shape[0]

    four = jnp.arange(4, dtype=jnp.int32)
    place_of = turn_bits(four ^ tp_index)
    qkv_block, rest_block = prep(req_count, place_of, wq, wk, wv, wo, wi_in, wi_gate, wo2)
    place = jnp.arange(count, dtype=jnp.int32)
    source = jnp.sum(
        jnp.where(shard_map[None, :] == place[:, None], place[None, :], 0), axis=1
    )
    rest_rows = jnp.concatenate(
        [rest_block[0], swap(rest_block[1], 2), swap(rest_block[2], 1), swap(rest_block[3], 3)], axis=0
    )
    hidden, lengths, rest_rows = lax.optimization_barrier((hidden_in, lengths, rest_rows))

    ends = jnp.cumsum(lengths)
    base = req_index * slots
    index = base - slots + jnp.arange(3 * slots, dtype=jnp.int32)
    segment = jnp.sum((ends[None, :] <= index[:, None]).astype(jnp.int32), axis=1)
    segment = jnp.where((index >= 0) & (index < slots * req_count), segment, -1)
    own = base + jnp.arange(slots, dtype=jnp.int32)
    start_of = jnp.max(jnp.where(ends[None, :] <= own[:, None], ends[None, :], 0), axis=1)
    position = (own - start_of).astype(F32)
    lane = jnp.arange(128, dtype=jnp.int32) % (HEAD_DIM // 2)
    freq = THETA ** (-(2.0 * lane.astype(F32)) / HEAD_DIM)
    angle = position[:, None] * freq[None, :]
    turn = (jnp.cos(angle), jnp.sin(angle))
    begin = base + jnp.arange(slots // QB, dtype=jnp.int32) * QB
    close = begin + QB - 1
    low = jnp.max(jnp.where(ends[None, :] <= begin[:, None], ends[None, :], 0), axis=1) - base
    high = jnp.min(jnp.where(ends[None, :] > close[:, None], ends[None, :], 1 << 30), axis=1) - base

    blocks = slots // KB
    own_0 = jnp.maximum(low, 0) // KB
    own_1 = (jnp.minimum(high, slots) + KB - 1) // KB
    left_0 = (jnp.minimum(low, 0) + slots) // KB
    right_1 = (jnp.maximum(high - slots, 0) + KB - 1) // KB
    table = jnp.stack(
        [own_0, own_1 - own_0, left_0, blocks - left_0, jnp.zeros_like(right_1), right_1]
    )
    segs = segment.reshape(3, slots, 1)
    qseg = segment[slots : 2 * slots].reshape(1, slots)

    normed = norm(hidden, attn_gain)
    qkv_all = exchange(qkv_block.reshape(count, 8, 768), BOTH)
    qkv_w = qkv_all[source].reshape(width, 768)
    rest = [lax.all_gather(rest_rows, "req", axis=0, tiled=True).reshape(count, 8, REST)]
    far = jnp.arange(count, dtype=jnp.int32)
    rest_target = shard_map[far // 4 * tp_count + (tp_index ^ turn_bits(far % 4))]
    query, kv, cache = qkv_project(normed, qkv_w, *turn)
    left = shift(kv, 1)
    right = shift(kv, -1)
    parts = 2
    state = attend(0, 1, table, query, qseg, (kv, segs[1]), ())
    mixed = [
        attend(part, parts, table, query, qseg, (left, segs[0], right, segs[2]), state)
        for part in range(parts)
    ]

    last_slot = (ends - 1 - base).reshape(requests, 1)
    order = jnp.concatenate([tp_index ^ turn_bits(four), rest_target])
    picked = jnp.zeros((2, requests, 512), F32)
    bulk = []
    after = mixed[1]
    for part in range(parts):
        keep, send, picked = mlp(
            order,
            gather_tp(mixed[part], after),
            hidden_in,
            part * (slots // parts // 256),
            mlp_gain,
            last_slot,
            picked,
            rest,
        )
        after = (keep, send)
        bulk.append((keep, send))

    each = requests // req_count
    last_mine = reduce_far(*reduce_core(picked[0], picked[1].astype(BF)))
    bulk, last_mine = lax.optimization_barrier((bulk, last_mine))
    taken = exchange(last_mine.reshape(req_count, each, 256), "req").astype(F32).sum(axis=0)
    spread = exchange(jnp.broadcast_to(taken.astype(BF)[None], (count, each, 256)), BOTH)
    hidden_out = jnp.concatenate([reduce_far(*reduce_core(*pair)) for pair in bulk], axis=0)
    last = (
        spread.reshape(req_count, tp_count, each, 256)
        .transpose(0, 2, 1, 3)
        .reshape(requests, width)
        .astype(F32)
    )
    last_rms = jnp.sqrt(jnp.mean(last * last, axis=-1))
    choose = (tenant[:, None] == jnp.arange(final_gain.shape[0], dtype=jnp.int32)[None, :]).astype(
        F32
    )
    gain_rows = jnp.dot(
        choose, final_gain, precision=lax.Precision.HIGHEST, preferred_element_type=F32
    )
    final = layer_norm(last, gain_rows).astype(BF)
    logits = contract_last(final, head.astype(BF))
    top = jnp.max(logits, axis=-1)
    tops = exchange(jnp.broadcast_to(top[None], (count, requests)), BOTH)
    top_logit = jnp.max(tops, axis=0)
    return (hidden_out, cache, last_rms, top_logit)


def solution(mesh):
    rows = P(BOTH, None)
    placed = (P("req", None), P(), P(), P()) + (rows,) * 8 + (P(), P(), P())
    return jax.shard_map(
        body,
        mesh=mesh,
        in_specs=placed,
        out_specs=(P("req", "tp"), P(None, "req", "tp"), P(), P()),
        check_vma=False,
    )
```

```python
import functools

import jax
import jax.numpy as jnp
from jax import lax
from jax.experimental import pallas as pl
from jax.experimental.pallas import tpu as pltpu
from jax.sharding import PartitionSpec as P

HEADS = 16
HEAD_DIM = 64
THETA = 160000.0
EPS = 1e-05
BF = jnp.bfloat16
F32 = jnp.float32
BOTH = ("req", "tp")
NEG = -1e30
FFP = 768
REST = 3 * FFP
QB = 256
KB = 256


def vmem(*shape):
    return pl.BlockSpec(shape, lambda *_: (0,) * len(shape))


def params():
    return pltpu.CompilerParams(vmem_limit_bytes=60 * 1024 * 1024)


def cost(flops, moved, transcendentals=0):
    return pl.CostEstimate(flops=flops, bytes_accessed=moved, transcendentals=transcendentals)


def prep_kernel(order, wq, wk, wv, wo, wi, wg, w2, first, rest):
    row = lax.broadcasted_iota(jnp.int32, (256, 256), 0)
    col = lax.broadcasted_iota(jnp.int32, (256, 256), 1)
    source = (col % 128) // 32 * 64 + col // 128 * 32 + col % 32
    turn = jnp.where(row == source, 1.0, 0.0).astype(BF)
    trow = lax.broadcasted_iota(jnp.int32, (64, 128), 0)
    tcol = lax.broadcasted_iota(jnp.int32, (64, 128), 1)
    for t in range(4):
        at = slice(256 * t, 256 * t + 256)
        q, k = (
            jnp.dot(w[:, at].astype(BF), turn, preferred_element_type=F32).astype(BF)
            for w in (wq, wk)
        )
        mine = jnp.concatenate([q, k, wv[:, at].astype(BF), wo[:, at].astype(BF)], axis=1)
        for r in range(first.shape[0]):
            first[r, t] = mine
        pick = jnp.where((trow == tcol + 16 * t) & (tcol < 16), 1.0, 0.0).astype(BF)
        to = order[t]
        for n, w in enumerate((wi, wg, w2)):
            rest[to, :, FFP * n : FFP * n + 640] = w[:, 640 * t : 640 * t + 640].astype(BF)
            rest[to, :, FFP * n + 640 : FFP * n + 768] = jnp.dot(
                w[:, 2560:2624].astype(BF), pick, preferred_element_type=F32
            ).astype(BF)


def prep(req_count, order, *weights):
    return pl.pallas_call(
        prep_kernel,
        in_specs=[pl.BlockSpec(memory_space=pltpu.SMEM)] + [vmem(*w.shape) for w in weights],
        out_shape=(
            jax.ShapeDtypeStruct((req_count, 4, 8, 1024), BF),
            jax.ShapeDtypeStruct((4, 8, REST), BF),
        ),
        compiler_params=params(),
        name="prep",
    )(order, *weights)


def layer_norm(values, gain):
    center = jnp.mean(values, axis=-1, keepdims=True)
    spread = jnp.mean(values * values, axis=-1, keepdims=True) - center * center
    return (values - center) * lax.rsqrt(spread + EPS) * gain


def norm_kernel(h, gain, out):
    out[...] = layer_norm(h[...].astype(F32), gain[...]).astype(BF)


def norm(h, gain):
    rows = h.shape[0]
    return pl.pallas_call(
        norm_kernel,
        grid=(rows // 512,),
        in_specs=[pl.BlockSpec((512, 1024), lambda i: (i, 0)), vmem(1, 1024)],
        out_specs=pl.BlockSpec((512, 1024), lambda i: (i, 0)),
        out_shape=jax.ShapeDtypeStruct((rows, 1024), BF),
        compiler_params=params(),
        cost_estimate=cost(1 << 24, 1 << 23),
        name="norm",
    )(h, gain.reshape(1, 1024))


def qkv_kernel(x, w, cos, sin, q, kv, cache):
    row = lax.broadcasted_iota(jnp.int32, (256, 256), 0)
    col = lax.broadcasted_iota(jnp.int32, (256, 256), 1)
    source = (col % 128) // 32 * 64 + col // 128 * 32 + col % 32
    back = jnp.where(source == row, 1.0, 0.0).astype(BF)
    y = jnp.dot(x[...], w[...], preferred_element_type=F32)
    c = cos[...]
    s = sin[...]

    def turned(a, b):
        return jnp.concatenate([a * c - b * s, b * c + a * s], axis=1)

    q[...] = (turned(y[:, :128], y[:, 128:256]).astype(BF).astype(F32) * 0.125).astype(BF)
    k = turned(y[:, 256:384], y[:, 384:512]).astype(BF)
    v = y[:, 512:].astype(BF)
    for n in range(x.shape[0] // KB):
        kv[n, 0] = k[KB * n : KB * n + KB]
        kv[n, 1] = jnp.transpose(v[KB * n : KB * n + KB])
    cache[0] = lax.dot_general(
        k, back, (((1,), (1,)), ((), ())), preferred_element_type=F32
    ).astype(BF)
    cache[1] = v


def qkv_project(x, w, cos, sin):
    rows = x.shape[0]
    n = 512
    return pl.pallas_call(
        qkv_kernel,
        grid=(rows // n,),
        in_specs=[
            pl.BlockSpec((n, 1024), lambda i: (i, 0)),
            vmem(1024, 768),
            pl.BlockSpec((n, 128), lambda i: (i, 0)),
            pl.BlockSpec((n, 128), lambda i: (i, 0)),
        ],
        out_specs=[
            pl.BlockSpec((n, 256), lambda i: (i, 0)),
            pl.BlockSpec((n // KB, 2, KB, 256), lambda i: (i, 0, 0, 0)),
            pl.BlockSpec((2, n, 256), lambda i: (0, i, 0)),
        ],
        out_shape=(
            jax.ShapeDtypeStruct((rows, 256), BF),
            jax.ShapeDtypeStruct((rows // KB, 2, KB, 256), BF),
            jax.ShapeDtypeStruct((2, rows, 256), BF),
        ),
        compiler_params=params(),
        cost_estimate=cost(2 * rows * 1024 * 768, 12 << 20),
        name="qkv",
    )(x, w, cos, sin)


VR = HEAD_DIM + 8


def attend_chunk(at, blocks, qm, kv, kseg, qseg, m_sc, acc):
    size = blocks * KB
    k = kv[pl.ds(at, blocks), 0].reshape(size, 256)
    same = kseg[pl.ds(pl.multiple_of(at * KB, KB), size), 0:1] == qseg[...]
    ones = jnp.ones((8, size), BF)
    scores = []
    for h in range(4):
        s = contract_last(k, qm[h])
        scores.append(jnp.where(same, s, NEG))
    for h in range(4):
        old = m_sc[h]
        new = jnp.maximum(old, jnp.max(scores[h], axis=0, keepdims=True))
        p = jnp.exp(scores[h] - new).astype(BF)
        fade = jnp.exp(old - new)
        m_sc[h] = new
        v = [kv[at + n, 1, HEAD_DIM * h : HEAD_DIM * h + HEAD_DIM, :] for n in range(blocks)]
        v = jnp.concatenate([jnp.concatenate(v, axis=1), ones], axis=0)
        acc[h] = acc[h] * fade + jnp.dot(v, p, preferred_element_type=F32)


def attend_span(table, at, i, *refs):
    start = table[at, i]
    pairs = table[at + 1, i] // 2

    @pl.loop(0, pairs)
    def _(c):
        attend_chunk(start + 2 * c, 2, *refs)

    @pl.when(table[at + 1, i] % 2 == 1)
    def _():
        attend_chunk(start + 2 * pairs, 1, *refs)


def spread_heads(q, qm):
    lane = lax.broadcasted_iota(jnp.int32, (QB, 256), 1)
    for h in range(4):
        qm[h] = jnp.where((lane % 128) // 32 == h, q[...].astype(F32), 0.0).astype(BF)


def own_kernel(table, q, qseg, kv, kseg, acc_out, m_out, qm, m_sc, acc):
    i = pl.program_id(0)
    spread_heads(q, qm)
    m_sc[...] = jnp.full_like(m_sc, NEG)
    acc[...] = jnp.zeros_like(acc)
    attend_span(table, 0, i, qm, kv, kseg, qseg, m_sc, acc)
    acc_out[...] = acc[...]
    m_out[...] = m_sc[...]


def halo_kernel(base, table, q, qseg, lkv, lseg, rkv, rseg, acc_in, m_in, out, qm, m_sc, acc):
    i = pl.program_id(0) + base
    spread_heads(q, qm)
    m_sc[...] = m_in[...]
    acc[...] = acc_in[...]
    attend_span(table, 2, i, qm, lkv, lseg, qseg, m_sc, acc)
    attend_span(table, 4, i, qm, rkv, rseg, qseg, m_sc, acc)
    heads = [acc[h, :HEAD_DIM] / acc[h, HEAD_DIM : HEAD_DIM + 1] for h in range(4)]
    out[...] = jnp.transpose(jnp.concatenate(heads, axis=0)).astype(BF)


def attend(part, parts, table, q, qseg, sources, state):
    rows = q.shape[0]
    steps = rows // QB // parts
    base = part * steps
    state_specs = [
        pl.BlockSpec((4, VR, QB), lambda i, *_: (0, 0, i + base)),
        pl.BlockSpec((4, 1, QB), lambda i, *_: (0, 0, i + base)),
    ]
    if state:
        kernel = functools.partial(halo_kernel, base)
        out_specs = pl.BlockSpec((QB, 256), lambda i, *_: (i, 0))
        out_shape = jax.ShapeDtypeStruct((rows // parts, 256), BF)
    else:
        kernel = own_kernel
        out_specs = state_specs
        out_shape = (
            jax.ShapeDtypeStruct((4, VR, rows), F32),
            jax.ShapeDtypeStruct((4, 1, rows), F32),
        )
    return pl.pallas_call(
        kernel,
        grid_spec=pltpu.PrefetchScalarGridSpec(
            num_scalar_prefetch=1,
            grid=(steps,),
            in_specs=[
                pl.BlockSpec((QB, 256), lambda i, *_: (i + base, 0)),
                pl.BlockSpec((1, QB), lambda i, *_: (0, i + base)),
            ]
            + [vmem(*x.shape) for x in sources]
            + state_specs[: len(state)],
            out_specs=out_specs,
            scratch_shapes=[
                pltpu.VMEM((4, QB, 256), BF),
                pltpu.VMEM((4, 1, QB), F32),
                pltpu.VMEM((4, VR, QB), F32),
            ],
        ),
        out_shape=out_shape,
        compiler_params=params(),
        cost_estimate=cost(12 << 30, 8 << 20, 12 << 20),
        name="attend_halo" if state else "attend_own",
    )(table, q, qseg, *sources, *state)


def contract_last(a, b):
    return lax.dot_general(a, b, (((1,), (1,)), ((), ())), preferred_element_type=F32)


def mlp_kernel(base, table, m0, m1, m2, m3, o0, o1, o2, o3, h, gain, last, before, *refs):
    *pieces, keep, send, picked, w, sem = refs
    count = w.shape[0]

    @pl.when(pl.program_id(0) == 0)
    def _():
        done = 4
        for piece in pieces:

            @pl.loop(0, piece.shape[0])
            def _(n, piece=piece, done=done):
                pltpu.make_async_copy(piece.at[n], w.at[table[done + n]], sem).start()

            done += piece.shape[0]
        pltpu.make_async_copy(w, w, sem).wait()

    def rows(at, size, lo, width):
        return w[pl.ds(at, size), :, pl.ds(lo, width)].reshape(8 * size, width)

    n = h.shape[0]
    wide = h[...].astype(F32)
    total = None
    for m, o in ((m0, o0), (m1, o1), (m2, o2), (m3, o3)):
        piece = contract_last(m[...], o[...])
        total = piece if total is None else total + piece
    first = (wide + total).astype(BF)
    wide = first.astype(F32)
    normed = layer_norm(wide, gain[...]).astype(BF)
    a = jnp.dot(normed, rows(0, count, 0, FFP), preferred_element_type=F32)
    b = jnp.dot(normed, rows(0, count, FFP, FFP), preferred_element_type=F32)
    inner = (0.5 * a * (1.0 + lax.erf(a * (0.5**0.5))) * b).astype(BF)
    mine = jnp.zeros((n, 256), F32)
    for t in range(4):
        mine = jnp.where(table[0] == t, wide[:, 256 * t : 256 * t + 256], mine)

    def down(j):
        return contract_last(inner, rows(table[j] * (count // 4), count // 4, 2 * FFP, FFP))

    kept = jnp.concatenate([down(0) + mine, down(1)], axis=1)
    sent = jnp.concatenate([down(2), down(3)], axis=1).astype(BF)
    keep[...] = kept
    send[...] = sent
    slot = lax.broadcasted_iota(jnp.int32, (last.shape[0], n), 1) + (pl.program_id(0) + base) * n
    ends_here = jnp.where(last[...] == slot, 1.0, 0.0).astype(BF)
    coarse = kept.astype(BF)
    fine = (kept - coarse.astype(F32)).astype(BF)

    def pick(x):
        return jnp.dot(ends_here, x, preferred_element_type=F32)

    @pl.when(pl.program_id(0) == 0)
    def _():
        picked[...] = before[...]

    picked[0] += pick(coarse) + pick(fine)
    picked[1] += pick(sent)


def mlp(table, mixed, out_w, h, base, gain, last, before, pieces):
    n = 256
    rows = mixed[0].shape[0]
    count = sum(piece.shape[0] for piece in pieces)

    def block(width):
        return pl.BlockSpec((n, width), lambda i, *_: (i, 0))

    return pl.pallas_call(
        functools.partial(mlp_kernel, base),
        grid_spec=pltpu.PrefetchScalarGridSpec(
            num_scalar_prefetch=1,
            grid=(rows // n,),
            in_specs=[block(256)] * 4
            + [vmem(1024, 256)] * 4
            + [pl.BlockSpec((n, 1024), lambda i, *_: (i + base, 0))]
            + [vmem(1, 1024), vmem(*last.shape), vmem(*before.shape)]
            + [pl.BlockSpec(memory_space=pl.ANY)] * len(pieces),
            out_specs=[block(512), block(512), vmem(*before.shape)],
            scratch_shapes=[pltpu.VMEM((count, 8, REST), BF), pltpu.SemaphoreType.DMA(())],
        ),
        out_shape=(
            jax.ShapeDtypeStruct((rows, 512), F32),
            jax.ShapeDtypeStruct((rows, 512), BF),
            jax.ShapeDtypeStruct(before.shape, F32),
        ),
        compiler_params=params(),
        cost_estimate=cost(rows * 1024 * (1024 + 3 * FFP) * 2, 12 << 20, rows * FFP),
        name="mlp",
    )(table, *mixed, *out_w, h, gain.reshape(1, 1024), last, before, *pieces)


def swap(x, bit):
    return lax.ppermute(x, "tp", [(i, i ^ bit) for i in range(4)])


def turn_bits(n):
    return n % 2 * 2 + n // 2


def reduce_core(keep, send):
    got = swap(send, 1).astype(F32)
    return keep[:, :256] + got[:, :256], (keep[:, 256:] + got[:, 256:]).astype(BF)


def reduce_far(mine, send):
    return (mine + swap(send, 2).astype(F32)).astype(BF)


def shift(x, by):
    count = lax.axis_size("req")
    return lax.ppermute(x, "req", [(i, i + by) for i in range(count) if 0 <= i + by < count])


def exchange(x, axes):
    return lax.all_to_all(x, axes, split_axis=0, concat_axis=0, tiled=True)


def body(
    hidden_in,
    lengths,
    tenant,
    shard_map,
    wq,
    wk,
    wv,
    wo,
    wi_in,
    wi_gate,
    wo2,
    head,
    attn_gain,
    mlp_gain,
    final_gain,
):
    req_count = lax.axis_size("req")
    tp_count = lax.axis_size("tp")
    count = req_count * tp_count
    req_index = lax.axis_index("req")
    tp_index = lax.axis_index("tp")
    slots, width = hidden_in.shape
    requests = lengths.shape[0]

    four = jnp.arange(4, dtype=jnp.int32)
    place_of = turn_bits(four ^ tp_index)
    first_block, rest_block = prep(req_count, place_of, wq, wk, wv, wo, wi_in, wi_gate, wo2)
    place = jnp.arange(count, dtype=jnp.int32)
    source = jnp.sum(
        jnp.where(shard_map[None, :] == place[:, None], place[None, :], 0), axis=1
    )
    rest_rows = jnp.concatenate(
        [rest_block[0], swap(rest_block[1], 2), swap(rest_block[2], 1), swap(rest_block[3], 3)], axis=0
    )
    hidden, lengths, rest_rows = lax.optimization_barrier((hidden_in, lengths, rest_rows))
    rest = lax.all_gather(rest_rows, "req", axis=0, tiled=True).reshape(count, 8, REST)
    far = jnp.arange(count, dtype=jnp.int32)
    rest_target = shard_map[far // 4 * tp_count + (tp_index ^ turn_bits(far % 4))]

    ends = jnp.cumsum(lengths)
    base = req_index * slots
    index = base - slots + jnp.arange(3 * slots, dtype=jnp.int32)
    segment = jnp.sum((ends[None, :] <= index[:, None]).astype(jnp.int32), axis=1)
    segment = jnp.where((index >= 0) & (index < slots * req_count), segment, -1)
    own = base + jnp.arange(slots, dtype=jnp.int32)
    start_of = jnp.max(jnp.where(ends[None, :] <= own[:, None], ends[None, :], 0), axis=1)
    position = (own - start_of).astype(F32)
    lane = jnp.arange(128, dtype=jnp.int32) % (HEAD_DIM // 2)
    freq = THETA ** (-(2.0 * lane.astype(F32)) / HEAD_DIM)
    angle = position[:, None] * freq[None, :]
    turn = (jnp.cos(angle), jnp.sin(angle))
    begin = base + jnp.arange(slots // QB, dtype=jnp.int32) * QB
    close = begin + QB - 1
    low = jnp.max(jnp.where(ends[None, :] <= begin[:, None], ends[None, :], 0), axis=1) - base
    high = jnp.min(jnp.where(ends[None, :] > close[:, None], ends[None, :], 1 << 30), axis=1) - base

    blocks = slots // KB
    own_0 = jnp.maximum(low, 0) // KB
    own_1 = (jnp.minimum(high, slots) + KB - 1) // KB
    left_0 = (jnp.minimum(low, 0) + slots) // KB
    right_1 = (jnp.maximum(high - slots, 0) + KB - 1) // KB
    table = jnp.stack(
        [own_0, own_1 - own_0, left_0, blocks - left_0, jnp.zeros_like(right_1), right_1]
    )
    segs = segment.reshape(3, slots, 1)
    qseg = segment[slots : 2 * slots].reshape(1, slots)

    normed = norm(hidden, attn_gain)
    first_all = exchange(first_block.reshape(count, 8, width), BOTH)
    first_w = first_all[source].reshape(width, width)
    query, kv, cache = qkv_project(normed, first_w, *turn)
    left = shift(kv, 1)
    right = shift(kv, -1)
    out_w, kv = lax.optimization_barrier((first_w[:, 768:], kv))
    out_far, out_near = swap(out_w, 2), swap(out_w, 1)
    parts = 2
    state = attend(0, 1, table, query, qseg, (kv, segs[1]), ())
    out_far, out_near, state = lax.optimization_barrier((out_far, out_near, state))
    out_w = (out_w, out_far, out_near, swap(out_far, 1))
    mixed = [
        attend(part, parts, table, query, qseg, (left, segs[0], right, segs[2]), state)
        for part in range(parts)
    ]

    last_slot = (ends - 1 - base).reshape(requests, 1)
    order = jnp.concatenate([tp_index ^ turn_bits(four), rest_target])
    steps = slots // parts // 256

    def feed(part, pieces, picked):
        return mlp(
            order, pieces, out_w, hidden_in, part * steps, mlp_gain, last_slot, picked, [rest]
        )

    far = [swap(m, 2) for m in mixed]
    near = [swap(m, 1) for m in mixed]
    far[0], _ = lax.optimization_barrier((far[0], mixed[1]))
    keep, send, picked = feed(
        0, (mixed[0], far[0], near[0], swap(far[0], 1)), jnp.zeros((2, requests, 512), F32)
    )
    keep, send, far[1] = lax.optimization_barrier((keep, send, far[1]))
    last_piece = swap(far[1], 1)
    pair, picked, last_piece = lax.optimization_barrier(
        (reduce_core(keep, send), picked, last_piece)
    )
    top = reduce_far(*pair)
    keep, send, picked = feed(1, (mixed[1], far[1], near[1], last_piece), picked)
    picked, top = lax.optimization_barrier((picked, top))

    each = requests // req_count
    last_mine = reduce_far(*reduce_core(picked[0], picked[1].astype(BF)))
    (keep, send), last_mine = lax.optimization_barrier(((keep, send), last_mine))
    taken = exchange(last_mine.reshape(req_count, each, 256), "req").astype(F32).sum(axis=0)
    spread = exchange(jnp.broadcast_to(taken.astype(BF)[None], (count, each, 256)), BOTH)
    hidden_out = jnp.concatenate([top, reduce_far(*reduce_core(keep, send))], axis=0)
    last = (
        spread.reshape(req_count, tp_count, each, 256)
        .transpose(0, 2, 1, 3)
        .reshape(requests, width)
        .astype(F32)
    )
    last_rms = jnp.sqrt(jnp.mean(last * last, axis=-1))
    choose = (tenant[:, None] == jnp.arange(final_gain.shape[0], dtype=jnp.int32)[None, :]).astype(
        F32
    )
    gain_rows = jnp.dot(
        choose, final_gain, precision=lax.Precision.HIGHEST, preferred_element_type=F32
    )
    final = layer_norm(last, gain_rows).astype(BF)
    logits = contract_last(final, head.astype(BF))
    top = jnp.max(logits, axis=-1)
    tops = exchange(jnp.broadcast_to(top[None], (count, requests)), BOTH)
    top_logit = jnp.max(tops, axis=0)
    return (hidden_out, cache, last_rms, top_logit)


def solution(mesh):
    rows = P(BOTH, None)
    placed = (P("req", None), P(), P(), P()) + (rows,) * 8 + (P(), P(), P())
    return jax.shard_map(
        body,
        mesh=mesh,
        in_specs=placed,
        out_specs=(P("req", "tp"), P(None, "req", "tp"), P(), P()),
        check_vma=False,
    )
```

```python
import functools

import jax
import jax.numpy as jnp
from jax import lax
from jax.experimental import pallas as pl
from jax.experimental.pallas import tpu as pltpu
from jax.sharding import PartitionSpec as P

HEADS = 16
HEAD_DIM = 64
THETA = 160000.0
EPS = 1e-05
BF = jnp.bfloat16
F32 = jnp.float32
BOTH = ("req", "tp")
NEG = -1e30
FFP = 768
REST = 3 * FFP
QB = 256
KB = 256


def vmem(*shape):
    return pl.BlockSpec(shape, lambda *_: (0,) * len(shape))


def params():
    return pltpu.CompilerParams(vmem_limit_bytes=60 * 1024 * 1024)


def cost(flops, moved, transcendentals=0):
    return pl.CostEstimate(flops=flops, bytes_accessed=moved, transcendentals=transcendentals)


def prep_kernel(order, wq, wk, wv, wo, wi, wg, w2, first, rest):
    row = lax.broadcasted_iota(jnp.int32, (256, 256), 0)
    col = lax.broadcasted_iota(jnp.int32, (256, 256), 1)
    source = (col % 128) // 32 * 64 + col // 128 * 32 + col % 32
    turn = jnp.where(row == source, 1.0, 0.0).astype(BF)
    trow = lax.broadcasted_iota(jnp.int32, (64, 128), 0)
    tcol = lax.broadcasted_iota(jnp.int32, (64, 128), 1)
    for t in range(4):
        at = slice(256 * t, 256 * t + 256)
        q, k = (
            jnp.dot(w[:, at].astype(BF), turn, preferred_element_type=F32).astype(BF)
            for w in (wq, wk)
        )
        mine = jnp.concatenate([q, k, wv[:, at].astype(BF), wo[:, at].astype(BF)], axis=1)
        for r in range(first.shape[0]):
            first[r, t] = mine
        pick = jnp.where((trow == tcol + 16 * t) & (tcol < 16), 1.0, 0.0).astype(BF)
        to = order[t]
        for n, w in enumerate((wi, wg, w2)):
            rest[to, :, FFP * n : FFP * n + 640] = w[:, 640 * t : 640 * t + 640].astype(BF)
            rest[to, :, FFP * n + 640 : FFP * n + 768] = jnp.dot(
                w[:, 2560:2624].astype(BF), pick, preferred_element_type=F32
            ).astype(BF)


def prep(req_count, order, *weights):
    return pl.pallas_call(
        prep_kernel,
        in_specs=[pl.BlockSpec(memory_space=pltpu.SMEM)] + [vmem(*w.shape) for w in weights],
        out_shape=(
            jax.ShapeDtypeStruct((req_count, 4, 8, 1024), BF),
            jax.ShapeDtypeStruct((4, 8, REST), BF),
        ),
        compiler_params=params(),
        name="prep",
    )(order, *weights)


def layer_norm(values, gain):
    center = jnp.mean(values, axis=-1, keepdims=True)
    spread = jnp.mean(values * values, axis=-1, keepdims=True) - center * center
    return (values - center) * lax.rsqrt(spread + EPS) * gain


def norm_kernel(h, gain, out):
    out[...] = layer_norm(h[...].astype(F32), gain[...]).astype(BF)


def norm(h, gain):
    rows = h.shape[0]
    return pl.pallas_call(
        norm_kernel,
        grid=(rows // 512,),
        in_specs=[pl.BlockSpec((512, 1024), lambda i: (i, 0)), vmem(1, 1024)],
        out_specs=pl.BlockSpec((512, 1024), lambda i: (i, 0)),
        out_shape=jax.ShapeDtypeStruct((rows, 1024), BF),
        compiler_params=params(),
        cost_estimate=cost(1 << 24, 1 << 23),
        name="norm",
    )(h, gain.reshape(1, 1024))


def qkv_kernel(x, w, cos, sin, q, kv, cache):
    row = lax.broadcasted_iota(jnp.int32, (256, 256), 0)
    col = lax.broadcasted_iota(jnp.int32, (256, 256), 1)
    source = (col % 128) // 32 * 64 + col // 128 * 32 + col % 32
    back = jnp.where(source == row, 1.0, 0.0).astype(BF)
    y = jnp.dot(x[...], w[...], preferred_element_type=F32)
    c = cos[...]
    s = sin[...]

    def turned(a, b):
        return jnp.concatenate([a * c - b * s, b * c + a * s], axis=1)

    q[...] = (turned(y[:, :128], y[:, 128:256]).astype(BF).astype(F32) * 0.125).astype(BF)
    k = turned(y[:, 256:384], y[:, 384:512]).astype(BF)
    v = y[:, 512:].astype(BF)
    for n in range(x.shape[0] // KB):
        kv[n, 0] = k[KB * n : KB * n + KB]
        kv[n, 1] = jnp.transpose(v[KB * n : KB * n + KB])
    cache[0] = lax.dot_general(
        k, back, (((1,), (1,)), ((), ())), preferred_element_type=F32
    ).astype(BF)
    cache[1] = v


def qkv_project(x, w, cos, sin):
    rows = x.shape[0]
    n = 512
    return pl.pallas_call(
        qkv_kernel,
        grid=(rows // n,),
        in_specs=[
            pl.BlockSpec((n, 1024), lambda i: (i, 0)),
            vmem(1024, 768),
            pl.BlockSpec((n, 128), lambda i: (i, 0)),
            pl.BlockSpec((n, 128), lambda i: (i, 0)),
        ],
        out_specs=[
            pl.BlockSpec((n, 256), lambda i: (i, 0)),
            pl.BlockSpec((n // KB, 2, KB, 256), lambda i: (i, 0, 0, 0)),
            pl.BlockSpec((2, n, 256), lambda i: (0, i, 0)),
        ],
        out_shape=(
            jax.ShapeDtypeStruct((rows, 256), BF),
            jax.ShapeDtypeStruct((rows // KB, 2, KB, 256), BF),
            jax.ShapeDtypeStruct((2, rows, 256), BF),
        ),
        compiler_params=params(),
        cost_estimate=cost(2 * rows * 1024 * 768, 12 << 20),
        name="qkv",
    )(x, w, cos, sin)


VR = HEAD_DIM + 8


def attend_chunk(at, blocks, qm, kv, kseg, qseg, m_sc, acc):
    size = blocks * KB
    k = kv[pl.ds(at, blocks), 0].reshape(size, 256)
    same = kseg[pl.ds(pl.multiple_of(at * KB, KB), size), 0:1] == qseg[...]
    ones = jnp.ones((8, size), BF)
    scores = []
    for h in range(4):
        s = contract_last(k, qm[h])
        scores.append(jnp.where(same, s, NEG))
    for h in range(4):
        old = m_sc[h]
        new = jnp.maximum(old, jnp.max(scores[h], axis=0, keepdims=True))
        p = jnp.exp(scores[h] - new).astype(BF)
        fade = jnp.exp(old - new)
        m_sc[h] = new
        v = [kv[at + n, 1, HEAD_DIM * h : HEAD_DIM * h + HEAD_DIM, :] for n in range(blocks)]
        v = jnp.concatenate([jnp.concatenate(v, axis=1), ones], axis=0)
        acc[h] = acc[h] * fade + jnp.dot(v, p, preferred_element_type=F32)


def attend_span(table, at, i, *refs):
    start = table[at, i]
    pairs = table[at + 1, i] // 2

    @pl.loop(0, pairs)
    def _(c):
        attend_chunk(start + 2 * c, 2, *refs)

    @pl.when(table[at + 1, i] % 2 == 1)
    def _():
        attend_chunk(start + 2 * pairs, 1, *refs)


def spread_heads(q, qm):
    lane = lax.broadcasted_iota(jnp.int32, (QB, 256), 1)
    for h in range(4):
        qm[h] = jnp.where((lane % 128) // 32 == h, q[...].astype(F32), 0.0).astype(BF)


def own_kernel(table, q, qseg, kv, kseg, acc_out, m_out, qm, m_sc, acc):
    i = pl.program_id(0)
    spread_heads(q, qm)
    m_sc[...] = jnp.full_like(m_sc, NEG)
    acc[...] = jnp.zeros_like(acc)
    attend_span(table, 0, i, qm, kv, kseg, qseg, m_sc, acc)
    acc_out[...] = acc[...]
    m_out[...] = m_sc[...]


def halo_kernel(
    base, table, q, qseg, lkv, lseg, rkv, rseg, last, acc_in, m_in, out, picked, qm, m_sc, acc
):
    i = pl.program_id(0) + base
    spread_heads(q, qm)
    m_sc[...] = m_in[...]
    acc[...] = acc_in[...]
    attend_span(table, 2, i, qm, lkv, lseg, qseg, m_sc, acc)
    attend_span(table, 4, i, qm, rkv, rseg, qseg, m_sc, acc)
    heads = [acc[h, :HEAD_DIM] / acc[h, HEAD_DIM : HEAD_DIM + 1] for h in range(4)]
    mixed = jnp.transpose(jnp.concatenate(heads, axis=0)).astype(BF)
    out[...] = mixed
    slot = lax.broadcasted_iota(jnp.int32, (last.shape[0], QB), 1) + i * QB
    ends_here = jnp.where(last[...] == slot, 1.0, 0.0).astype(BF)

    @pl.when(pl.program_id(0) == 0)
    def _():
        picked[...] = jnp.zeros_like(picked)

    picked[...] += jnp.dot(ends_here, mixed, preferred_element_type=F32)


def attend(part, parts, table, q, qseg, sources, state):
    rows = q.shape[0]
    steps = rows // QB // parts
    base = part * steps
    state_specs = [
        pl.BlockSpec((4, VR, QB), lambda i, *_: (0, 0, i + base)),
        pl.BlockSpec((4, 1, QB), lambda i, *_: (0, 0, i + base)),
    ]
    if state:
        kernel = functools.partial(halo_kernel, base)
        requests = sources[-1].shape[0]
        out_specs = [pl.BlockSpec((QB, 256), lambda i, *_: (i, 0)), vmem(requests, 256)]
        out_shape = (
            jax.ShapeDtypeStruct((rows // parts, 256), BF),
            jax.ShapeDtypeStruct((requests, 256), F32),
        )
    else:
        kernel = own_kernel
        out_specs = state_specs
        out_shape = (
            jax.ShapeDtypeStruct((4, VR, rows), F32),
            jax.ShapeDtypeStruct((4, 1, rows), F32),
        )
    return pl.pallas_call(
        kernel,
        grid_spec=pltpu.PrefetchScalarGridSpec(
            num_scalar_prefetch=1,
            grid=(steps,),
            in_specs=[
                pl.BlockSpec((QB, 256), lambda i, *_: (i + base, 0)),
                pl.BlockSpec((1, QB), lambda i, *_: (0, i + base)),
            ]
            + [vmem(*x.shape) for x in sources]
            + state_specs[: len(state)],
            out_specs=out_specs,
            scratch_shapes=[
                pltpu.VMEM((4, QB, 256), BF),
                pltpu.VMEM((4, 1, QB), F32),
                pltpu.VMEM((4, VR, QB), F32),
            ],
        ),
        out_shape=out_shape,
        compiler_params=params(),
        cost_estimate=cost(12 << 30, 8 << 20, 12 << 20),
        name="attend_halo" if state else "attend_own",
    )(table, q, qseg, *sources, *state)


def contract_last(a, b):
    return lax.dot_general(a, b, (((1,), (1,)), ((), ())), preferred_element_type=F32)


def mlp_kernel(extra, table, m0, m1, m2, m3, o0, o1, o2, o3, h, gain, weights, *refs):
    lasts = refs[: 5 * extra]
    outs = refs[5 * extra :]
    *outs, w, sem = outs
    keep, send = outs[:2]
    count = w.shape[0]
    step = pl.program_id(0)

    def load(ref, n):
        x = ref[...]
        if extra:
            last = lasts[n][...]
            fill = jnp.zeros((x.shape[0] - last.shape[0], x.shape[1]), BF)
            x = jnp.where(step == 0, jnp.concatenate([last, fill], axis=0), x)
        return x

    @pl.when(pl.program_id(0) == 0)
    def _():
        @pl.loop(0, count)
        def _(k):
            pltpu.make_async_copy(weights.at[k], w.at[table[4 + k]], sem).start()

        pltpu.make_async_copy(w, w, sem).wait()

    def rows(at, size, lo, width):
        return w[pl.ds(at, size), :, pl.ds(lo, width)].reshape(8 * size, width)

    n = h.shape[0]
    wide = load(h, 4).astype(F32)
    total = None
    for j, (m, o) in enumerate(((m0, o0), (m1, o1), (m2, o2), (m3, o3))):
        piece = contract_last(load(m, j), o[...])
        total = piece if total is None else total + piece
    first = (wide + total).astype(BF)
    wide = first.astype(F32)
    normed = layer_norm(wide, gain[...]).astype(BF)
    a = jnp.dot(normed, rows(0, count, 0, FFP), preferred_element_type=F32)
    b = jnp.dot(normed, rows(0, count, FFP, FFP), preferred_element_type=F32)
    inner = (0.5 * a * (1.0 + lax.erf(a * (0.5**0.5))) * b).astype(BF)
    mine = jnp.zeros((n, 256), F32)
    for t in range(4):
        mine = jnp.where(table[0] == t, wide[:, 256 * t : 256 * t + 256], mine)

    def down(j):
        return contract_last(inner, rows(table[j] * (count // 4), count // 4, 2 * FFP, FFP))

    kept = jnp.concatenate([down(0) + mine, down(1)], axis=1)
    sent = jnp.concatenate([down(2), down(3)], axis=1).astype(BF)
    keep[...] = kept
    send[...] = sent
    if extra:

        @pl.when(step == 0)
        def _():
            rows = lasts[0].shape[0]
            outs[2][...] = kept[:rows]
            outs[3][...] = sent[:rows]


def mlp(table, mixed, out_w, h, base, gain, weights, lasts=()):
    n = 256
    rows = mixed[0].shape[0]
    count = weights.shape[0]
    extra = 1 if lasts else 0

    def block(width, base=0):
        return pl.BlockSpec((n, width), lambda i, *_: (jnp.maximum(i - extra, 0) + base, 0))

    out_specs = [block(512), block(512)]
    out_shape = [
        jax.ShapeDtypeStruct((rows, 512), F32),
        jax.ShapeDtypeStruct((rows, 512), BF),
    ]
    if lasts:
        held = lasts[0].shape[0]
        out_specs += [vmem(held, 512), vmem(held, 512)]
        out_shape += [
            jax.ShapeDtypeStruct((held, 512), F32),
            jax.ShapeDtypeStruct((held, 512), BF),
        ]
    return pl.pallas_call(
        functools.partial(mlp_kernel, extra),
        grid_spec=pltpu.PrefetchScalarGridSpec(
            num_scalar_prefetch=1,
            grid=(rows // n + extra,),
            in_specs=[block(256)] * 4
            + [vmem(1024, 256)] * 4
            + [block(1024, base), vmem(1, 1024), pl.BlockSpec(memory_space=pl.ANY)]
            + [vmem(*x.shape) for x in lasts],
            out_specs=out_specs,
            scratch_shapes=[pltpu.VMEM((count, 8, REST), BF), pltpu.SemaphoreType.DMA(())],
        ),
        out_shape=tuple(out_shape),
        compiler_params=params(),
        cost_estimate=cost(rows * 1024 * (1024 + 3 * FFP) * 2, 12 << 20, rows * FFP),
        name="mlp",
    )(table, *mixed, *out_w, h, gain.reshape(1, 1024), weights, *lasts)


def turn_bits(n):
    return n % 2 * 2 + n // 2


def swap(x, bit):
    return lax.ppermute(x, "tp", [(i, i ^ bit) for i in range(4)])


def reduce_core(keep, send):
    got = swap(send, 1).astype(F32)
    return keep[:, :256] + got[:, :256], (keep[:, 256:] + got[:, 256:]).astype(BF)


def reduce_far(mine, send):
    return (mine + swap(send, 2).astype(F32)).astype(BF)


def shift(x, by):
    count = lax.axis_size("req")
    return lax.ppermute(x, "req", [(i, i + by) for i in range(count) if 0 <= i + by < count])


def exchange(x, axes):
    return lax.all_to_all(x, axes, split_axis=0, concat_axis=0, tiled=True)


def body(
    hidden_in,
    lengths,
    tenant,
    shard_map,
    wq,
    wk,
    wv,
    wo,
    wi_in,
    wi_gate,
    wo2,
    head,
    attn_gain,
    mlp_gain,
    final_gain,
):
    req_count = lax.axis_size("req")
    tp_count = lax.axis_size("tp")
    count = req_count * tp_count
    req_index = lax.axis_index("req")
    tp_index = lax.axis_index("tp")
    slots, width = hidden_in.shape
    requests = lengths.shape[0]

    four = jnp.arange(4, dtype=jnp.int32)
    place_of = turn_bits(four ^ tp_index)
    first_block, rest_block = prep(req_count, place_of, wq, wk, wv, wo, wi_in, wi_gate, wo2)
    place = jnp.arange(count, dtype=jnp.int32)
    source = jnp.sum(
        jnp.where(shard_map[None, :] == place[:, None], place[None, :], 0), axis=1
    )
    rest_rows = jnp.concatenate(
        [rest_block[0], swap(rest_block[1], 2), swap(rest_block[2], 1), swap(rest_block[3], 3)], axis=0
    )
    hidden, lengths, rest_rows = lax.optimization_barrier((hidden_in, lengths, rest_rows))
    rest = lax.all_gather(rest_rows, "req", axis=0, tiled=True).reshape(count, 8, REST)
    far = jnp.arange(count, dtype=jnp.int32)
    rest_target = shard_map[far // 4 * tp_count + (tp_index ^ turn_bits(far % 4))]

    ends = jnp.cumsum(lengths)
    base = req_index * slots
    index = base - slots + jnp.arange(3 * slots, dtype=jnp.int32)
    segment = jnp.sum((ends[None, :] <= index[:, None]).astype(jnp.int32), axis=1)
    segment = jnp.where((index >= 0) & (index < slots * req_count), segment, -1)
    own = base + jnp.arange(slots, dtype=jnp.int32)
    start_of = jnp.max(jnp.where(ends[None, :] <= own[:, None], ends[None, :], 0), axis=1)
    position = (own - start_of).astype(F32)
    lane = jnp.arange(128, dtype=jnp.int32) % (HEAD_DIM // 2)
    freq = THETA ** (-(2.0 * lane.astype(F32)) / HEAD_DIM)
    angle = position[:, None] * freq[None, :]
    turn = (jnp.cos(angle), jnp.sin(angle))
    begin = base + jnp.arange(slots // QB, dtype=jnp.int32) * QB
    close = begin + QB - 1
    low = jnp.max(jnp.where(ends[None, :] <= begin[:, None], ends[None, :], 0), axis=1) - base
    high = jnp.min(jnp.where(ends[None, :] > close[:, None], ends[None, :], 1 << 30), axis=1) - base

    blocks = slots // KB
    own_0 = jnp.maximum(low, 0) // KB
    own_1 = (jnp.minimum(high, slots) + KB - 1) // KB
    left_0 = (jnp.minimum(low, 0) + slots) // KB
    right_1 = (jnp.maximum(high - slots, 0) + KB - 1) // KB
    table = jnp.stack(
        [own_0, own_1 - own_0, left_0, blocks - left_0, jnp.zeros_like(right_1), right_1]
    )
    segs = segment.reshape(3, slots, 1)
    qseg = segment[slots : 2 * slots].reshape(1, slots)

    normed = norm(hidden, attn_gain)
    first_all = exchange(first_block.reshape(count, 8, width), BOTH)
    first_w = first_all[source].reshape(width, width)
    query, kv, cache = qkv_project(normed, first_w, *turn)
    left = shift(kv, 1)
    right = shift(kv, -1)
    out_w, kv = lax.optimization_barrier((first_w[:, 768:], kv))
    out_far, out_near = swap(out_w, 2), swap(out_w, 1)
    parts = 2
    state = attend(0, 1, table, query, qseg, (kv, segs[1]), ())
    out_far, out_near, state = lax.optimization_barrier((out_far, out_near, state))
    out_w = (out_w, out_far, out_near, swap(out_far, 1))
    last_slot = (ends - 1 - base).reshape(requests, 1)
    halo = (left, segs[0], right, segs[2], last_slot)
    mixed, picked = zip(
        *[attend(part, parts, table, query, qseg, halo, state) for part in range(parts)]
    )

    holds = (last_slot >= 0) & (last_slot < slots)
    last_in = jnp.where(holds, hidden[jnp.clip(last_slot[:, 0], 0, slots - 1)], 0)
    last_mixed = sum(picked).astype(BF)
    last_far = swap(last_mixed, 2)
    lasts = (last_mixed, last_far, swap(last_mixed, 1), swap(last_far, 1), last_in)

    order = jnp.concatenate([tp_index ^ turn_bits(four), rest_target])
    steps = slots // parts // 256

    def feed(part, pieces, *lasts):
        return mlp(
            order, pieces, out_w, hidden_in, part * steps, mlp_gain, rest, *lasts
        )

    far = [swap(m, 2) for m in mixed]
    near = [swap(m, 1) for m in mixed]
    far[0], _ = lax.optimization_barrier((far[0], mixed[1]))
    keep, send, last_keep, last_send = feed(
        0, (mixed[0], far[0], near[0], swap(far[0], 1)), lasts
    )
    last_keep, last_send, keep, send, far[1] = lax.optimization_barrier(
        (last_keep, last_send, keep, send, far[1])
    )
    last_piece = swap(far[1], 1)
    last_mine = reduce_far(*reduce_core(last_keep, last_send))
    pair, last_mine, last_piece, piece = lax.optimization_barrier(
        (reduce_core(keep, send), last_mine, last_piece, mixed[1])
    )
    top = reduce_far(*pair)
    each = requests // req_count
    taken = exchange(last_mine.reshape(req_count, each, 256), "req").astype(F32).sum(axis=0)
    keep, send = feed(1, (piece, far[1], near[1], last_piece))
    taken, keep, send, top = lax.optimization_barrier((taken, keep, send, top))
    spread = exchange(jnp.broadcast_to(taken.astype(BF)[None], (count, each, 256)), BOTH)
    hidden_out = jnp.concatenate([top, reduce_far(*reduce_core(keep, send))], axis=0)
    last = (
        spread.reshape(req_count, tp_count, each, 256)
        .transpose(0, 2, 1, 3)
        .reshape(requests, width)
        .astype(F32)
    )
    last_rms = jnp.sqrt(jnp.mean(last * last, axis=-1))
    choose = (tenant[:, None] == jnp.arange(final_gain.shape[0], dtype=jnp.int32)[None, :]).astype(
        F32
    )
    gain_rows = jnp.dot(
        choose, final_gain, precision=lax.Precision.HIGHEST, preferred_element_type=F32
    )
    final = layer_norm(last, gain_rows).astype(BF)
    logits = contract_last(final, head.astype(BF))
    top = jnp.max(logits, axis=-1)
    tops = exchange(jnp.broadcast_to(top[None], (count, requests)), BOTH)
    top_logit = jnp.max(tops, axis=0)
    return (hidden_out, cache, last_rms, top_logit)


def solution(mesh):
    rows = P(BOTH, None)
    placed = (P("req", None), P(), P(), P()) + (rows,) * 8 + (P(), P(), P())
    return jax.shard_map(
        body,
        mesh=mesh,
        in_specs=placed,
        out_specs=(P("req", "tp"), P(None, "req", "tp"), P(), P()),
        check_vma=False,
    )
```

```python
import functools

import jax
import jax.numpy as jnp
from jax import lax
from jax.experimental import pallas as pl
from jax.experimental.pallas import tpu as pltpu
from jax.sharding import PartitionSpec as P

HEADS = 16
HEAD_DIM = 64
THETA = 160000.0
EPS = 1e-05
BF = jnp.bfloat16
F32 = jnp.float32
BOTH = ("req", "tp")
NEG = -1e30
FFP = 768
REST = 3 * FFP
QB = 256
KB = 256


def vmem(*shape):
    return pl.BlockSpec(shape, lambda *_: (0,) * len(shape))


def params():
    return pltpu.CompilerParams(vmem_limit_bytes=60 * 1024 * 1024)


def cost(flops, moved, transcendentals=0):
    return pl.CostEstimate(flops=flops, bytes_accessed=moved, transcendentals=transcendentals)


def prep_kernel(order, wq, wk, wv, wo, wi, wg, w2, first, *rest):
    row = lax.broadcasted_iota(jnp.int32, (256, 256), 0)
    col = lax.broadcasted_iota(jnp.int32, (256, 256), 1)
    source = (col % 128) // 32 * 64 + col // 128 * 32 + col % 32
    turn = jnp.where(row == source, 1.0, 0.0).astype(BF)
    trow = lax.broadcasted_iota(jnp.int32, (64, 128), 0)
    tcol = lax.broadcasted_iota(jnp.int32, (64, 128), 1)
    for t in range(4):
        at = slice(256 * t, 256 * t + 256)
        q, k = (
            jnp.dot(w[:, at].astype(BF), turn, preferred_element_type=F32).astype(BF)
            for w in (wq, wk)
        )
        mine = jnp.concatenate([q, k, wv[:, at].astype(BF), wo[:, at].astype(BF)], axis=1)
        for r in range(first.shape[0]):
            first[r, t] = mine
    for piece, out in enumerate(rest):
        t = order[piece]
        pick = jnp.where((trow == tcol + 16 * t) & (tcol < 16), 1.0, 0.0).astype(BF)
        for n, w in enumerate((wi, wg, w2)):
            main = pl.ds(pl.multiple_of(640 * t, 128), 640)
            out[:, FFP * n : FFP * n + 640] = w[:, main].astype(BF)
            out[:, FFP * n + 640 : FFP * n + 768] = jnp.dot(
                w[:, 2560:2624].astype(BF), pick, preferred_element_type=F32
            ).astype(BF)


def prep(req_count, order, *weights):
    return pl.pallas_call(
        prep_kernel,
        in_specs=[pl.BlockSpec(memory_space=pltpu.SMEM)] + [vmem(*w.shape) for w in weights],
        out_shape=(
            jax.ShapeDtypeStruct((req_count, 4, 8, 1024), BF),
        )
        + (jax.ShapeDtypeStruct((8, REST), BF),) * 4,
        compiler_params=params(),
        name="prep",
    )(order, *weights)


def layer_norm(values, gain):
    center = jnp.mean(values, axis=-1, keepdims=True)
    spread = jnp.mean(values * values, axis=-1, keepdims=True) - center * center
    return (values - center) * lax.rsqrt(spread + EPS) * gain


def norm_kernel(h, gain, out):
    out[...] = layer_norm(h[...].astype(F32), gain[...]).astype(BF)


def norm(h, gain):
    rows = h.shape[0]
    return pl.pallas_call(
        norm_kernel,
        grid=(rows // 512,),
        in_specs=[pl.BlockSpec((512, 1024), lambda i: (i, 0)), vmem(1, 1024)],
        out_specs=pl.BlockSpec((512, 1024), lambda i: (i, 0)),
        out_shape=jax.ShapeDtypeStruct((rows, 1024), BF),
        compiler_params=params(),
        cost_estimate=cost(1 << 24, 1 << 23),
        name="norm",
    )(h, gain.reshape(1, 1024))


def qkv_kernel(x, w, cos, sin, q, kv, cache):
    row = lax.broadcasted_iota(jnp.int32, (256, 256), 0)
    col = lax.broadcasted_iota(jnp.int32, (256, 256), 1)
    source = (col % 128) // 32 * 64 + col // 128 * 32 + col % 32
    back = jnp.where(source == row, 1.0, 0.0).astype(BF)
    y = jnp.dot(x[...], w[...], preferred_element_type=F32)
    c = cos[...]
    s = sin[...]

    def turned(a, b):
        return jnp.concatenate([a * c - b * s, b * c + a * s], axis=1)

    q[...] = (turned(y[:, :128], y[:, 128:256]).astype(BF).astype(F32) * 0.125).astype(BF)
    k = turned(y[:, 256:384], y[:, 384:512]).astype(BF)
    v = y[:, 512:].astype(BF)
    for n in range(x.shape[0] // KB):
        kv[n, 0] = k[KB * n : KB * n + KB]
        kv[n, 1] = jnp.transpose(v[KB * n : KB * n + KB])
    cache[0] = lax.dot_general(
        k, back, (((1,), (1,)), ((), ())), preferred_element_type=F32
    ).astype(BF)
    cache[1] = v


def qkv_project(x, w, cos, sin):
    rows = x.shape[0]
    n = 512
    return pl.pallas_call(
        qkv_kernel,
        grid=(rows // n,),
        in_specs=[
            pl.BlockSpec((n, 1024), lambda i: (i, 0)),
            vmem(1024, 768),
            pl.BlockSpec((n, 128), lambda i: (i, 0)),
            pl.BlockSpec((n, 128), lambda i: (i, 0)),
        ],
        out_specs=[
            pl.BlockSpec((n, 256), lambda i: (i, 0)),
            pl.BlockSpec((n // KB, 2, KB, 256), lambda i: (i, 0, 0, 0)),
            pl.BlockSpec((2, n, 256), lambda i: (0, i, 0)),
        ],
        out_shape=(
            jax.ShapeDtypeStruct((rows, 256), BF),
            jax.ShapeDtypeStruct((rows // KB, 2, KB, 256), BF),
            jax.ShapeDtypeStruct((2, rows, 256), BF),
        ),
        compiler_params=params(),
        cost_estimate=cost(2 * rows * 1024 * 768, 12 << 20),
        name="qkv",
    )(x, w, cos, sin)


VR = HEAD_DIM + 8


def attend_chunk(at, blocks, qm, kv, kseg, qseg, m_sc, acc):
    size = blocks * KB
    k = kv[pl.ds(at, blocks), 0].reshape(size, 256)
    same = kseg[pl.ds(pl.multiple_of(at * KB, KB), size), 0:1] == qseg[...]
    ones = jnp.ones((8, size), BF)
    scores = []
    for h in range(4):
        s = contract_last(k, qm[h])
        scores.append(jnp.where(same, s, NEG))
    for h in range(4):
        old = m_sc[h]
        new = jnp.maximum(old, jnp.max(scores[h], axis=0, keepdims=True))
        p = jnp.exp(scores[h] - new).astype(BF)
        fade = jnp.exp(old - new)
        m_sc[h] = new
        v = [kv[at + n, 1, HEAD_DIM * h : HEAD_DIM * h + HEAD_DIM, :] for n in range(blocks)]
        v = jnp.concatenate([jnp.concatenate(v, axis=1), ones], axis=0)
        acc[h] = acc[h] * fade + jnp.dot(v, p, preferred_element_type=F32)


def attend_span(table, at, i, *refs):
    start = table[at, i]
    pairs = table[at + 1, i] // 2

    @pl.loop(0, pairs)
    def _(c):
        attend_chunk(start + 2 * c, 2, *refs)

    @pl.when(table[at + 1, i] % 2 == 1)
    def _():
        attend_chunk(start + 2 * pairs, 1, *refs)


def spread_heads(q, qm):
    lane = lax.broadcasted_iota(jnp.int32, (QB, 256), 1)
    for h in range(4):
        qm[h] = jnp.where((lane % 128) // 32 == h, q[...].astype(F32), 0.0).astype(BF)


def own_kernel(table, q, qseg, kv, kseg, acc_out, m_out, qm, m_sc, acc):
    i = pl.program_id(0)
    spread_heads(q, qm)
    m_sc[...] = jnp.full_like(m_sc, NEG)
    acc[...] = jnp.zeros_like(acc)
    attend_span(table, 0, i, qm, kv, kseg, qseg, m_sc, acc)
    acc_out[...] = acc[...]
    m_out[...] = m_sc[...]


def halo_kernel(
    base, table, q, qseg, lkv, lseg, rkv, rseg, last, acc_in, m_in, out, picked, qm, m_sc, acc
):
    i = pl.program_id(0) + base
    spread_heads(q, qm)
    m_sc[...] = m_in[...]
    acc[...] = acc_in[...]
    attend_span(table, 2, i, qm, lkv, lseg, qseg, m_sc, acc)
    attend_span(table, 4, i, qm, rkv, rseg, qseg, m_sc, acc)
    heads = [acc[h, :HEAD_DIM] / acc[h, HEAD_DIM : HEAD_DIM + 1] for h in range(4)]
    mixed = jnp.transpose(jnp.concatenate(heads, axis=0)).astype(BF)
    out[...] = mixed
    slot = lax.broadcasted_iota(jnp.int32, (last.shape[0], QB), 1) + i * QB
    ends_here = jnp.where(last[...] == slot, 1.0, 0.0).astype(BF)

    @pl.when(pl.program_id(0) == 0)
    def _():
        picked[...] = jnp.zeros_like(picked)

    picked[...] += jnp.dot(ends_here, mixed, preferred_element_type=F32)


def attend(part, parts, table, q, qseg, sources, state):
    rows = q.shape[0]
    steps = rows // QB // parts
    base = part * steps
    state_specs = [
        pl.BlockSpec((4, VR, QB), lambda i, *_: (0, 0, i + base)),
        pl.BlockSpec((4, 1, QB), lambda i, *_: (0, 0, i + base)),
    ]
    if state:
        kernel = functools.partial(halo_kernel, base)
        requests = sources[-1].shape[0]
        out_specs = [pl.BlockSpec((QB, 256), lambda i, *_: (i, 0)), vmem(requests, 256)]
        out_shape = (
            jax.ShapeDtypeStruct((rows // parts, 256), BF),
            jax.ShapeDtypeStruct((requests, 256), F32),
        )
    else:
        kernel = own_kernel
        out_specs = state_specs
        out_shape = (
            jax.ShapeDtypeStruct((4, VR, rows), F32),
            jax.ShapeDtypeStruct((4, 1, rows), F32),
        )
    return pl.pallas_call(
        kernel,
        grid_spec=pltpu.PrefetchScalarGridSpec(
            num_scalar_prefetch=1,
            grid=(steps,),
            in_specs=[
                pl.BlockSpec((QB, 256), lambda i, *_: (i + base, 0)),
                pl.BlockSpec((1, QB), lambda i, *_: (0, i + base)),
            ]
            + [vmem(*x.shape) for x in sources]
            + state_specs[: len(state)],
            out_specs=out_specs,
            scratch_shapes=[
                pltpu.VMEM((4, QB, 256), BF),
                pltpu.VMEM((4, 1, QB), F32),
                pltpu.VMEM((4, VR, QB), F32),
            ],
        ),
        out_shape=out_shape,
        compiler_params=params(),
        cost_estimate=cost(12 << 30, 8 << 20, 12 << 20),
        name="attend_halo" if state else "attend_own",
    )(table, q, qseg, *sources, *state)


def contract_last(a, b):
    return lax.dot_general(a, b, (((1,), (1,)), ((), ())), preferred_element_type=F32)


def mlp_kernel(extra, table, m0, m1, m2, m3, o0, o1, o2, o3, h, gain, weights, *refs):
    lasts = refs[: 5 * extra]
    outs = refs[5 * extra :]
    *outs, w, sem = outs
    keep, send = outs[:2]
    count = w.shape[0]
    step = pl.program_id(0)

    def load(ref, n):
        x = ref[...]
        if extra:
            last = lasts[n][...]
            fill = jnp.zeros((x.shape[0] - last.shape[0], x.shape[1]), BF)
            x = jnp.where(step == 0, jnp.concatenate([last, fill], axis=0), x)
        return x

    @pl.when(pl.program_id(0) == 0)
    def _():
        @pl.loop(0, count)
        def _(k):
            pltpu.make_async_copy(weights.at[k], w.at[table[4 + k]], sem).start()

    def rows(at, size, lo, width):
        return w[pl.ds(at, size), :, pl.ds(lo, width)].reshape(8 * size, width)

    n = h.shape[0]
    wide = load(h, 4).astype(F32)
    total = None
    for j, (m, o) in enumerate(((m0, o0), (m1, o1), (m2, o2), (m3, o3))):
        piece = contract_last(load(m, j), o[...])
        total = piece if total is None else total + piece
    first = (wide + total).astype(BF)
    wide = first.astype(F32)
    normed = layer_norm(wide, gain[...]).astype(BF)

    @pl.when(step == 0)
    def _():
        pltpu.make_async_copy(w, w, sem).wait()

    a = jnp.dot(normed, rows(0, count, 0, FFP), preferred_element_type=F32)
    b = jnp.dot(normed, rows(0, count, FFP, FFP), preferred_element_type=F32)
    inner = (0.5 * a * (1.0 + lax.erf(a * (0.5**0.5))) * b).astype(BF)
    mine = jnp.zeros((n, 256), F32)
    for t in range(4):
        mine = jnp.where(table[0] == t, wide[:, 256 * t : 256 * t + 256], mine)

    def down(j):
        return contract_last(inner, rows(table[j] * (count // 4), count // 4, 2 * FFP, FFP))

    kept = jnp.concatenate([down(0) + mine, down(1)], axis=1)
    sent = jnp.concatenate([down(2), down(3)], axis=1)
    keep[...] = kept
    send[...] = sent.astype(BF)
    if extra:

        @pl.when(step == 0)
        def _():
            held = lasts[0].shape[0]
            for j, x in enumerate((kept, sent)):
                for n in range(2):
                    at = pl.ds(pl.multiple_of(256 * table[2 * j + n], 128), 256)
                    outs[2][:, at] = x[:held, 256 * n : 256 * n + 256]


def mlp(table, mixed, out_w, h, base, gain, weights, lasts=()):
    n = 256
    rows = mixed[0].shape[0]
    count = weights.shape[0]
    extra = 1 if lasts else 0

    def block(width, base=0):
        return pl.BlockSpec((n, width), lambda i, *_: (jnp.maximum(i - extra, 0) + base, 0))

    out_specs = [block(512), block(512)]
    out_shape = [
        jax.ShapeDtypeStruct((rows, 512), F32),
        jax.ShapeDtypeStruct((rows, 512), BF),
    ]
    if lasts:
        held = lasts[0].shape[0]
        out_specs.append(vmem(held, 1024))
        out_shape.append(jax.ShapeDtypeStruct((held, 1024), F32))
    return pl.pallas_call(
        functools.partial(mlp_kernel, extra),
        grid_spec=pltpu.PrefetchScalarGridSpec(
            num_scalar_prefetch=1,
            grid=(rows // n + extra,),
            in_specs=[block(256)] * 4
            + [vmem(1024, 256)] * 4
            + [block(1024, base), vmem(1, 1024), pl.BlockSpec(memory_space=pl.ANY)]
            + [vmem(*x.shape) for x in lasts],
            out_specs=out_specs,
            scratch_shapes=[pltpu.VMEM((count, 8, REST), BF), pltpu.SemaphoreType.DMA(())],
        ),
        out_shape=tuple(out_shape),
        compiler_params=params(),
        cost_estimate=cost(rows * 1024 * (1024 + 3 * FFP) * 2, 12 << 20, rows * FFP),
        name="mlp",
    )(table, *mixed, *out_w, h, gain.reshape(1, 1024), weights, *lasts)


def turn_bits(n):
    return n % 2 * 2 + n // 2


def swap(x, bit):
    return lax.ppermute(x, "tp", [(i, i ^ bit) for i in range(4)])


def reduce_core(keep, send):
    got = swap(send, 1).astype(F32)
    return keep[:, :256] + got[:, :256], (keep[:, 256:] + got[:, 256:]).astype(BF)


def reduce_far(mine, send):
    return (mine + swap(send, 2).astype(F32)).astype(BF)


def shift(x, by):
    count = lax.axis_size("req")
    return lax.ppermute(x, "req", [(i, i + by) for i in range(count) if 0 <= i + by < count])


def exchange(x, axes):
    return lax.all_to_all(x, axes, split_axis=0, concat_axis=0, tiled=True)


def body(
    hidden_in,
    lengths,
    tenant,
    shard_map,
    wq,
    wk,
    wv,
    wo,
    wi_in,
    wi_gate,
    wo2,
    head,
    attn_gain,
    mlp_gain,
    final_gain,
):
    req_count = lax.axis_size("req")
    tp_count = lax.axis_size("tp")
    count = req_count * tp_count
    req_index = lax.axis_index("req")
    tp_index = lax.axis_index("tp")
    slots, width = hidden_in.shape
    requests = lengths.shape[0]

    four = jnp.arange(4, dtype=jnp.int32)
    near_first = tp_index ^ turn_bits(four)
    first_block, *rest_block = prep(req_count, near_first, wq, wk, wv, wo, wi_in, wi_gate, wo2)
    place = jnp.arange(count, dtype=jnp.int32)
    source = jnp.sum(
        jnp.where(shard_map[None, :] == place[:, None], place[None, :], 0), axis=1
    )
    rest_rows = jnp.concatenate(
        [rest_block[0], swap(rest_block[1], 2), swap(rest_block[2], 1), swap(rest_block[3], 3)], axis=0
    )
    hidden, lengths, rest_rows = lax.optimization_barrier((hidden_in, lengths, rest_rows))
    rest = lax.all_gather(rest_rows, "req", axis=0, tiled=True).reshape(count, 8, REST)
    far = jnp.arange(count, dtype=jnp.int32)
    rest_target = shard_map[far // 4 * tp_count + (tp_index ^ turn_bits(far % 4))]

    ends = jnp.cumsum(lengths)
    base = req_index * slots
    index = base - slots + jnp.arange(3 * slots, dtype=jnp.int32)
    segment = jnp.sum((ends[None, :] <= index[:, None]).astype(jnp.int32), axis=1)
    segment = jnp.where((index >= 0) & (index < slots * req_count), segment, -1)
    own = base + jnp.arange(slots, dtype=jnp.int32)
    start_of = jnp.max(jnp.where(ends[None, :] <= own[:, None], ends[None, :], 0), axis=1)
    position = (own - start_of).astype(F32)
    lane = jnp.arange(128, dtype=jnp.int32) % (HEAD_DIM // 2)
    freq = THETA ** (-(2.0 * lane.astype(F32)) / HEAD_DIM)
    angle = position[:, None] * freq[None, :]
    turn = (jnp.cos(angle), jnp.sin(angle))
    begin = base + jnp.arange(slots // QB, dtype=jnp.int32) * QB
    close = begin + QB - 1
    low = jnp.max(jnp.where(ends[None, :] <= begin[:, None], ends[None, :], 0), axis=1) - base
    high = jnp.min(jnp.where(ends[None, :] > close[:, None], ends[None, :], 1 << 30), axis=1) - base

    blocks = slots // KB
    own_0 = jnp.maximum(low, 0) // KB
    own_1 = (jnp.minimum(high, slots) + KB - 1) // KB
    left_0 = (jnp.minimum(low, 0) + slots) // KB
    right_1 = (jnp.maximum(high - slots, 0) + KB - 1) // KB
    table = jnp.stack(
        [own_0, own_1 - own_0, left_0, blocks - left_0, jnp.zeros_like(right_1), right_1]
    )
    segs = segment.reshape(3, slots, 1)
    qseg = segment[slots : 2 * slots].reshape(1, slots)

    normed = norm(hidden, attn_gain)
    first_all = exchange(first_block.reshape(count, 8, width), BOTH)
    first_w = first_all[source].reshape(width, width)
    query, kv, cache = qkv_project(normed, first_w, *turn)
    left = shift(kv, 1)
    right = shift(kv, -1)
    out_w, kv = lax.optimization_barrier((first_w[:, 768:], kv))
    out_far, out_near = swap(out_w, 2), swap(out_w, 1)
    parts = 2
    state = attend(0, 1, table, query, qseg, (kv, segs[1]), ())
    out_far, out_near, state = lax.optimization_barrier((out_far, out_near, state))
    out_w = (out_w, out_far, out_near, swap(out_far, 1))
    last_slot = (ends - 1 - base).reshape(requests, 1)
    halo = (left, segs[0], right, segs[2], last_slot)
    mixed, picked = zip(
        *[attend(part, parts, table, query, qseg, halo, state) for part in range(parts)]
    )

    holds = (last_slot >= 0) & (last_slot < slots)
    last_in = jnp.where(holds, hidden[jnp.clip(last_slot[:, 0], 0, slots - 1)], 0)
    last_mixed = sum(picked).astype(BF)
    last_far = swap(last_mixed, 2)
    lasts = (last_mixed, last_far, swap(last_mixed, 1), swap(last_far, 1), last_in)

    order = jnp.concatenate([near_first, rest_target])
    steps = slots // parts // 256

    def feed(part, pieces, *lasts):
        return mlp(
            order, pieces, out_w, hidden_in, part * steps, mlp_gain, rest, *lasts
        )

    far = [swap(m, 2) for m in mixed]
    near = [swap(m, 1) for m in mixed]
    far[0], _ = lax.optimization_barrier((far[0], mixed[1]))
    keep, send, last_part = feed(0, (mixed[0], far[0], near[0], swap(far[0], 1)), lasts)
    keep, send, far[1] = lax.optimization_barrier((keep, send, far[1]))
    last_piece = swap(far[1], 1)
    each = requests // req_count
    last_part = last_part.reshape(req_count, each, tp_count, 256).transpose(0, 2, 1, 3)
    pair, last_part, last_piece, piece = lax.optimization_barrier(
        (reduce_core(keep, send), last_part, last_piece, mixed[1])
    )
    top = reduce_far(*pair)
    taken = exchange(last_part.reshape(count, each, 256), BOTH).sum(axis=0)
    keep, send = feed(1, (piece, far[1], near[1], last_piece))
    taken, keep, send, top = lax.optimization_barrier((taken, keep, send, top))
    spread = exchange(jnp.broadcast_to(taken.astype(BF)[None], (count, each, 256)), BOTH)
    hidden_out = jnp.concatenate([top, reduce_far(*reduce_core(keep, send))], axis=0)
    last = (
        spread.reshape(req_count, tp_count, each, 256)
        .transpose(0, 2, 1, 3)
        .reshape(requests, width)
        .astype(F32)
    )
    last_rms = jnp.sqrt(jnp.mean(last * last, axis=-1))
    choose = (tenant[:, None] == jnp.arange(final_gain.shape[0], dtype=jnp.int32)[None, :]).astype(
        F32
    )
    gain_rows = jnp.dot(
        choose, final_gain, precision=lax.Precision.HIGHEST, preferred_element_type=F32
    )
    final = layer_norm(last, gain_rows).astype(BF)
    logits = contract_last(final, head.astype(BF))
    top = jnp.max(logits, axis=-1)
    tops = exchange(jnp.broadcast_to(top[None], (count, requests)), BOTH)
    top_logit = jnp.max(tops, axis=0)
    return (hidden_out, cache, last_rms, top_logit)


def solution(mesh):
    rows = P(BOTH, None)
    placed = (P("req", None), P(), P(), P()) + (rows,) * 8 + (P(), P(), P())
    return jax.shard_map(
        body,
        mesh=mesh,
        in_specs=placed,
        out_specs=(P("req", "tp"), P(None, "req", "tp"), P(), P()),
        check_vma=False,
    )
```

```python
import functools

import jax
import jax.numpy as jnp
from jax import lax
from jax.experimental import pallas as pl
from jax.experimental.pallas import tpu as pltpu
from jax.sharding import PartitionSpec as P

HEADS = 16
HEAD_DIM = 64
THETA = 160000.0
EPS = 1e-05
BF = jnp.bfloat16
F32 = jnp.float32
BOTH = ("req", "tp")
NEG = -1e30
FFP = 768
REST = 3 * FFP
QB = 256
KB = 256


def vmem(*shape):
    return pl.BlockSpec(shape, lambda *_: (0,) * len(shape))


def params():
    return pltpu.CompilerParams(vmem_limit_bytes=60 * 1024 * 1024)


def cost(flops, moved, transcendentals=0):
    return pl.CostEstimate(flops=flops, bytes_accessed=moved, transcendentals=transcendentals)


def prep_kernel(order, wq, wk, wv, wo, wi, wg, w2, first, *rest):
    row = lax.broadcasted_iota(jnp.int32, (256, 256), 0)
    col = lax.broadcasted_iota(jnp.int32, (256, 256), 1)
    source = (col % 128) // 32 * 64 + col // 128 * 32 + col % 32
    turn = jnp.where(row == source, 1.0, 0.0).astype(BF)
    trow = lax.broadcasted_iota(jnp.int32, (64, 128), 0)
    tcol = lax.broadcasted_iota(jnp.int32, (64, 128), 1)
    for t in range(4):
        at = slice(256 * t, 256 * t + 256)
        q, k = (
            jnp.dot(w[:, at].astype(BF), turn, preferred_element_type=F32).astype(BF)
            for w in (wq, wk)
        )
        mine = jnp.concatenate([q, k, wv[:, at].astype(BF), wo[:, at].astype(BF)], axis=1)
        for r in range(first.shape[0]):
            first[r, t] = mine
    for piece, out in enumerate(rest):
        t = order[piece]
        pick = jnp.where((trow == tcol + 16 * t) & (tcol < 16), 1.0, 0.0).astype(BF)
        for n, w in enumerate((wi, wg, w2)):
            main = pl.ds(pl.multiple_of(640 * t, 128), 640)
            out[:, FFP * n : FFP * n + 640] = w[:, main].astype(BF)
            out[:, FFP * n + 640 : FFP * n + 768] = jnp.dot(
                w[:, 2560:2624].astype(BF), pick, preferred_element_type=F32
            ).astype(BF)


def prep(req_count, order, *weights):
    return pl.pallas_call(
        prep_kernel,
        in_specs=[pl.BlockSpec(memory_space=pltpu.SMEM)] + [vmem(*w.shape) for w in weights],
        out_shape=(
            jax.ShapeDtypeStruct((req_count, 4, 8, 1024), BF),
        )
        + (jax.ShapeDtypeStruct((8, REST), BF),) * 4,
        compiler_params=params(),
        name="prep",
    )(order, *weights)


def layer_norm(values, gain):
    center = jnp.mean(values, axis=-1, keepdims=True)
    spread = jnp.mean(values * values, axis=-1, keepdims=True) - center * center
    return (values - center) * lax.rsqrt(spread + EPS) * gain


def norm_kernel(h, gain, out):
    out[...] = layer_norm(h[...].astype(F32), gain[...]).astype(BF)


def norm(h, gain):
    rows = h.shape[0]
    return pl.pallas_call(
        norm_kernel,
        grid=(rows // 512,),
        in_specs=[pl.BlockSpec((512, 1024), lambda i: (i, 0)), vmem(1, 1024)],
        out_specs=pl.BlockSpec((512, 1024), lambda i: (i, 0)),
        out_shape=jax.ShapeDtypeStruct((rows, 1024), BF),
        compiler_params=params(),
        cost_estimate=cost(1 << 24, 1 << 23),
        name="norm",
    )(h, gain.reshape(1, 1024))


def qkv_kernel(x, w, cos, sin, q, kv, cache):
    row = lax.broadcasted_iota(jnp.int32, (256, 256), 0)
    col = lax.broadcasted_iota(jnp.int32, (256, 256), 1)
    source = (col % 128) // 32 * 64 + col // 128 * 32 + col % 32
    back = jnp.where(source == row, 1.0, 0.0).astype(BF)
    y = jnp.dot(x[...], w[...], preferred_element_type=F32)
    c = cos[...]
    s = sin[...]

    def turned(a, b):
        return jnp.concatenate([a * c - b * s, b * c + a * s], axis=1)

    q[...] = (turned(y[:, :128], y[:, 128:256]).astype(BF).astype(F32) * 0.125).astype(BF)
    k = turned(y[:, 256:384], y[:, 384:512]).astype(BF)
    v = y[:, 512:].astype(BF)
    for n in range(x.shape[0] // KB):
        kv[n, 0] = k[KB * n : KB * n + KB]
        kv[n, 1] = jnp.transpose(v[KB * n : KB * n + KB])
    cache[0] = lax.dot_general(
        k, back, (((1,), (1,)), ((), ())), preferred_element_type=F32
    ).astype(BF)
    cache[1] = v


def qkv_project(x, w, cos, sin):
    rows = x.shape[0]
    n = 512
    return pl.pallas_call(
        qkv_kernel,
        grid=(rows // n,),
        in_specs=[
            pl.BlockSpec((n, 1024), lambda i: (i, 0)),
            vmem(1024, 768),
            pl.BlockSpec((n, 128), lambda i: (i, 0)),
            pl.BlockSpec((n, 128), lambda i: (i, 0)),
        ],
        out_specs=[
            pl.BlockSpec((n, 256), lambda i: (i, 0)),
            pl.BlockSpec((n // KB, 2, KB, 256), lambda i: (i, 0, 0, 0)),
            pl.BlockSpec((2, n, 256), lambda i: (0, i, 0)),
        ],
        out_shape=(
            jax.ShapeDtypeStruct((rows, 256), BF),
            jax.ShapeDtypeStruct((rows // KB, 2, KB, 256), BF),
            jax.ShapeDtypeStruct((2, rows, 256), BF),
        ),
        compiler_params=params(),
        cost_estimate=cost(2 * rows * 1024 * 768, 12 << 20),
        name="qkv",
    )(x, w, cos, sin)


VR = HEAD_DIM + 8


def attend_chunk(at, blocks, qm, kv, kseg, qseg, m_sc, acc):
    size = blocks * KB
    k = kv[pl.ds(at, blocks), 0].reshape(size, 256)
    same = kseg[pl.ds(pl.multiple_of(at * KB, KB), size), 0:1] == qseg[...]
    ones = jnp.ones((8, size), BF)
    scores = []
    for h in range(4):
        s = contract_last(k, qm[h])
        scores.append(jnp.where(same, s, NEG))
    for h in range(4):
        old = m_sc[h]
        new = jnp.maximum(old, jnp.max(scores[h], axis=0, keepdims=True))
        p = jnp.exp(scores[h] - new).astype(BF)
        fade = jnp.exp(old - new)
        m_sc[h] = new
        v = [kv[at + n, 1, HEAD_DIM * h : HEAD_DIM * h + HEAD_DIM, :] for n in range(blocks)]
        v = jnp.concatenate([jnp.concatenate(v, axis=1), ones], axis=0)
        acc[h] = acc[h] * fade + jnp.dot(v, p, preferred_element_type=F32)


def attend_span(table, at, i, *refs):
    start = table[at, i]
    pairs = table[at + 1, i] // 2

    @pl.loop(0, pairs)
    def _(c):
        attend_chunk(start + 2 * c, 2, *refs)

    @pl.when(table[at + 1, i] % 2 == 1)
    def _():
        attend_chunk(start + 2 * pairs, 1, *refs)


def spread_heads(q, qm):
    lane = lax.broadcasted_iota(jnp.int32, (QB, 256), 1)
    for h in range(4):
        qm[h] = jnp.where((lane % 128) // 32 == h, q[...].astype(F32), 0.0).astype(BF)


def own_kernel(table, q, qseg, kv, kseg, acc_out, m_out, qm, m_sc, acc):
    i = pl.program_id(0)
    spread_heads(q, qm)
    m_sc[...] = jnp.full_like(m_sc, NEG)
    acc[...] = jnp.zeros_like(acc)
    attend_span(table, 0, i, qm, kv, kseg, qseg, m_sc, acc)
    acc_out[...] = acc[...]
    m_out[...] = m_sc[...]


def halo_kernel(
    base, table, q, qseg, lkv, lseg, rkv, rseg, last, acc_in, m_in, out, picked, qm, m_sc, acc
):
    i = pl.program_id(0) + base
    spread_heads(q, qm)
    m_sc[...] = m_in[...]
    acc[...] = acc_in[...]
    attend_span(table, 2, i, qm, lkv, lseg, qseg, m_sc, acc)
    attend_span(table, 4, i, qm, rkv, rseg, qseg, m_sc, acc)
    heads = [acc[h, :HEAD_DIM] / acc[h, HEAD_DIM : HEAD_DIM + 1] for h in range(4)]
    mixed = jnp.transpose(jnp.concatenate(heads, axis=0)).astype(BF)
    out[...] = mixed
    slot = lax.broadcasted_iota(jnp.int32, (last.shape[0], QB), 1) + i * QB
    ends_here = jnp.where(last[...] == slot, 1.0, 0.0).astype(BF)

    @pl.when(pl.program_id(0) == 0)
    def _():
        picked[...] = jnp.zeros_like(picked)

    picked[...] += jnp.dot(ends_here, mixed, preferred_element_type=F32)


def attend(part, parts, table, q, qseg, sources, state):
    rows = q.shape[0]
    steps = rows // QB // parts
    base = part * steps
    state_specs = [
        pl.BlockSpec((4, VR, QB), lambda i, *_: (0, 0, i + base)),
        pl.BlockSpec((4, 1, QB), lambda i, *_: (0, 0, i + base)),
    ]
    if state:
        kernel = functools.partial(halo_kernel, base)
        requests = sources[-1].shape[0]
        out_specs = [pl.BlockSpec((QB, 256), lambda i, *_: (i, 0)), vmem(requests, 256)]
        out_shape = (
            jax.ShapeDtypeStruct((rows // parts, 256), BF),
            jax.ShapeDtypeStruct((requests, 256), F32),
        )
    else:
        kernel = own_kernel
        out_specs = state_specs
        out_shape = (
            jax.ShapeDtypeStruct((4, VR, rows), F32),
            jax.ShapeDtypeStruct((4, 1, rows), F32),
        )
    return pl.pallas_call(
        kernel,
        grid_spec=pltpu.PrefetchScalarGridSpec(
            num_scalar_prefetch=1,
            grid=(steps,),
            in_specs=[
                pl.BlockSpec((QB, 256), lambda i, *_: (i + base, 0)),
                pl.BlockSpec((1, QB), lambda i, *_: (0, i + base)),
            ]
            + [vmem(*x.shape) for x in sources]
            + state_specs[: len(state)],
            out_specs=out_specs,
            scratch_shapes=[
                pltpu.VMEM((4, QB, 256), BF),
                pltpu.VMEM((4, 1, QB), F32),
                pltpu.VMEM((4, VR, QB), F32),
            ],
        ),
        out_shape=out_shape,
        compiler_params=params(),
        cost_estimate=cost(12 << 30, 8 << 20, 12 << 20),
        name="attend_halo" if state else "attend_own",
    )(table, q, qseg, *sources, *state)


def contract_last(a, b):
    return lax.dot_general(a, b, (((1,), (1,)), ((), ())), preferred_element_type=F32)


def mlp_kernel(extra, table, m0, m1, m2, m3, o0, o1, o2, o3, h, gain, weights, *refs):
    lasts = refs[: 5 * extra]
    outs = refs[5 * extra :]
    *outs, w, sem = outs
    count = w.shape[0]
    step = pl.program_id(0)

    def load(ref, n):
        x = ref[...]
        if extra:
            last = lasts[n][...]
            fill = jnp.zeros((x.shape[0] - last.shape[0], x.shape[1]), BF)
            x = jnp.where(step == 0, jnp.concatenate([last, fill], axis=0), x)
        return x

    @pl.when(pl.program_id(0) == 0)
    def _():
        @pl.loop(0, count)
        def _(k):
            pltpu.make_async_copy(weights.at[k], w.at[table[4 + k]], sem).start()

    def rows(at, size, lo, width):
        return w[pl.ds(at, size), :, pl.ds(lo, width)].reshape(8 * size, width)

    n = h.shape[0]
    wide = load(h, 4).astype(F32)
    total = None
    for j, (m, o) in enumerate(((m0, o0), (m1, o1), (m2, o2), (m3, o3))):
        piece = contract_last(load(m, j), o[...])
        total = piece if total is None else total + piece
    first = (wide + total).astype(BF)
    wide = first.astype(F32)
    normed = layer_norm(wide, gain[...]).astype(BF)

    @pl.when(step == 0)
    def _():
        pltpu.make_async_copy(w, w, sem).wait()

    a = jnp.dot(normed, rows(0, count, 0, FFP), preferred_element_type=F32)
    b = jnp.dot(normed, rows(0, count, FFP, FFP), preferred_element_type=F32)
    inner = (0.5 * a * (1.0 + lax.erf(a * (0.5**0.5))) * b).astype(BF)
    mine = jnp.zeros((n, 256), F32)
    for t in range(4):
        mine = jnp.where(table[0] == t, wide[:, 256 * t : 256 * t + 256], mine)

    def down(j):
        return contract_last(inner, rows(table[j] * (count // 4), count // 4, 2 * FFP, FFP))

    quarters = (down(0) + mine, down(1), down(2), down(3))
    for out, x in zip(outs, quarters):
        out[...] = x.astype(out.dtype)
    if extra:

        @pl.when(step == 0)
        def _():
            held = lasts[0].shape[0]
            for j, x in enumerate(quarters):
                outs[4][:, pl.ds(pl.multiple_of(256 * table[j], 128), 256)] = x[:held]


def mlp(table, mixed, out_w, h, base, gain, weights, lasts=()):
    n = 256
    rows = mixed[0].shape[0]
    count = weights.shape[0]
    extra = 1 if lasts else 0

    def block(width, base=0):
        return pl.BlockSpec((n, width), lambda i, *_: (jnp.maximum(i - extra, 0) + base, 0))

    out_specs = [block(256)] * 4
    out_shape = [
        jax.ShapeDtypeStruct((rows, 256), kind) for kind in (F32, F32, BF, BF)
    ]
    if lasts:
        held = lasts[0].shape[0]
        out_specs.append(vmem(held, 1024))
        out_shape.append(jax.ShapeDtypeStruct((held, 1024), F32))
    return pl.pallas_call(
        functools.partial(mlp_kernel, extra),
        grid_spec=pltpu.PrefetchScalarGridSpec(
            num_scalar_prefetch=1,
            grid=(rows // n + extra,),
            in_specs=[block(256)] * 4
            + [vmem(1024, 256)] * 4
            + [block(1024, base), vmem(1, 1024), pl.BlockSpec(memory_space=pl.ANY)]
            + [vmem(*x.shape) for x in lasts],
            out_specs=out_specs,
            scratch_shapes=[pltpu.VMEM((count, 8, REST), BF), pltpu.SemaphoreType.DMA(())],
        ),
        out_shape=tuple(out_shape),
        compiler_params=params(),
        cost_estimate=cost(rows * 1024 * (1024 + 3 * FFP) * 2, 12 << 20, rows * FFP),
        name="mlp",
    )(table, *mixed, *out_w, h, gain.reshape(1, 1024), weights, *lasts)


def turn_bits(n):
    return n % 2 * 2 + n // 2


def swap(x, bit):
    return lax.ppermute(x, "tp", [(i, i ^ bit) for i in range(4)])


def reduce_core(mine, over, add, add_over):
    return mine, swap(add, 1), (over + swap(add_over, 1).astype(F32)).astype(BF)


def reduce_far(mine, got, over):
    return (mine + got.astype(F32) + swap(over, 2).astype(F32)).astype(BF)


def shift(x, by):
    count = lax.axis_size("req")
    return lax.ppermute(x, "req", [(i, i + by) for i in range(count) if 0 <= i + by < count])


def exchange(x, axes):
    return lax.all_to_all(x, axes, split_axis=0, concat_axis=0, tiled=True)


def body(
    hidden_in,
    lengths,
    tenant,
    shard_map,
    wq,
    wk,
    wv,
    wo,
    wi_in,
    wi_gate,
    wo2,
    head,
    attn_gain,
    mlp_gain,
    final_gain,
):
    req_count = lax.axis_size("req")
    tp_count = lax.axis_size("tp")
    count = req_count * tp_count
    req_index = lax.axis_index("req")
    tp_index = lax.axis_index("tp")
    slots, width = hidden_in.shape
    requests = lengths.shape[0]

    four = jnp.arange(4, dtype=jnp.int32)
    near_first = tp_index ^ turn_bits(four)
    first_block, *rest_block = prep(req_count, near_first, wq, wk, wv, wo, wi_in, wi_gate, wo2)
    place = jnp.arange(count, dtype=jnp.int32)
    source = jnp.sum(
        jnp.where(shard_map[None, :] == place[:, None], place[None, :], 0), axis=1
    )
    rest_rows = jnp.concatenate(
        [rest_block[0], swap(rest_block[1], 2), swap(rest_block[2], 1), swap(rest_block[3], 3)], axis=0
    )
    hidden, lengths, rest_rows = lax.optimization_barrier((hidden_in, lengths, rest_rows))
    rest = lax.all_gather(rest_rows, "req", axis=0, tiled=True).reshape(count, 8, REST)
    far = jnp.arange(count, dtype=jnp.int32)
    rest_target = shard_map[far // 4 * tp_count + (tp_index ^ turn_bits(far % 4))]

    ends = jnp.cumsum(lengths)
    base = req_index * slots
    index = base - slots + jnp.arange(3 * slots, dtype=jnp.int32)
    segment = jnp.sum((ends[None, :] <= index[:, None]).astype(jnp.int32), axis=1)
    segment = jnp.where((index >= 0) & (index < slots * req_count), segment, -1)
    own = base + jnp.arange(slots, dtype=jnp.int32)
    start_of = jnp.max(jnp.where(ends[None, :] <= own[:, None], ends[None, :], 0), axis=1)
    position = (own - start_of).astype(F32)
    lane = jnp.arange(128, dtype=jnp.int32) % (HEAD_DIM // 2)
    freq = THETA ** (-(2.0 * lane.astype(F32)) / HEAD_DIM)
    angle = position[:, None] * freq[None, :]
    turn = (jnp.cos(angle), jnp.sin(angle))
    begin = base + jnp.arange(slots // QB, dtype=jnp.int32) * QB
    close = begin + QB - 1
    low = jnp.max(jnp.where(ends[None, :] <= begin[:, None], ends[None, :], 0), axis=1) - base
    high = jnp.min(jnp.where(ends[None, :] > close[:, None], ends[None, :], 1 << 30), axis=1) - base

    blocks = slots // KB
    own_0 = jnp.maximum(low, 0) // KB
    own_1 = (jnp.minimum(high, slots) + KB - 1) // KB
    left_0 = (jnp.minimum(low, 0) + slots) // KB
    right_1 = (jnp.maximum(high - slots, 0) + KB - 1) // KB
    table = jnp.stack(
        [own_0, own_1 - own_0, left_0, blocks - left_0, jnp.zeros_like(right_1), right_1]
    )
    segs = segment.reshape(3, slots, 1)
    qseg = segment[slots : 2 * slots].reshape(1, slots)

    normed = norm(hidden, attn_gain)
    first_all = exchange(first_block.reshape(count, 8, width), BOTH)
    first_w = first_all[source].reshape(width, width)
    query, kv, cache = qkv_project(normed, first_w, *turn)
    left = shift(kv, 1)
    right = shift(kv, -1)
    out_w, kv = lax.optimization_barrier((first_w[:, 768:], kv))
    out_far, out_near = swap(out_w, 2), swap(out_w, 1)
    parts = 2
    state = attend(0, 1, table, query, qseg, (kv, segs[1]), ())
    last_slot = (ends - 1 - base).reshape(requests, 1)
    holds = (last_slot >= 0) & (last_slot < slots)
    last_in = jnp.where(holds, hidden[jnp.clip(last_slot[:, 0], 0, slots - 1)], 0)
    out_far, out_near, last_in, state = lax.optimization_barrier(
        (out_far, out_near, last_in, state)
    )
    out_w = (out_w, out_far, out_near, swap(out_far, 1))
    halo = (left, segs[0], right, segs[2], last_slot)
    mixed, picked = zip(
        *[attend(part, parts, table, query, qseg, halo, state) for part in range(parts)]
    )

    last_mixed = sum(picked).astype(BF)
    last_far = swap(last_mixed, 2)
    lasts = (last_mixed, last_far, swap(last_mixed, 1), swap(last_far, 1), last_in)

    order = jnp.concatenate([near_first, rest_target])
    steps = slots // parts // 256

    def feed(part, pieces, *lasts):
        return mlp(
            order, pieces, out_w, hidden_in, part * steps, mlp_gain, rest, *lasts
        )

    far = [swap(m, 2) for m in mixed]
    near = [swap(m, 1) for m in mixed]
    far[0], _ = lax.optimization_barrier((far[0], mixed[1]))
    *sums, last_part = feed(0, (mixed[0], far[0], near[0], swap(far[0], 1)), lasts)
    sums, far[1] = lax.optimization_barrier((sums, far[1]))
    last_piece = swap(far[1], 1)
    each = requests // req_count
    last_part = last_part.reshape(req_count, each, tp_count, 256).transpose(0, 2, 1, 3)
    pair, last_part, last_piece, piece = lax.optimization_barrier(
        (reduce_core(*sums), last_part, last_piece, mixed[1])
    )
    top = reduce_far(*pair)
    taken = exchange(last_part.reshape(count, each, 256), BOTH).sum(axis=0)
    sums = feed(1, (piece, far[1], near[1], last_piece))
    taken, sums, top = lax.optimization_barrier((taken, sums, top))
    spread = exchange(jnp.broadcast_to(taken.astype(BF)[None], (count, each, 256)), BOTH)
    hidden_out = jnp.concatenate([top, reduce_far(*reduce_core(*sums))], axis=0)
    last = (
        spread.reshape(req_count, tp_count, each, 256)
        .transpose(0, 2, 1, 3)
        .reshape(requests, width)
        .astype(F32)
    )
    last_rms = jnp.sqrt(jnp.mean(last * last, axis=-1))
    choose = (tenant[:, None] == jnp.arange(final_gain.shape[0], dtype=jnp.int32)[None, :]).astype(
        F32
    )
    gain_rows = jnp.dot(
        choose, final_gain, precision=lax.Precision.HIGHEST, preferred_element_type=F32
    )
    final = layer_norm(last, gain_rows).astype(BF)
    logits = contract_last(final, head.astype(BF))
    top = jnp.max(logits, axis=-1)
    tops = exchange(jnp.broadcast_to(top[None], (count, requests)), BOTH)
    top_logit = jnp.max(tops, axis=0)
    return (hidden_out, cache, last_rms, top_logit)


def solution(mesh):
    rows = P(BOTH, None)
    placed = (P("req", None), P(), P(), P()) + (rows,) * 8 + (P(), P(), P())
    return jax.shard_map(
        body,
        mesh=mesh,
        in_specs=placed,
        out_specs=(P("req", "tp"), P(None, "req", "tp"), P(), P()),
        check_vma=False,
    )
```

```python
import functools

import jax
import jax.numpy as jnp
from jax import lax
from jax.experimental import pallas as pl
from jax.experimental.pallas import tpu as pltpu
from jax.sharding import PartitionSpec as P

HEADS = 16
HEAD_DIM = 64
THETA = 160000.0
EPS = 1e-05
BF = jnp.bfloat16
F32 = jnp.float32
BOTH = ("req", "tp")
NEG = -1e30
FFP = 768
REST = 3 * FFP
QB = 256
KB = 256


def vmem(*shape):
    return pl.BlockSpec(shape, lambda *_: (0,) * len(shape))


def params():
    return pltpu.CompilerParams(vmem_limit_bytes=60 * 1024 * 1024)


def cost(flops, moved, transcendentals=0):
    return pl.CostEstimate(flops=flops, bytes_accessed=moved, transcendentals=transcendentals)


def prep_kernel(order, wq, wk, wv, wo, wi, wg, w2, first, *rest):
    row = lax.broadcasted_iota(jnp.int32, (256, 256), 0)
    col = lax.broadcasted_iota(jnp.int32, (256, 256), 1)
    source = (col % 128) // 32 * 64 + col // 128 * 32 + col % 32
    turn = jnp.where(row == source, 1.0, 0.0).astype(BF)
    trow = lax.broadcasted_iota(jnp.int32, (64, 128), 0)
    tcol = lax.broadcasted_iota(jnp.int32, (64, 128), 1)
    for t in range(4):
        at = slice(256 * t, 256 * t + 256)
        q, k = (
            jnp.dot(w[:, at].astype(BF), turn, preferred_element_type=F32).astype(BF)
            for w in (wq, wk)
        )
        mine = jnp.concatenate([q, k, wv[:, at].astype(BF), wo[:, at].astype(BF)], axis=1)
        for r in range(first.shape[0]):
            first[r, t] = mine
    for piece, out in enumerate(rest):
        t = order[piece]
        pick = jnp.where((trow == tcol + 16 * t) & (tcol < 16), 1.0, 0.0).astype(BF)
        for n, w in enumerate((wi, wg, w2)):
            main = pl.ds(pl.multiple_of(640 * t, 128), 640)
            out[:, FFP * n : FFP * n + 640] = w[:, main].astype(BF)
            out[:, FFP * n + 640 : FFP * n + 768] = jnp.dot(
                w[:, 2560:2624].astype(BF), pick, preferred_element_type=F32
            ).astype(BF)


def prep(req_count, order, *weights):
    return pl.pallas_call(
        prep_kernel,
        in_specs=[pl.BlockSpec(memory_space=pltpu.SMEM)] + [vmem(*w.shape) for w in weights],
        out_shape=(
            jax.ShapeDtypeStruct((req_count, 4, 8, 1024), BF),
        )
        + (jax.ShapeDtypeStruct((8, REST), BF),) * 4,
        compiler_params=params(),
        name="prep",
    )(order, *weights)


def layer_norm(values, gain):
    center = jnp.mean(values, axis=-1, keepdims=True)
    spread = jnp.mean(values * values, axis=-1, keepdims=True) - center * center
    return (values - center) * lax.rsqrt(spread + EPS) * gain


def norm_kernel(h, gain, out):
    out[...] = layer_norm(h[...].astype(F32), gain[...]).astype(BF)


def norm(h, gain):
    rows = h.shape[0]
    return pl.pallas_call(
        norm_kernel,
        grid=(rows // 512,),
        in_specs=[pl.BlockSpec((512, 1024), lambda i: (i, 0)), vmem(1, 1024)],
        out_specs=pl.BlockSpec((512, 1024), lambda i: (i, 0)),
        out_shape=jax.ShapeDtypeStruct((rows, 1024), BF),
        compiler_params=params(),
        cost_estimate=cost(1 << 24, 1 << 23),
        name="norm",
    )(h, gain.reshape(1, 1024))


def qkv_kernel(x, w, cos, sin, q, kv, cache):
    row = lax.broadcasted_iota(jnp.int32, (256, 256), 0)
    col = lax.broadcasted_iota(jnp.int32, (256, 256), 1)
    source = (col % 128) // 32 * 64 + col // 128 * 32 + col % 32
    back = jnp.where(source == row, 1.0, 0.0).astype(BF)
    y = jnp.dot(x[...], w[...], preferred_element_type=F32)
    c = cos[...]
    s = sin[...]

    def turned(a, b):
        return jnp.concatenate([a * c - b * s, b * c + a * s], axis=1)

    q[...] = (turned(y[:, :128], y[:, 128:256]).astype(BF).astype(F32) * 0.125).astype(BF)
    k = turned(y[:, 256:384], y[:, 384:512]).astype(BF)
    v = y[:, 512:].astype(BF)
    for n in range(x.shape[0] // KB):
        kv[n, 0] = k[KB * n : KB * n + KB]
        kv[n, 1] = jnp.transpose(v[KB * n : KB * n + KB])
    cache[0] = lax.dot_general(
        k, back, (((1,), (1,)), ((), ())), preferred_element_type=F32
    ).astype(BF)
    cache[1] = v


def qkv_project(x, w, cos, sin):
    rows = x.shape[0]
    n = 512
    return pl.pallas_call(
        qkv_kernel,
        grid=(rows // n,),
        in_specs=[
            pl.BlockSpec((n, 1024), lambda i: (i, 0)),
            vmem(1024, 768),
            pl.BlockSpec((n, 128), lambda i: (i, 0)),
            pl.BlockSpec((n, 128), lambda i: (i, 0)),
        ],
        out_specs=[
            pl.BlockSpec((n, 256), lambda i: (i, 0)),
            pl.BlockSpec((n // KB, 2, KB, 256), lambda i: (i, 0, 0, 0)),
            pl.BlockSpec((2, n, 256), lambda i: (0, i, 0)),
        ],
        out_shape=(
            jax.ShapeDtypeStruct((rows, 256), BF),
            jax.ShapeDtypeStruct((rows // KB, 2, KB, 256), BF),
            jax.ShapeDtypeStruct((2, rows, 256), BF),
        ),
        compiler_params=params(),
        cost_estimate=cost(2 * rows * 1024 * 768, 12 << 20),
        name="qkv",
    )(x, w, cos, sin)


VR = HEAD_DIM + 8


def attend_chunk(at, blocks, qm, kv, kseg, qseg, m_sc, acc):
    size = blocks * KB
    k = kv[pl.ds(at, blocks), 0].reshape(size, 256)
    same = kseg[pl.ds(pl.multiple_of(at * KB, KB), size), 0:1] == qseg[...]
    ones = jnp.ones((8, size), BF)
    scores = []
    for h in range(4):
        s = contract_last(k, qm[h])
        scores.append(jnp.where(same, s, NEG))
    for h in range(4):
        old = m_sc[h]
        new = jnp.maximum(old, jnp.max(scores[h], axis=0, keepdims=True))
        p = jnp.exp(scores[h] - new).astype(BF)
        fade = jnp.exp(old - new)
        m_sc[h] = new
        v = [kv[at + n, 1, HEAD_DIM * h : HEAD_DIM * h + HEAD_DIM, :] for n in range(blocks)]
        v = jnp.concatenate([jnp.concatenate(v, axis=1), ones], axis=0)
        acc[h] = acc[h] * fade + jnp.dot(v, p, preferred_element_type=F32)


def attend_span(table, at, i, *refs):
    start = table[at, i]
    pairs = table[at + 1, i] // 2

    @pl.loop(0, pairs)
    def _(c):
        attend_chunk(start + 2 * c, 2, *refs)

    @pl.when(table[at + 1, i] % 2 == 1)
    def _():
        attend_chunk(start + 2 * pairs, 1, *refs)


def spread_heads(q, qm):
    lane = lax.broadcasted_iota(jnp.int32, (QB, 256), 1)
    for h in range(4):
        qm[h] = jnp.where((lane % 128) // 32 == h, q[...].astype(F32), 0.0).astype(BF)


def own_kernel(table, q, qseg, kv, kseg, acc_out, m_out, qm, m_sc, acc):
    i = pl.program_id(0)
    spread_heads(q, qm)
    m_sc[...] = jnp.full_like(m_sc, NEG)
    acc[...] = jnp.zeros_like(acc)
    attend_span(table, 0, i, qm, kv, kseg, qseg, m_sc, acc)
    acc_out[...] = acc[...]
    m_out[...] = m_sc[...]


def halo_kernel(
    base, table, q, qseg, lkv, lseg, rkv, rseg, last, acc_in, m_in, out, picked, qm, m_sc, acc
):
    i = pl.program_id(0) + base
    spread_heads(q, qm)
    m_sc[...] = m_in[...]
    acc[...] = acc_in[...]
    attend_span(table, 2, i, qm, lkv, lseg, qseg, m_sc, acc)
    attend_span(table, 4, i, qm, rkv, rseg, qseg, m_sc, acc)
    heads = [acc[h, :HEAD_DIM] / acc[h, HEAD_DIM : HEAD_DIM + 1] for h in range(4)]
    mixed = jnp.transpose(jnp.concatenate(heads, axis=0)).astype(BF)
    out[...] = mixed
    slot = lax.broadcasted_iota(jnp.int32, (last.shape[0], QB), 1) + i * QB
    ends_here = jnp.where(last[...] == slot, 1.0, 0.0).astype(BF)

    @pl.when(pl.program_id(0) == 0)
    def _():
        picked[...] = jnp.zeros_like(picked)

    picked[...] += jnp.dot(ends_here, mixed, preferred_element_type=F32)


def attend(part, parts, table, q, qseg, sources, state):
    rows = q.shape[0]
    steps = rows // QB // parts
    base = part * steps
    state_specs = [
        pl.BlockSpec((4, VR, QB), lambda i, *_: (0, 0, i + base)),
        pl.BlockSpec((4, 1, QB), lambda i, *_: (0, 0, i + base)),
    ]
    if state:
        kernel = functools.partial(halo_kernel, base)
        requests = sources[-1].shape[0]
        out_specs = [pl.BlockSpec((QB, 256), lambda i, *_: (i, 0)), vmem(requests, 256)]
        out_shape = (
            jax.ShapeDtypeStruct((rows // parts, 256), BF),
            jax.ShapeDtypeStruct((requests, 256), F32),
        )
    else:
        kernel = own_kernel
        out_specs = state_specs
        out_shape = (
            jax.ShapeDtypeStruct((4, VR, rows), F32),
            jax.ShapeDtypeStruct((4, 1, rows), F32),
        )
    return pl.pallas_call(
        kernel,
        grid_spec=pltpu.PrefetchScalarGridSpec(
            num_scalar_prefetch=1,
            grid=(steps,),
            in_specs=[
                pl.BlockSpec((QB, 256), lambda i, *_: (i + base, 0)),
                pl.BlockSpec((1, QB), lambda i, *_: (0, i + base)),
            ]
            + [vmem(*x.shape) for x in sources]
            + state_specs[: len(state)],
            out_specs=out_specs,
            scratch_shapes=[
                pltpu.VMEM((4, QB, 256), BF),
                pltpu.VMEM((4, 1, QB), F32),
                pltpu.VMEM((4, VR, QB), F32),
            ],
        ),
        out_shape=out_shape,
        compiler_params=params(),
        cost_estimate=cost(12 << 30, 8 << 20, 12 << 20),
        name="attend_halo" if state else "attend_own",
    )(table, q, qseg, *sources, *state)


def contract_last(a, b):
    return lax.dot_general(a, b, (((1,), (1,)), ((), ())), preferred_element_type=F32)


def mlp_kernel(extra, table, m0, m1, m2, m3, o0, o1, o2, o3, h, gain, weights, *refs):
    lasts = refs[: 5 * extra]
    outs = refs[5 * extra :]
    *outs, w, sem = outs
    count = w.shape[0]
    step = pl.program_id(0)

    def load(ref, n):
        x = ref[...]
        if extra:
            last = lasts[n][...]
            fill = jnp.zeros((x.shape[0] - last.shape[0], x.shape[1]), BF)
            x = jnp.where(step == 0, jnp.concatenate([last, fill], axis=0), x)
        return x

    @pl.when(pl.program_id(0) == 0)
    def _():
        @pl.loop(0, count)
        def _(k):
            pltpu.make_async_copy(weights.at[k], w.at[table[4 + k]], sem).start()

    def rows(at, size, lo, width):
        return w[pl.ds(at, size), :, pl.ds(lo, width)].reshape(8 * size, width)

    n = h.shape[0]
    wide = load(h, 4).astype(F32)
    total = None
    for j, (m, o) in enumerate(((m0, o0), (m1, o1), (m2, o2), (m3, o3))):
        piece = contract_last(load(m, j), o[...])
        total = piece if total is None else total + piece
    first = (wide + total).astype(BF)
    wide = first.astype(F32)
    normed = layer_norm(wide, gain[...]).astype(BF)

    @pl.when(step == 0)
    def _():
        pltpu.make_async_copy(w, w, sem).wait()

    a = jnp.dot(normed, rows(0, count, 0, FFP), preferred_element_type=F32)
    b = jnp.dot(normed, rows(0, count, FFP, FFP), preferred_element_type=F32)
    inner = (0.5 * a * (1.0 + lax.erf(a * (0.5**0.5))) * b).astype(BF)
    mine = jnp.zeros((n, 256), F32)
    for t in range(4):
        mine = jnp.where(table[0] == t, wide[:, 256 * t : 256 * t + 256], mine)

    def down(j):
        return contract_last(inner, rows(table[j] * (count // 4), count // 4, 2 * FFP, FFP))

    quarters = (down(0) + mine, down(1), down(2), down(3))
    for out, x in zip(outs, quarters):
        out[...] = x.astype(out.dtype)
    if extra:

        @pl.when(step == 0)
        def _():
            held = lasts[0].shape[0]
            for j, x in enumerate(quarters):
                outs[4][:, pl.ds(pl.multiple_of(256 * table[j], 128), 256)] = x[:held]


def mlp(table, mixed, out_w, h, base, gain, weights, lasts=()):
    n = 256
    rows = mixed[0].shape[0]
    count = weights.shape[0]
    extra = 1 if lasts else 0

    def block(width, base=0):
        return pl.BlockSpec((n, width), lambda i, *_: (jnp.maximum(i - extra, 0) + base, 0))

    out_specs = [block(256)] * 4
    out_shape = [
        jax.ShapeDtypeStruct((rows, 256), kind) for kind in (F32, F32, BF, BF)
    ]
    if lasts:
        held = lasts[0].shape[0]
        out_specs.append(vmem(held, 1024))
        out_shape.append(jax.ShapeDtypeStruct((held, 1024), F32))
    return pl.pallas_call(
        functools.partial(mlp_kernel, extra),
        grid_spec=pltpu.PrefetchScalarGridSpec(
            num_scalar_prefetch=1,
            grid=(rows // n + extra,),
            in_specs=[block(256)] * 4
            + [vmem(1024, 256)] * 4
            + [block(1024, base), vmem(1, 1024), pl.BlockSpec(memory_space=pl.ANY)]
            + [vmem(*x.shape) for x in lasts],
            out_specs=out_specs,
            scratch_shapes=[pltpu.VMEM((count, 8, REST), BF), pltpu.SemaphoreType.DMA(())],
        ),
        out_shape=tuple(out_shape),
        compiler_params=params(),
        cost_estimate=cost(rows * 1024 * (1024 + 3 * FFP) * 2, 12 << 20, rows * FFP),
        name="mlp",
    )(table, *mixed, *out_w, h, gain.reshape(1, 1024), weights, *lasts)


def turn_bits(n):
    return n % 2 * 2 + n // 2


def swap(x, bit):
    return lax.ppermute(x, "tp", [(i, i ^ bit) for i in range(4)])


def reduce_core(mine, over, add, add_over):
    return mine, swap(add, 1), (over + swap(add_over, 1).astype(F32)).astype(BF)


def reduce_far(mine, got, over):
    return (mine + got.astype(F32) + swap(over, 2).astype(F32)).astype(BF)


def shift(x, by):
    count = lax.axis_size("req")
    return lax.ppermute(x, "req", [(i, i + by) for i in range(count) if 0 <= i + by < count])


def exchange(x, axes):
    return lax.all_to_all(x, axes, split_axis=0, concat_axis=0, tiled=True)


def body(
    hidden_in,
    lengths,
    tenant,
    shard_map,
    wq,
    wk,
    wv,
    wo,
    wi_in,
    wi_gate,
    wo2,
    head,
    attn_gain,
    mlp_gain,
    final_gain,
):
    req_count = lax.axis_size("req")
    tp_count = lax.axis_size("tp")
    count = req_count * tp_count
    req_index = lax.axis_index("req")
    tp_index = lax.axis_index("tp")
    slots, width = hidden_in.shape
    requests = lengths.shape[0]

    four = jnp.arange(4, dtype=jnp.int32)
    near_first = tp_index ^ turn_bits(four)
    first_block, *rest_block = prep(req_count, near_first, wq, wk, wv, wo, wi_in, wi_gate, wo2)
    place = jnp.arange(count, dtype=jnp.int32)
    source = jnp.sum(
        jnp.where(shard_map[None, :] == place[:, None], place[None, :], 0), axis=1
    )
    rest_rows = jnp.concatenate(
        [rest_block[0], swap(rest_block[1], 2), swap(rest_block[2], 1), swap(rest_block[3], 3)], axis=0
    )
    hidden, lengths, rest_rows = lax.optimization_barrier((hidden_in, lengths, rest_rows))
    sides = (4, 4)
    plane = sides[0] * sides[1]
    group = [
        z * plane + x * sides[1] + y
        for z in range(req_count // plane)
        for y in range(sides[1])
        for x in range(sides[0])
    ]
    rest = lax.all_gather(rest_rows, "req", axis=0, tiled=True, axis_index_groups=[group])
    rest = rest.reshape(count, 8, REST)
    far = jnp.arange(count, dtype=jnp.int32)
    at = far // tp_count
    from_req = at // plane * plane + at % sides[0] * sides[1] + at // sides[0] % sides[1]
    rest_target = shard_map[from_req * tp_count + (tp_index ^ turn_bits(far % tp_count))]

    ends = jnp.cumsum(lengths)
    base = req_index * slots
    index = base - slots + jnp.arange(3 * slots, dtype=jnp.int32)
    segment = jnp.sum((ends[None, :] <= index[:, None]).astype(jnp.int32), axis=1)
    segment = jnp.where((index >= 0) & (index < slots * req_count), segment, -1)
    own = base + jnp.arange(slots, dtype=jnp.int32)
    start_of = jnp.max(jnp.where(ends[None, :] <= own[:, None], ends[None, :], 0), axis=1)
    position = (own - start_of).astype(F32)
    lane = jnp.arange(128, dtype=jnp.int32) % (HEAD_DIM // 2)
    freq = THETA ** (-(2.0 * lane.astype(F32)) / HEAD_DIM)
    angle = position[:, None] * freq[None, :]
    turn = (jnp.cos(angle), jnp.sin(angle))
    begin = base + jnp.arange(slots // QB, dtype=jnp.int32) * QB
    close = begin + QB - 1
    low = jnp.max(jnp.where(ends[None, :] <= begin[:, None], ends[None, :], 0), axis=1) - base
    high = jnp.min(jnp.where(ends[None, :] > close[:, None], ends[None, :], 1 << 30), axis=1) - base

    blocks = slots // KB
    own_0 = jnp.maximum(low, 0) // KB
    own_1 = (jnp.minimum(high, slots) + KB - 1) // KB
    left_0 = (jnp.minimum(low, 0) + slots) // KB
    right_1 = (jnp.maximum(high - slots, 0) + KB - 1) // KB
    table = jnp.stack(
        [own_0, own_1 - own_0, left_0, blocks - left_0, jnp.zeros_like(right_1), right_1]
    )
    segs = segment.reshape(3, slots, 1)
    qseg = segment[slots : 2 * slots].reshape(1, slots)

    normed = norm(hidden, attn_gain)
    first_all = exchange(first_block.reshape(count, 8, width), BOTH)
    first_w = first_all[source].reshape(width, width)
    query, kv, cache = qkv_project(normed, first_w, *turn)
    left = shift(kv, 1)
    right = shift(kv, -1)
    out_w, kv = lax.optimization_barrier((first_w[:, 768:], kv))
    out_far, out_near = swap(out_w, 2), swap(out_w, 1)
    parts = 2
    state = attend(0, 1, table, query, qseg, (kv, segs[1]), ())
    last_slot = (ends - 1 - base).reshape(requests, 1)
    holds = (last_slot >= 0) & (last_slot < slots)
    last_in = jnp.where(holds, hidden[jnp.clip(last_slot[:, 0], 0, slots - 1)], 0)
    out_far, out_near, last_in, state = lax.optimization_barrier(
        (out_far, out_near, last_in, state)
    )
    out_w = (out_w, out_far, out_near, swap(out_far, 1))
    halo = (left, segs[0], right, segs[2], last_slot)
    mixed, picked = zip(
        *[attend(part, parts, table, query, qseg, halo, state) for part in range(parts)]
    )

    last_mixed = sum(picked).astype(BF)
    last_far = swap(last_mixed, 2)
    lasts = (last_mixed, last_far, swap(last_mixed, 1), swap(last_far, 1), last_in)

    order = jnp.concatenate([near_first, rest_target])
    steps = slots // parts // 256

    def feed(part, pieces, *lasts):
        return mlp(
            order, pieces, out_w, hidden_in, part * steps, mlp_gain, rest, *lasts
        )

    far = [swap(m, 2) for m in mixed]
    near = [swap(m, 1) for m in mixed]
    far[0], _ = lax.optimization_barrier((far[0], mixed[1]))
    *sums, last_part = feed(0, (mixed[0], far[0], near[0], swap(far[0], 1)), lasts)
    sums, far[1] = lax.optimization_barrier((sums, far[1]))
    last_piece = swap(far[1], 1)
    each = requests // req_count
    last_part = last_part.reshape(req_count, each, tp_count, 256).transpose(0, 2, 1, 3)
    pair, last_part, last_piece, piece = lax.optimization_barrier(
        (reduce_core(*sums), last_part, last_piece, mixed[1])
    )
    top = reduce_far(*pair)
    taken = exchange(last_part.reshape(count, each, 256), BOTH).sum(axis=0)
    sums = feed(1, (piece, far[1], near[1], last_piece))
    taken, sums, top = lax.optimization_barrier((taken, sums, top))
    spread = exchange(jnp.broadcast_to(taken.astype(BF)[None], (count, each, 256)), BOTH)
    hidden_out = jnp.concatenate([top, reduce_far(*reduce_core(*sums))], axis=0)
    last = (
        spread.reshape(req_count, tp_count, each, 256)
        .transpose(0, 2, 1, 3)
        .reshape(requests, width)
        .astype(F32)
    )
    last_rms = jnp.sqrt(jnp.mean(last * last, axis=-1))
    choose = (tenant[:, None] == jnp.arange(final_gain.shape[0], dtype=jnp.int32)[None, :]).astype(
        F32
    )
    gain_rows = jnp.dot(
        choose, final_gain, precision=lax.Precision.HIGHEST, preferred_element_type=F32
    )
    final = layer_norm(last, gain_rows).astype(BF)
    logits = contract_last(final, head.astype(BF))
    top = jnp.max(logits, axis=-1)
    tops = exchange(jnp.broadcast_to(top[None], (count, requests)), BOTH)
    top_logit = jnp.max(tops, axis=0)
    return (hidden_out, cache, last_rms, top_logit)


def solution(mesh):
    rows = P(BOTH, None)
    placed = (P("req", None), P(), P(), P()) + (rows,) * 8 + (P(), P(), P())
    return jax.shard_map(
        body,
        mesh=mesh,
        in_specs=placed,
        out_specs=(P("req", "tp"), P(None, "req", "tp"), P(), P()),
        check_vma=False,
    )
```

```python
import functools

import jax
import jax.numpy as jnp
from jax import lax
from jax.experimental import pallas as pl
from jax.experimental.pallas import tpu as pltpu
from jax.sharding import PartitionSpec as P

HEADS = 16
HEAD_DIM = 64
THETA = 160000.0
EPS = 1e-05
BF = jnp.bfloat16
F32 = jnp.float32
BOTH = ("req", "tp")
NEG = -1e30
FFP = 768
REST = 3 * FFP
QB = 256
KB = 256


def vmem(*shape):
    return pl.BlockSpec(shape, lambda *_: (0,) * len(shape))


def params():
    return pltpu.CompilerParams(vmem_limit_bytes=60 * 1024 * 1024)


def cost(flops, moved, transcendentals=0):
    return pl.CostEstimate(flops=flops, bytes_accessed=moved, transcendentals=transcendentals)


def prep_kernel(order, wq, wk, wv, wo, wi, wg, w2, first, *rest):
    row = lax.broadcasted_iota(jnp.int32, (256, 256), 0)
    col = lax.broadcasted_iota(jnp.int32, (256, 256), 1)
    source = (col % 128) // 32 * 64 + col // 128 * 32 + col % 32
    turn = jnp.where(row == source, 1.0, 0.0).astype(BF)
    trow = lax.broadcasted_iota(jnp.int32, (64, 128), 0)
    tcol = lax.broadcasted_iota(jnp.int32, (64, 128), 1)
    for t in range(4):
        at = slice(256 * t, 256 * t + 256)
        q, k = (
            jnp.dot(w[:, at].astype(BF), turn, preferred_element_type=F32).astype(BF)
            for w in (wq, wk)
        )
        mine = jnp.concatenate([q, k, wv[:, at].astype(BF), wo[:, at].astype(BF)], axis=1)
        for r in range(first.shape[0]):
            first[r, t] = mine
    for piece, out in enumerate(rest):
        t = order[piece]
        pick = jnp.where((trow == tcol + 16 * t) & (tcol < 16), 1.0, 0.0).astype(BF)
        for n, w in enumerate((wi, wg, w2)):
            main = pl.ds(pl.multiple_of(640 * t, 128), 640)
            out[:, FFP * n : FFP * n + 640] = w[:, main].astype(BF)
            out[:, FFP * n + 640 : FFP * n + 768] = jnp.dot(
                w[:, 2560:2624].astype(BF), pick, preferred_element_type=F32
            ).astype(BF)


def prep(req_count, order, *weights):
    return pl.pallas_call(
        prep_kernel,
        in_specs=[pl.BlockSpec(memory_space=pltpu.SMEM)] + [vmem(*w.shape) for w in weights],
        out_shape=(
            jax.ShapeDtypeStruct((req_count, 4, 8, 1024), BF),
        )
        + (jax.ShapeDtypeStruct((8, REST), BF),) * 4,
        compiler_params=params(),
        name="prep",
    )(order, *weights)


def layer_norm(values, gain):
    center = jnp.mean(values, axis=-1, keepdims=True)
    spread = jnp.mean(values * values, axis=-1, keepdims=True) - center * center
    return (values - center) * lax.rsqrt(spread + EPS) * gain


def norm_kernel(h, gain, out):
    out[...] = layer_norm(h[...].astype(F32), gain[...]).astype(BF)


def norm(h, gain):
    rows = h.shape[0]
    return pl.pallas_call(
        norm_kernel,
        grid=(rows // 512,),
        in_specs=[pl.BlockSpec((512, 1024), lambda i: (i, 0)), vmem(1, 1024)],
        out_specs=pl.BlockSpec((512, 1024), lambda i: (i, 0)),
        out_shape=jax.ShapeDtypeStruct((rows, 1024), BF),
        compiler_params=params(),
        cost_estimate=cost(1 << 24, 1 << 23),
        name="norm",
    )(h, gain.reshape(1, 1024))


def qkv_kernel(x, w, cos, sin, q, kv, cache):
    row = lax.broadcasted_iota(jnp.int32, (256, 256), 0)
    col = lax.broadcasted_iota(jnp.int32, (256, 256), 1)
    source = (col % 128) // 32 * 64 + col // 128 * 32 + col % 32
    back = jnp.where(source == row, 1.0, 0.0).astype(BF)
    y = jnp.dot(x[...], w[...], preferred_element_type=F32)
    c = cos[...]
    s = sin[...]

    def turned(a, b):
        return jnp.concatenate([a * c - b * s, b * c + a * s], axis=1)

    q[...] = (turned(y[:, :128], y[:, 128:256]).astype(BF).astype(F32) * 0.125).astype(BF)
    k = turned(y[:, 256:384], y[:, 384:512]).astype(BF)
    v = y[:, 512:].astype(BF)
    for n in range(x.shape[0] // KB):
        kv[n, 0] = k[KB * n : KB * n + KB]
        kv[n, 1] = jnp.transpose(v[KB * n : KB * n + KB])
    cache[0] = lax.dot_general(
        k, back, (((1,), (1,)), ((), ())), preferred_element_type=F32
    ).astype(BF)
    cache[1] = v


def qkv_project(x, w, cos, sin):
    rows = x.shape[0]
    n = 512
    return pl.pallas_call(
        qkv_kernel,
        grid=(rows // n,),
        in_specs=[
            pl.BlockSpec((n, 1024), lambda i: (i, 0)),
            vmem(1024, 768),
            pl.BlockSpec((n, 128), lambda i: (i, 0)),
            pl.BlockSpec((n, 128), lambda i: (i, 0)),
        ],
        out_specs=[
            pl.BlockSpec((n, 256), lambda i: (i, 0)),
            pl.BlockSpec((n // KB, 2, KB, 256), lambda i: (i, 0, 0, 0)),
            pl.BlockSpec((2, n, 256), lambda i: (0, i, 0)),
        ],
        out_shape=(
            jax.ShapeDtypeStruct((rows, 256), BF),
            jax.ShapeDtypeStruct((rows // KB, 2, KB, 256), BF),
            jax.ShapeDtypeStruct((2, rows, 256), BF),
        ),
        compiler_params=params(),
        cost_estimate=cost(2 * rows * 1024 * 768, 12 << 20),
        name="qkv",
    )(x, w, cos, sin)


VR = HEAD_DIM + 8


def attend_chunk(at, blocks, qm, kv, kseg, qseg, m_sc, acc):
    size = blocks * KB
    k = kv[pl.ds(at, blocks), 0].reshape(size, 256)
    same = kseg[pl.ds(pl.multiple_of(at * KB, KB), size), 0:1] == qseg[...]
    ones = jnp.ones((8, size), BF)
    scores = []
    for h in range(4):
        s = contract_last(k, qm[h])
        scores.append(jnp.where(same, s, NEG))
    for h in range(4):
        old = m_sc[h]
        new = jnp.maximum(old, jnp.max(scores[h], axis=0, keepdims=True))
        p = jnp.exp(scores[h] - new).astype(BF)
        fade = jnp.exp(old - new)
        m_sc[h] = new
        v = [kv[at + n, 1, HEAD_DIM * h : HEAD_DIM * h + HEAD_DIM, :] for n in range(blocks)]
        v = jnp.concatenate([jnp.concatenate(v, axis=1), ones], axis=0)
        acc[h] = acc[h] * fade + jnp.dot(v, p, preferred_element_type=F32)


def attend_span(table, at, i, *refs):
    start = table[at, i]
    pairs = table[at + 1, i] // 2

    @pl.loop(0, pairs)
    def _(c):
        attend_chunk(start + 2 * c, 2, *refs)

    @pl.when(table[at + 1, i] % 2 == 1)
    def _():
        attend_chunk(start + 2 * pairs, 1, *refs)


def spread_heads(q, qm):
    lane = lax.broadcasted_iota(jnp.int32, (QB, 256), 1)
    for h in range(4):
        qm[h] = jnp.where((lane % 128) // 32 == h, q[...].astype(F32), 0.0).astype(BF)


def own_kernel(table, q, qseg, kv, kseg, acc_out, m_out, qm, m_sc, acc):
    i = pl.program_id(0)
    spread_heads(q, qm)
    m_sc[...] = jnp.full_like(m_sc, NEG)
    acc[...] = jnp.zeros_like(acc)
    attend_span(table, 0, i, qm, kv, kseg, qseg, m_sc, acc)
    acc_out[...] = acc[...]
    m_out[...] = m_sc[...]


def halo_kernel(
    base, table, q, qseg, lkv, lseg, rkv, rseg, last, acc_in, m_in, out, picked, qm, m_sc, acc
):
    i = pl.program_id(0) + base
    spread_heads(q, qm)
    m_sc[...] = m_in[...]
    acc[...] = acc_in[...]
    attend_span(table, 2, i, qm, lkv, lseg, qseg, m_sc, acc)
    attend_span(table, 4, i, qm, rkv, rseg, qseg, m_sc, acc)
    heads = [acc[h, :HEAD_DIM] / acc[h, HEAD_DIM : HEAD_DIM + 1] for h in range(4)]
    mixed = jnp.transpose(jnp.concatenate(heads, axis=0)).astype(BF)
    out[...] = mixed
    slot = lax.broadcasted_iota(jnp.int32, (last.shape[0], QB), 1) + i * QB
    ends_here = jnp.where(last[...] == slot, 1.0, 0.0).astype(BF)

    @pl.when(pl.program_id(0) == 0)
    def _():
        picked[...] = jnp.zeros_like(picked)

    picked[...] += jnp.dot(ends_here, mixed, preferred_element_type=F32)


def attend(part, parts, table, q, qseg, sources, state):
    rows = q.shape[0]
    steps = rows // QB // parts
    base = part * steps
    state_specs = [
        pl.BlockSpec((4, VR, QB), lambda i, *_: (0, 0, i + base)),
        pl.BlockSpec((4, 1, QB), lambda i, *_: (0, 0, i + base)),
    ]
    if state:
        kernel = functools.partial(halo_kernel, base)
        requests = sources[-1].shape[0]
        out_specs = [pl.BlockSpec((QB, 256), lambda i, *_: (i, 0)), vmem(requests, 256)]
        out_shape = (
            jax.ShapeDtypeStruct((rows // parts, 256), BF),
            jax.ShapeDtypeStruct((requests, 256), F32),
        )
    else:
        kernel = own_kernel
        out_specs = state_specs
        out_shape = (
            jax.ShapeDtypeStruct((4, VR, rows), F32),
            jax.ShapeDtypeStruct((4, 1, rows), F32),
        )
    return pl.pallas_call(
        kernel,
        grid_spec=pltpu.PrefetchScalarGridSpec(
            num_scalar_prefetch=1,
            grid=(steps,),
            in_specs=[
                pl.BlockSpec((QB, 256), lambda i, *_: (i + base, 0)),
                pl.BlockSpec((1, QB), lambda i, *_: (0, i + base)),
            ]
            + [vmem(*x.shape) for x in sources]
            + state_specs[: len(state)],
            out_specs=out_specs,
            scratch_shapes=[
                pltpu.VMEM((4, QB, 256), BF),
                pltpu.VMEM((4, 1, QB), F32),
                pltpu.VMEM((4, VR, QB), F32),
            ],
        ),
        out_shape=out_shape,
        compiler_params=params(),
        cost_estimate=cost(12 << 30, 8 << 20, 12 << 20),
        name="attend_halo" if state else "attend_own",
    )(table, q, qseg, *sources, *state)


def contract_last(a, b):
    return lax.dot_general(a, b, (((1,), (1,)), ((), ())), preferred_element_type=F32)


def mlp_kernel(extra, table, m0, m1, m2, m3, o0, o1, o2, o3, h, gain, weights, *refs):
    lasts = refs[: 5 * extra]
    outs = refs[5 * extra :]
    *outs, w, sem = outs
    keep, send = outs[:2]
    count = w.shape[0]
    step = pl.program_id(0)

    def load(ref, n):
        x = ref[...]
        if extra:
            last = lasts[n][...]
            fill = jnp.zeros((x.shape[0] - last.shape[0], x.shape[1]), BF)
            x = jnp.where(step == 0, jnp.concatenate([last, fill], axis=0), x)
        return x

    @pl.when(pl.program_id(0) == 0)
    def _():
        @pl.loop(0, count)
        def _(k):
            pltpu.make_async_copy(weights.at[k], w.at[table[4 + k]], sem).start()

    def rows(at, size, lo, width):
        return w[pl.ds(at, size), :, pl.ds(lo, width)].reshape(8 * size, width)

    n = h.shape[0]
    wide = load(h, 4).astype(F32)
    total = None
    for j, (m, o) in enumerate(((m0, o0), (m1, o1), (m2, o2), (m3, o3))):
        piece = contract_last(load(m, j), o[...])
        total = piece if total is None else total + piece
    first = (wide + total).astype(BF)
    wide = first.astype(F32)
    normed = layer_norm(wide, gain[...]).astype(BF)

    @pl.when(step == 0)
    def _():
        pltpu.make_async_copy(w, w, sem).wait()

    a = jnp.dot(normed, rows(0, count, 0, FFP), preferred_element_type=F32)
    b = jnp.dot(normed, rows(0, count, FFP, FFP), preferred_element_type=F32)
    inner = (0.5 * a * (1.0 + lax.erf(a * (0.5**0.5))) * b).astype(BF)
    mine = jnp.zeros((n, 256), F32)
    for t in range(4):
        mine = jnp.where(table[0] == t, wide[:, 256 * t : 256 * t + 256], mine)

    def down(j):
        return contract_last(inner, rows(table[j] * (count // 4), count // 4, 2 * FFP, FFP))

    kept = jnp.concatenate([down(0) + mine, down(1)], axis=1)
    sent = jnp.concatenate([down(2), down(3)], axis=1)
    keep[...] = kept
    send[...] = sent.astype(BF)
    if extra:

        @pl.when(step == 0)
        def _():
            held = lasts[0].shape[0]
            for j, x in enumerate((kept, sent)):
                for n in range(2):
                    at = pl.ds(pl.multiple_of(256 * table[2 * j + n], 128), 256)
                    outs[2][:, at] = x[:held, 256 * n : 256 * n + 256]


def mlp(table, mixed, out_w, h, base, gain, weights, lasts=()):
    n = 256 if lasts else 512
    rows = mixed[0].shape[0]
    count = weights.shape[0]
    extra = 1 if lasts else 0
    base = base // n

    def block(width, base=0):
        return pl.BlockSpec((n, width), lambda i, *_: (jnp.maximum(i - extra, 0) + base, 0))

    out_specs = [block(512), block(512)]
    out_shape = [
        jax.ShapeDtypeStruct((rows, 512), F32),
        jax.ShapeDtypeStruct((rows, 512), BF),
    ]
    if lasts:
        held = lasts[0].shape[0]
        out_specs.append(vmem(held, 1024))
        out_shape.append(jax.ShapeDtypeStruct((held, 1024), F32))
    return pl.pallas_call(
        functools.partial(mlp_kernel, extra),
        grid_spec=pltpu.PrefetchScalarGridSpec(
            num_scalar_prefetch=1,
            grid=(rows // n + extra,),
            in_specs=[block(256)] * 4
            + [vmem(1024, 256)] * 4
            + [block(1024, base), vmem(1, 1024), pl.BlockSpec(memory_space=pl.ANY)]
            + [vmem(*x.shape) for x in lasts],
            out_specs=out_specs,
            scratch_shapes=[pltpu.VMEM((count, 8, REST), BF), pltpu.SemaphoreType.DMA(())],
        ),
        out_shape=tuple(out_shape),
        compiler_params=params(),
        cost_estimate=cost(rows * 1024 * (1024 + 3 * FFP) * 2, 12 << 20, rows * FFP),
        name="mlp",
    )(table, *mixed, *out_w, h, gain.reshape(1, 1024), weights, *lasts)


def turn_bits(n):
    return n % 2 * 2 + n // 2


def swap(x, bit):
    return lax.ppermute(x, "tp", [(i, i ^ bit) for i in range(4)])


def reduce_core(keep, send):
    got = swap(send, 1).astype(F32)
    return keep[:, :256] + got[:, :256], (keep[:, 256:] + got[:, 256:]).astype(BF)


def reduce_far(mine, send):
    return (mine + swap(send, 2).astype(F32)).astype(BF)


def shift(x, by):
    count = lax.axis_size("req")
    return lax.ppermute(x, "req", [(i, i + by) for i in range(count) if 0 <= i + by < count])


def exchange(x, axes):
    return lax.all_to_all(x, axes, split_axis=0, concat_axis=0, tiled=True)


def body(
    hidden_in,
    lengths,
    tenant,
    shard_map,
    wq,
    wk,
    wv,
    wo,
    wi_in,
    wi_gate,
    wo2,
    head,
    attn_gain,
    mlp_gain,
    final_gain,
):
    req_count = lax.axis_size("req")
    tp_count = lax.axis_size("tp")
    count = req_count * tp_count
    req_index = lax.axis_index("req")
    tp_index = lax.axis_index("tp")
    slots, width = hidden_in.shape
    requests = lengths.shape[0]

    four = jnp.arange(4, dtype=jnp.int32)
    near_first = tp_index ^ turn_bits(four)
    first_block, *rest_block = prep(req_count, near_first, wq, wk, wv, wo, wi_in, wi_gate, wo2)
    place = jnp.arange(count, dtype=jnp.int32)
    source = jnp.sum(
        jnp.where(shard_map[None, :] == place[:, None], place[None, :], 0), axis=1
    )
    rest_rows = jnp.concatenate(
        [rest_block[0], swap(rest_block[1], 2), swap(rest_block[2], 1), swap(rest_block[3], 3)], axis=0
    )
    hidden, lengths, rest_rows = lax.optimization_barrier((hidden_in, lengths, rest_rows))
    rest = lax.all_gather(rest_rows, "req", axis=0, tiled=True).reshape(count, 8, REST)
    far = jnp.arange(count, dtype=jnp.int32)
    rest_target = shard_map[far // 4 * tp_count + (tp_index ^ turn_bits(far % 4))]

    ends = jnp.cumsum(lengths)
    base = req_index * slots
    index = base - slots + jnp.arange(3 * slots, dtype=jnp.int32)
    segment = jnp.sum((ends[None, :] <= index[:, None]).astype(jnp.int32), axis=1)
    segment = jnp.where((index >= 0) & (index < slots * req_count), segment, -1)
    own = base + jnp.arange(slots, dtype=jnp.int32)
    start_of = jnp.max(jnp.where(ends[None, :] <= own[:, None], ends[None, :], 0), axis=1)
    position = (own - start_of).astype(F32)
    lane = jnp.arange(128, dtype=jnp.int32) % (HEAD_DIM // 2)
    freq = THETA ** (-(2.0 * lane.astype(F32)) / HEAD_DIM)
    angle = position[:, None] * freq[None, :]
    turn = (jnp.cos(angle), jnp.sin(angle))
    begin = base + jnp.arange(slots // QB, dtype=jnp.int32) * QB
    close = begin + QB - 1
    low = jnp.max(jnp.where(ends[None, :] <= begin[:, None], ends[None, :], 0), axis=1) - base
    high = jnp.min(jnp.where(ends[None, :] > close[:, None], ends[None, :], 1 << 30), axis=1) - base

    blocks = slots // KB
    own_0 = jnp.maximum(low, 0) // KB
    own_1 = (jnp.minimum(high, slots) + KB - 1) // KB
    left_0 = (jnp.minimum(low, 0) + slots) // KB
    right_1 = (jnp.maximum(high - slots, 0) + KB - 1) // KB
    table = jnp.stack(
        [own_0, own_1 - own_0, left_0, blocks - left_0, jnp.zeros_like(right_1), right_1]
    )
    segs = segment.reshape(3, slots, 1)
    qseg = segment[slots : 2 * slots].reshape(1, slots)

    normed = norm(hidden, attn_gain)
    first_all = exchange(first_block.reshape(count, 8, width), BOTH)
    first_w = first_all[source].reshape(width, width)
    query, kv, cache = qkv_project(normed, first_w, *turn)
    left = shift(kv, 1)
    right = shift(kv, -1)
    out_w, kv = lax.optimization_barrier((first_w[:, 768:], kv))
    out_far, out_near = swap(out_w, 2), swap(out_w, 1)
    parts = 2
    state = attend(0, 1, table, query, qseg, (kv, segs[1]), ())
    out_far, out_near, state = lax.optimization_barrier((out_far, out_near, state))
    out_w = (out_w, out_far, out_near, swap(out_far, 1))
    last_slot = (ends - 1 - base).reshape(requests, 1)
    halo = (left, segs[0], right, segs[2], last_slot)
    mixed, picked = zip(
        *[attend(part, parts, table, query, qseg, halo, state) for part in range(parts)]
    )

    holds = (last_slot >= 0) & (last_slot < slots)
    last_in = jnp.where(holds, hidden[jnp.clip(last_slot[:, 0], 0, slots - 1)], 0)
    last_mixed = sum(picked).astype(BF)
    last_far = swap(last_mixed, 2)
    lasts = (last_mixed, last_far, swap(last_mixed, 1), swap(last_far, 1), last_in)

    order = jnp.concatenate([near_first, rest_target])
    part_rows = slots // parts

    def feed(part, pieces, *lasts):
        return mlp(
            order, pieces, out_w, hidden_in, part * part_rows, mlp_gain, rest, *lasts
        )

    far = [swap(m, 2) for m in mixed]
    near = [swap(m, 1) for m in mixed]
    far[0], _ = lax.optimization_barrier((far[0], mixed[1]))
    keep, send, last_part = feed(0, (mixed[0], far[0], near[0], swap(far[0], 1)), lasts)
    keep, send, far[1] = lax.optimization_barrier((keep, send, far[1]))
    last_piece = swap(far[1], 1)
    each = requests // req_count
    last_part = last_part.reshape(req_count, each, tp_count, 256).transpose(0, 2, 1, 3)
    pair, last_part, last_piece, piece = lax.optimization_barrier(
        (reduce_core(keep, send), last_part, last_piece, mixed[1])
    )
    top = reduce_far(*pair)
    taken = exchange(last_part.reshape(count, each, 256), BOTH).sum(axis=0)
    keep, send = feed(1, (piece, far[1], near[1], last_piece))
    taken, keep, send, top = lax.optimization_barrier((taken, keep, send, top))
    spread = exchange(jnp.broadcast_to(taken.astype(BF)[None], (count, each, 256)), BOTH)
    hidden_out = jnp.concatenate([top, reduce_far(*reduce_core(keep, send))], axis=0)
    last = (
        spread.reshape(req_count, tp_count, each, 256)
        .transpose(0, 2, 1, 3)
        .reshape(requests, width)
        .astype(F32)
    )
    last_rms = jnp.sqrt(jnp.mean(last * last, axis=-1))
    choose = (tenant[:, None] == jnp.arange(final_gain.shape[0], dtype=jnp.int32)[None, :]).astype(
        F32
    )
    gain_rows = jnp.dot(
        choose, final_gain, precision=lax.Precision.HIGHEST, preferred_element_type=F32
    )
    final = layer_norm(last, gain_rows).astype(BF)
    logits = contract_last(final, head.astype(BF))
    top = jnp.max(logits, axis=-1)
    tops = exchange(jnp.broadcast_to(top[None], (count, requests)), BOTH)
    top_logit = jnp.max(tops, axis=0)
    return (hidden_out, cache, last_rms, top_logit)


def solution(mesh):
    rows = P(BOTH, None)
    placed = (P("req", None), P(), P(), P()) + (rows,) * 8 + (P(), P(), P())
    return jax.shard_map(
        body,
        mesh=mesh,
        in_specs=placed,
        out_specs=(P("req", "tp"), P(None, "req", "tp"), P(), P()),
        check_vma=False,
    )
```
